32 devices in a mesh: tm: 8 (over z, y), pix: 4 (over x, core).
Axes of the slice: x: 2, y: 2, z: 4, core: 2. Of those that a mesh axis runs over, the one named last changes fastest.
Arguments:
- counts: float32 [1024, 16384], P('tm', 'pix'), may hold values from 0.5 to 15
- dead_time: float32 [16384], P('pix'), may hold values from 0.002 to 0.03
- flat_field: float32 [16384], P('pix'), may hold values from 0.3 to 3
- cycle_map: int32 [16384], P('pix'), may hold values from 0 to 31, as said below
Outputs:
- two_time: float32 [32, 1024, 1024], P('pix', 'tm')
The draws below stay inside these ranges and needn't reach their ends.
Inputs may be any that keep to these rules, and one draw needn't show every extreme that they name: `cycle_map`: every cycle holds at least one pixel.
All inputs are finite; a program needn't handle non-finite values.
Results may differ from the reference program's by a relative error of at most 0.00042.
Values may be sent and summed in bfloat16 or wider, within the bound.
A program may use at most 64 MiB of HBM per device.

```python
import math
import jax
import jax.numpy as jnp
from jax import lax

FRAMES = 1024
CYCLES = 32
PIXELS = 16384


def draw_cycle_map(key, part):
    first_key = jax.random.fold_in(key, 11)
    second_key = jax.random.fold_in(key, 23)
    uniform_ints = jax.random.randint(first_key, (PIXELS,), 0, CYCLES * CYCLES)
    bounds = jnp.arange(1, CYCLES, dtype=jnp.int32) ** 2
    cycles = jnp.sum((uniform_ints[:, None] >= bounds[None, :]).astype(jnp.int32), axis=1).astype(jnp.int32)
    chosen = jax.random.permutation(second_key, PIXELS)[:CYCLES]
    return cycles.at[chosen].set(jnp.arange(CYCLES, dtype=jnp.int32))


def level_of(own_key, extent, cuts, smallest, high):
    def one(axis_at, blocks):
        draws = jax.random.uniform(jax.random.fold_in(jax.random.fold_in(own_key, 6), axis_at), (blocks,), jnp.float32, smallest / len(cuts), high / len(cuts))
        return jnp.repeat(jnp.exp(draws), extent[axis_at] // blocks).reshape((-1,) + (1,) * (len(extent) - axis_at - 1))

    level = one(*cuts[0])
    for cut in cuts[1:]:
        level = level * one(*cut)
    return level


def setup_inputs(seed: int = 0) -> dict:
    streams_of = jax.random.split(jax.random.key(seed), 5)
    counts = jnp.clip(jnp.exp(math.log(15.0) - 3.4011974 * jax.random.uniform(streams_of[0], (FRAMES, PIXELS), jnp.float32) ** level_of(streams_of[0], (FRAMES, PIXELS), ((0, 8), (1, 4)), -0.2, 0.2)), 0.5, 15.0)
    dead_time = jnp.clip(jnp.exp(math.log(0.03) - 2.70805 * jax.random.uniform(streams_of[1], (PIXELS,), jnp.float32) ** level_of(streams_of[1], (PIXELS,), ((0, 4),), -0.2, 0.2)), 0.002, 0.03)
    flat_field = jnp.clip(jnp.exp(math.log(3.0) - 2.3025851 * jax.random.uniform(streams_of[2], (PIXELS,), jnp.float32) ** level_of(streams_of[2], (PIXELS,), ((0, 4),), -0.2, 0.2)), 0.3, 3.0)
    cycle_map = draw_cycle_map(jax.random.fold_in(streams_of[4], 71), 0)
    return dict(counts=counts, dead_time=dead_time, flat_field=flat_field, cycle_map=cycle_map)


def reference(counts, dead_time, flat_field, cycle_map):
    photons = counts.astype(jnp.float32)
    intensity = (photons / (1.0 - dead_time[None, :] * photons) * flat_field[None, :]).astype(jnp.bfloat16)
    widened = intensity.astype(jnp.float32)
    cycle_onehot = (cycle_map[None, :] == jnp.arange(CYCLES, dtype=jnp.int32)[:, None]).astype(jnp.float32)
    cycle_size = jnp.sum(cycle_onehot, axis=1)
    cycle_sum = jnp.dot(cycle_onehot, widened.T, precision=lax.Precision.HIGHEST)

    def one_cycle(weights):
        masked = widened * weights[None, :]
        return jnp.dot(masked, widened.T, precision=lax.Precision.HIGHEST)

    gram = lax.map(one_cycle, cycle_onehot)
    return cycle_size[:, None, None] * gram / (cycle_sum[:, :, None] * cycle_sum[:, None, :])
```

```python
import math

import jax
import jax.numpy as jnp
from jax import lax
from jax.sharding import PartitionSpec as P

CYCLES = 32


def inner_extent(count):
    return max(d for d in range(1, count + 1) if count % d == 0 and d * d <= count)


class LogCode:
    def __init__(self, low, high, zero):
        self.low, self.zero = low, zero
        low, high = math.log2(low), math.log2(high)
        self.centre, self.steps = (high + low) / 2, 65400 / (high - low)

    def encode(self, value):
        level = (jnp.log2(jnp.maximum(value, self.low)) - self.centre) * self.steps
        return jnp.round(level).astype(jnp.int16)

    def decode(self, code):
        level = code.astype(jnp.float32)
        value = jnp.exp2(level * (1.0 / self.steps) + self.centre)
        return jnp.where(level > -32700 + 32, value, 0.0) if self.zero else value


def per_device(counts, dead_time, flat_field, cycle_map):
    intensity = (counts / (1.0 - dead_time[None, :] * counts) * flat_field[None, :]).astype(
        jnp.bfloat16
    )
    frames, pixels = intensity.shape
    tm, pix = lax.axis_size("tm"), lax.axis_size("pix")
    inner = inner_extent(tm)
    outer = tm // inner
    cores = 2 if pix % 2 == 0 else 1
    across = pix // cores
    owned = CYCLES // pix
    at_tm, at_pix = lax.axis_index("tm"), lax.axis_index("pix")
    z, y = at_tm // inner, at_tm % inner
    x, core = at_pix // cores, at_pix % cores

    def shift_z(value, k=1):
        return lax.ppermute(
            value, "tm", [(i, (i // inner + k) % outer * inner + i % inner) for i in range(tm)]
        )

    def shift_y(value, k):
        return lax.ppermute(
            value, "tm", [(i, i // inner * inner + (i % inner + k) % inner) for i in range(tm)]
        )

    def shift_x(value, k):
        return lax.ppermute(
            value, "pix", [(i, (i // cores + k) % across * cores + i % cores) for i in range(pix)]
        )

    def swap_core(value):
        return lax.ppermute(
            value, "pix", [(i, i // cores * cores + (i % cores + 1) % cores) for i in range(pix)]
        )

    half = outer // 2
    remote = {0: intensity}
    for s in range(1, half + 1):
        remote[s] = shift_z(remote[s - 1])
    beside = [intensity]
    for k in range(1, inner):
        beside.append(shift_y(intensity, k))

    def onehot_of(owner_core, ks):
        ids = jnp.concatenate(
            [
                ((x + k) % across * cores + owner_core) * owned
                + jnp.arange(owned, dtype=jnp.int32)
                for k in ks
            ]
        )
        return (cycle_map[None, :] == ids[:, None]).astype(jnp.bfloat16)

    other = (core + 1) % cores
    away_ks, own_ks = range(1, across), range(1)
    rows = frames + 8

    def gram(onehot, left, right, sums):
        masked = (onehot[:, None, :] * left[None, :, :]).reshape(-1, pixels)
        value = lax.dot_general(
            masked, right, (((1,), (1,)), ((), ())), preferred_element_type=jnp.float32
        ).reshape(onehot.shape[0], rows, right.shape[0])
        if sums is not None:
            own = lax.dot_general(
                onehot, sums, (((1,), (1,)), ((), ())), preferred_element_type=jnp.float32
            )
            value = value + jnp.pad(
                own[:, None, :], ((0, 0), (frames, 7), (0, right.shape[0] - frames))
            )
        return value

    partials = LogCode(0.0218, 6800.0 * pixels * cores, True)
    results = LogCode(1 / 140.0, 140.0, False)

    def reduce_owned(left, right, sums=None, exact=False):
        def part(owner_core, ks):
            return gram(onehot_of(owner_core, ks), left, right, sums)

        theirs = {}
        for name, ks in (("o", away_ks), ("x", own_ks)):
            if cores > 1 and len(ks):
                theirs[name] = swap_core(part(other, ks))
        total = None
        if across > 1:
            sent = part(core, away_ks)
            if cores > 1:
                sent = sent + theirs["o"]
            got = []
            for k in range(1, across):
                value = sent[(k - 1) * owned : k * owned]
                if not exact:
                    value = partials.encode(value)
                value = shift_x(value, k)
                got.append(value if exact else partials.decode(value))
            total = sum(got[1:], got[0])
        here = part(core, own_ks)
        if cores > 1:
            here = here + theirs["x"]
        here = lax.optimization_barrier(here)
        return here if total is None else here + total

    out = jnp.zeros((owned, frames, tm * frames), jnp.float32)

    def place(out, value, zs, ys):
        at = (zs % outer * inner + ys % inner) * frames
        return lax.dynamic_update_slice_in_dim(out, value, at, 2)

    ones = jnp.ones((8, pixels), jnp.bfloat16)
    extended = jnp.concatenate([intensity, ones], axis=0)
    total = reduce_owned(extended, extended, exact=True)
    row_sums = total[:, :frames, frames]
    scale = total[:, frames, frames][:, None, None] / row_sums[:, :, None]
    column_sums = [total[:, frames : frames + 1, :frames]]
    size = total[:, frames : frames + 1, frames : frames + 1]
    out = place(out, total[:, :frames, :frames] * scale / column_sums[0], z, y)
    group = jnp.concatenate(beside, axis=0)

    def beside_group(out):
        if inner == 1:
            return out
        total = reduce_owned(extended, group[frames:])
        for k in range(1, inner):
            part = total[:, :, (k - 1) * frames : k * frames]
            column_sums.append(part[:, frames : frames + 1])
            out = place(out, part[:, :frames] * scale / column_sums[k], z, y - k)
        return out

    def remote_group(s, out):
        left = jnp.concatenate([remote[s], jnp.zeros((8, pixels), jnp.bfloat16)], axis=0)
        total = reduce_owned(left, group, sums=remote[s])
        left_sums = jnp.transpose(total[:, frames : frames + 1, :frames], (0, 2, 1))
        value = total[:, :frames] * (size / left_sums) / jnp.concatenate(column_sums, axis=2)
        if 2 * s != outer:
            back = shift_z(results.encode(value), -s)
            back = results.decode(back)
            for k in range(inner):
                out = place(out, back[:, :, k * frames : (k + 1) * frames], z + s, y - k)
        for k in range(inner):
            block = jnp.transpose(value[:, :, k * frames : (k + 1) * frames], (0, 2, 1))
            if k > 0:
                block = results.decode(shift_y(results.encode(block), -k))
            out = place(out, block, z - s, y + k)
        return out

    out = beside_group(out)
    for s in range(1, half + 1):
        out = remote_group(s, out)
    return out


def solution(mesh):
    placed = (P("tm", "pix"), P("pix"), P("pix"), P("pix"))

    return jax.shard_map(
        per_device, mesh=mesh, in_specs=placed, out_specs=P("pix", "tm", None), check_vma=False
    )
```

```python
import functools
import math

import jax
import jax.numpy as jnp
from jax import lax
from jax.experimental import pallas as pl
from jax.experimental.pallas import tpu as pltpu
from jax.sharding import PartitionSpec as P

CYCLES = 32


def inner_extent(count):
    return max(d for d in range(1, count + 1) if count % d == 0 and d * d <= count)


class LogCode:
    def __init__(self, low, high, zero):
        self.low, self.zero = low, zero
        low, high = math.log2(low), math.log2(high)
        self.centre, self.steps = (high + low) / 2, 65400 / (high - low)

    def encode(self, value):
        level = (jnp.log2(jnp.maximum(value, self.low)) - self.centre) * self.steps
        return jnp.round(level).astype(jnp.int16)

    def decode(self, code):
        level = code.astype(jnp.float32)
        value = jnp.exp2(level * (1.0 / self.steps) + self.centre)
        return jnp.where(level > -32700 + 32, value, 0.0) if self.zero else value


def per_device(counts, dead_time, flat_field, cycle_map):
    intensity = (counts / (1.0 - dead_time[None, :] * counts) * flat_field[None, :]).astype(
        jnp.bfloat16
    )
    frames, pixels = intensity.shape
    tm, pix = lax.axis_size("tm"), lax.axis_size("pix")
    inner = inner_extent(tm)
    outer = tm // inner
    cores = 2 if pix % 2 == 0 else 1
    across = pix // cores
    owned = CYCLES // pix
    at_tm, at_pix = lax.axis_index("tm"), lax.axis_index("pix")
    z, y = at_tm // inner, at_tm % inner
    x, core = at_pix // cores, at_pix % cores

    def shift_z(value, k=1):
        return lax.ppermute(
            value, "tm", [(i, (i // inner + k) % outer * inner + i % inner) for i in range(tm)]
        )

    def shift_y(value, k):
        return lax.ppermute(
            value, "tm", [(i, i // inner * inner + (i % inner + k) % inner) for i in range(tm)]
        )

    def shift_x(value, k):
        return lax.ppermute(
            value, "pix", [(i, (i // cores + k) % across * cores + i % cores) for i in range(pix)]
        )

    def swap_core(value):
        return lax.ppermute(
            value, "pix", [(i, i // cores * cores + (i % cores + 1) % cores) for i in range(pix)]
        )

    half = outer // 2
    remote = {0: intensity}
    for s in range(1, half + 1):
        remote[s] = shift_z(remote[s - 1])
    beside = [intensity]
    for k in range(1, inner):
        beside.append(shift_y(intensity, k))

    def onehot_of(owner_core, ks):
        ids = jnp.concatenate(
            [
                ((x + k) % across * cores + owner_core) * owned
                + jnp.arange(owned, dtype=jnp.int32)
                for k in ks
            ]
        )
        return (cycle_map[None, :] == ids[:, None]).astype(jnp.bfloat16)

    other = (core + 1) % cores
    away_ks, own_ks = range(1, across), range(1)
    rows = frames + 8

    def gram(onehot, left, right, sums):
        masked = (onehot[:, None, :] * left[None, :, :]).reshape(-1, pixels)
        value = lax.dot_general(
            masked, right, (((1,), (1,)), ((), ())), preferred_element_type=jnp.float32
        ).reshape(onehot.shape[0], rows, right.shape[0])
        if sums is not None:
            own = lax.dot_general(
                onehot, sums, (((1,), (1,)), ((), ())), preferred_element_type=jnp.float32
            )
            value = value + jnp.pad(
                own[:, None, :], ((0, 0), (frames, 7), (0, right.shape[0] - frames))
            )
        return value

    partials = LogCode(0.0218, 6800.0 * pixels * cores, True)
    results = LogCode(1 / 140.0, 140.0, False)

    def reduce_owned(left, right, sums=None, exact=False):
        def part(owner_core, ks):
            return gram(onehot_of(owner_core, ks), left, right, sums)

        theirs = {}
        for name, ks in (("o", away_ks), ("x", own_ks)):
            if cores > 1 and len(ks):
                theirs[name] = swap_core(part(other, ks))
        total = None
        if across > 1:
            sent = part(core, away_ks)
            if cores > 1:
                sent = sent + theirs["o"]
            got = []
            for k in range(1, across):
                value = sent[(k - 1) * owned : k * owned]
                if not exact:
                    value = partials.encode(value)
                value = shift_x(value, k)
                got.append(value if exact else partials.decode(value))
            total = sum(got[1:], got[0])
        here = part(core, own_ks)
        if cores > 1:
            here = here + theirs["x"]
        here = lax.optimization_barrier(here)
        return here if total is None else here + total

    out = jnp.zeros((owned, frames, tm * frames), jnp.float32)

    def place(out, value, zs, ys):
        at = (zs % outer * inner + ys % inner) * frames
        return lax.dynamic_update_slice_in_dim(out, value, at, 2)

    ones = jnp.ones((8, pixels), jnp.bfloat16)
    extended = jnp.concatenate([intensity, ones], axis=0)
    total = reduce_owned(extended, extended, exact=True)
    row_sums = total[:, :frames, frames]
    scale = total[:, frames, frames][:, None, None] / row_sums[:, :, None]
    column_sums = [total[:, frames : frames + 1, :frames]]
    size = total[:, frames : frames + 1, frames : frames + 1]
    out = place(out, total[:, :frames, :frames] * scale / column_sums[0], z, y)
    group = jnp.concatenate(beside, axis=0)

    def beside_group(out):
        if inner == 1:
            return out
        total = reduce_owned(extended, group[frames:])
        for k in range(1, inner):
            part = total[:, :, (k - 1) * frames : k * frames]
            column_sums.append(part[:, frames : frames + 1])
            out = place(out, part[:, :frames] * scale / column_sums[k], z, y - k)
        return out

    def remote_group(s, out):
        left = jnp.concatenate([remote[s], jnp.zeros((8, pixels), jnp.bfloat16)], axis=0)
        total = reduce_owned(left, group, sums=remote[s])
        left_sums = jnp.transpose(total[:, frames : frames + 1, :frames], (0, 2, 1))
        value = total[:, :frames] * (size / left_sums) / jnp.concatenate(column_sums, axis=2)
        if 2 * s != outer:
            back = shift_z(results.encode(value), -s)
            back = results.decode(back)
            for k in range(inner):
                out = place(out, back[:, :, k * frames : (k + 1) * frames], z + s, y - k)
        for k in range(inner):
            block = jnp.transpose(value[:, :, k * frames : (k + 1) * frames], (0, 2, 1))
            if k > 0:
                block = results.decode(shift_y(results.encode(block), -k))
            out = place(out, block, z - s, y + k)
        return out

    out = beside_group(out)
    for s in range(1, half + 1):
        out = remote_group(s, out)
    return out


MESH = pl.DeviceIdType.MESH
TILE = 16
HALVES = 2


def fits_kernel(shape):
    inner = inner_extent(shape["tm"])
    return shape["tm"] // inner == 4 and inner == 2 and shape["pix"] == 4


def correlate(owned, partials, results, *refs):
    (own, onehot, cycle_map, out, wide, right, first, second, swap_out, swap_in, x_out, x_in, here,
     back_out, back_in, side_out, side_in, stash, sums_out, sums_core, sums_chip, sums_x,
     scale_own, scale_side, scale_first, scale_second, columns,
     core_send, core_recv, x_send, x_recv, y_send, y_recv, up_send, up_recv,
     back_send, back_recv, side_send, side_recv, sum_send, sum_recv) = refs
    frames, pixels = own.shape
    step = frames // HALVES
    deep = pixels // HALVES
    at_tm, at_pix = lax.axis_index("tm"), lax.axis_index("pix")
    z, y = at_tm // 2, at_tm % 2
    x, core = at_pix // 2, at_pix % 2
    to_y = {"tm": z * 2 + 1 - y}
    to_up = {"tm": (z + 1) % 4 * 2 + y}
    to_down = {"tm": (z + 3) % 4 * 2 + y}
    to_core = {"pix": x * 2 + 1 - core}
    to_x = {"pix": (1 - x) * 2 + core}

    barrier = pltpu.get_barrier_semaphore()
    for target in (to_y, to_up, to_down, to_core, to_x):
        pl.semaphore_signal(barrier, inc=1, device_id=target, device_id_type=MESH)
    pl.semaphore_wait(barrier, 5)

    def remote(source, target, send, recv, device):
        return pltpu.make_async_remote_copy(
            src_ref=source, dst_ref=target, send_sem=send, recv_sem=recv,
            device_id=device, device_id_type=MESH,
        )

    copies = []

    def start(*args):
        copy = remote(*args)
        copy.start()
        copies.append(copy)
        return copy

    part = lambda h: pl.ds(h * step, step)
    depth = lambda h: pl.ds(h * deep, deep)
    beside, ring1, ring2 = [], [], []
    for h in range(HALVES):
        beside.append(start(own.at[:, depth(h)], right.at[pl.ds(frames, frames), depth(h)],
                            y_send.at[h], y_recv.at[h], to_y))
        ring1.append(start(own.at[part(h)], first.at[part(h)], up_send.at[h], up_recv.at[h], to_up))

    counted = lax.dot_general(
        onehot[...], own[...], (((1,), (1,)), ((), ())), preferred_element_type=jnp.float32
    )
    size = jnp.sum(onehot[...].astype(jnp.float32), axis=1, keepdims=True)
    sums_out[:, pl.ds(0, frames)] = counted
    sums_out[:, pl.ds(frames, frames)] = jnp.broadcast_to(size, counted.shape)
    by_core = start(sums_out, sums_core, sum_send.at[0], sum_recv.at[0], to_core)

    def fill(r, carry):
        hit = jnp.broadcast_to(cycle_map[...], (TILE, pixels)) == r
        wide[r] = jnp.where(hit, 1.0, 0.0).astype(jnp.bfloat16)
        return carry

    lax.fori_loop(0, wide.shape[0] // 2, fill, 0)
    by_core.wait_recv()
    sums_chip[...] = sums_out[...] + sums_core[...]
    by_x = start(sums_chip, sums_x, sum_send.at[1], sum_recv.at[1], to_x)
    lax.fori_loop(wide.shape[0] // 2, wide.shape[0], fill, 0)
    right[pl.ds(0, frames), :] = own[...]
    by_x.wait_recv()
    mine = pl.ds(pl.multiple_of(at_pix * owned, owned), owned)
    scale_own[...] = sums_chip[mine, :] + sums_x[mine, :]
    by_y = start(scale_own, scale_side, sum_send.at[2], sum_recv.at[2], to_y)
    by_up = start(scale_own, scale_first, sum_send.at[3], sum_recv.at[3], to_up)

    bases = [((1 - x) * 2 + 1 - core) * owned, (x * 2 + 1 - core) * owned,
             ((1 - x) * 2 + core) * owned, at_pix * owned]

    def product(left, rows, count, group, ks, kc):
        block = left[rows, ks].reshape(count // TILE, TILE, kc)
        masked = jnp.concatenate(
            [(block * wide[bases[group] + i, :, ks][None]).reshape(count, kc) for i in range(owned)],
            axis=0,
        )
        value = lax.dot_general(
            masked, right[:, ks], (((1,), (1,)), ((), ())), preferred_element_type=jnp.float32
        )
        return value.reshape(owned, count, 2 * frames)

    def reduce_unit(n, u, left, lo, count, accumulate=False):
        rows = pl.ds(lo, count)
        ks, kc = (depth(HALVES - 1), deep) if accumulate else (pl.ds(0, pixels), pixels)
        away = []
        for g in range(2):
            value = product(left, rows, count, g, ks, kc)
            if accumulate:
                value = swap_out[u, g, :, rows] + value
            swap_out[u, g, :, rows] = value
            away.append(start(swap_out.at[u, g, :, rows], swap_in.at[u, g, :, rows],
                              core_send.at[n, g], core_recv.at[n, g], to_core))
        value = product(left, rows, count, 2, ks, kc)
        if accumulate:
            value = stash[...] + value
        away[0].wait_recv()
        x_out[u, :, rows] = partials.encode(value + swap_in[u, 0, :, rows])
        across = start(x_out.at[u, :, rows], x_in.at[u, :, rows], x_send.at[n], x_recv.at[n], to_x)
        value = product(left, rows, count, 3, ks, kc)
        if accumulate:
            value = here[u, :, rows] + value
        away[1].wait_recv()
        here[u, :, rows] = value + swap_in[u, 1, :, rows]
        return across

    def total(u, r, rows):
        return here[u, r, rows] + partials.decode(x_in[u, r, rows])

    def column_block(dz, dy):
        block = (z + dz + 4) % 4 * 2 + (y + dy) % 2
        return pl.ds(pl.multiple_of(block * frames, frames), frames)

    beside[0].wait_recv()
    for g, target in enumerate((swap_out.at[0, 0], swap_out.at[0, 1], stash, here.at[0])):
        if g == 1:
            ring1[0].wait_recv()
            ring2.append(start(first.at[part(0)], second.at[part(0)],
                               up_send.at[HALVES], up_recv.at[HALVES], to_up))
        target[...] = product(own, pl.ds(0, frames), frames, g, depth(0), deep)
    by_up.wait_recv()
    by_up2 = start(scale_first, scale_second, sum_send.at[4], sum_recv.at[4], to_up)
    beside[1].wait_recv()
    ring1[1].wait_recv()
    ring2.append(start(first.at[part(1)], second.at[part(1)],
                       up_send.at[HALVES + 1], up_recv.at[HALVES + 1], to_up))
    across_own = reduce_unit(0, 0, own, 0, frames, accumulate=True)
    across_first = reduce_unit(1, 1, first, 0, frames)

    by_y.wait_recv()
    by_up2.wait_recv()
    size = scale_own[:, pl.ds(frames, frames)]
    columns[0] = jnp.transpose(size / scale_own[:, pl.ds(0, frames)], (1, 0))
    columns[1] = jnp.transpose(size / scale_first[:, pl.ds(0, frames)], (1, 0))
    columns[2] = jnp.transpose(size / scale_second[:, pl.ds(0, frames)], (1, 0))
    lanes = jnp.concatenate(
        [1.0 / scale_own[:, pl.ds(0, frames)], 1.0 / scale_side[:, pl.ds(0, frames)]], axis=1
    )

    def normal(u, r, rows):
        return total(u, r, rows) * columns[u, rows, r : r + 1] * lanes[r : r + 1]

    across_own.wait_recv()
    every = pl.ds(0, frames)
    for r in range(owned):
        value = normal(0, r, every)
        out[r, :, column_block(0, 0)] = value[:, :frames]
        out[r, :, column_block(0, 1)] = value[:, frames:]

    across_second = []
    ring2[0].wait_recv()
    across_second.append(reduce_unit(2, 2, second, 0, step))

    across_first.wait_recv()
    for r in range(owned):
        value = normal(1, r, every)
        back_out[r] = results.encode(value)
        side_out[0, r] = results.encode(value[:, frames:])
        out[r, :, column_block(-1, 0)] = jnp.transpose(value[:, :frames], (1, 0))
    back = start(back_out, back_in, back_send, back_recv, to_down)
    side = [start(side_out.at[0], side_in.at[0], side_send.at[0], side_recv.at[0], to_y)]

    ring2[1].wait_recv()
    across_second.append(reduce_unit(3, 2, second, step, step))
    for h in range(HALVES):
        across_second[h].wait_recv()
        rows = part(h)
        for r in range(owned):
            value = normal(2, r, rows)
            stash[r, rows, pl.ds(0, frames)] = value[:, :frames]
            side_out[1, r, rows] = results.encode(value[:, frames:])
        side.append(start(side_out.at[1, :, rows], side_in.at[1, :, rows],
                          side_send.at[1 + h], side_recv.at[1 + h], to_y))

    for r in range(owned):
        out[r, :, column_block(-2, 0)] = jnp.transpose(stash[r, :, pl.ds(0, frames)], (1, 0))
    side[0].wait_recv()
    for r in range(owned):
        out[r, :, column_block(-1, 1)] = jnp.transpose(results.decode(side_in[0, r]), (1, 0))
    back.wait_recv()
    for r in range(owned):
        value = results.decode(back_in[r])
        out[r, :, column_block(1, 0)] = value[:, :frames]
        out[r, :, column_block(1, 1)] = value[:, frames:]
    for copy in side[1:]:
        copy.wait_recv()
    for r in range(owned):
        out[r, :, column_block(-2, 1)] = jnp.transpose(results.decode(side_in[1, r]), (1, 0))
    for copy in copies:
        copy.wait_send()


def per_device_kernel(counts, dead_time, flat_field, cycle_map):
    intensity = (counts / (1.0 - dead_time[None, :] * counts) * flat_field[None, :]).astype(
        jnp.bfloat16
    )
    frames, pixels = intensity.shape
    tm, pix = lax.axis_size("tm"), lax.axis_size("pix")
    owned = CYCLES // pix
    onehot = (cycle_map[None, :] == jnp.arange(CYCLES, dtype=jnp.int32)[:, None]).astype(jnp.bfloat16)
    partials = LogCode(0.0218, 6800.0 * pixels * 2, True)
    results = LogCode(1 / 140.0, 140.0, False)
    f32, bf16, i16 = jnp.float32, jnp.bfloat16, jnp.int16
    vmem, dma = pltpu.VMEM, pltpu.SemaphoreType.DMA
    both, small = 2 * frames, (owned, 2 * frames)
    scratch = [
        vmem((CYCLES, TILE, pixels), bf16),
        vmem((both, pixels), bf16),
        vmem((frames, pixels), bf16),
        vmem((frames, pixels), bf16),
        vmem((3, 2, owned, frames, both), f32),
        vmem((3, 2, owned, frames, both), f32),
        vmem((3, owned, frames, both), i16),
        vmem((3, owned, frames, both), i16),
        vmem((3, owned, frames, both), f32),
        vmem((owned, frames, both), i16),
        vmem((owned, frames, both), i16),
        vmem((2, owned, frames, frames), i16),
        vmem((2, owned, frames, frames), i16),
        vmem((owned, frames, both), f32),
        *[vmem((CYCLES, both), f32)] * 4,
        *[vmem(small, f32)] * 4,
        vmem((3, frames, owned), f32),
        dma((4, 2)), dma((4, 2)), dma((4,)), dma((4,)),
        dma((HALVES,)), dma((HALVES,)), dma((2 * HALVES,)), dma((2 * HALVES,)),
        dma, dma, dma((1 + HALVES,)), dma((1 + HALVES,)), dma((5,)), dma((5,)),
    ]
    return pl.pallas_call(
        functools.partial(correlate, owned, partials, results),
        out_shape=jax.ShapeDtypeStruct((owned, frames, tm * frames), f32),
        in_specs=[pl.BlockSpec(memory_space=pltpu.VMEM)] * 3,
        out_specs=pl.BlockSpec(memory_space=pltpu.VMEM),
        scratch_shapes=scratch,
        compiler_params=pltpu.CompilerParams(
            collective_id=0, has_side_effects=True, vmem_limit_bytes=63 << 20
        ),
    )(intensity, onehot, cycle_map[None, :])


def solution(mesh):
    kernel_path = fits_kernel(mesh.shape)
    device_program = per_device_kernel if kernel_path else per_device
    placed = (P("tm", "pix"), P("pix"), P("pix"), P("pix"))

    return jax.shard_map(
        device_program, mesh=mesh, in_specs=placed, out_specs=P("pix", "tm", None), check_vma=False
    )
```

```python
import functools
import math

import jax
import jax.numpy as jnp
from jax import lax
from jax.experimental import pallas as pl
from jax.experimental.pallas import tpu as pltpu
from jax.sharding import PartitionSpec as P

CYCLES = 32


def inner_extent(count):
    return max(d for d in range(1, count + 1) if count % d == 0 and d * d <= count)


class LogCode:
    def __init__(self, low, high, zero):
        self.low, self.zero = low, zero
        low, high = math.log2(low), math.log2(high)
        self.centre, self.steps = (high + low) / 2, 65400 / (high - low)

    def encode(self, value):
        level = (jnp.log2(jnp.maximum(value, self.low)) - self.centre) * self.steps
        return jnp.round(level).astype(jnp.int16)

    def decode(self, code):
        level = code.astype(jnp.float32)
        value = jnp.exp2(level * (1.0 / self.steps) + self.centre)
        return jnp.where(level > -32700 + 32, value, 0.0) if self.zero else value


def per_device(counts, dead_time, flat_field, cycle_map):
    intensity = (counts / (1.0 - dead_time[None, :] * counts) * flat_field[None, :]).astype(
        jnp.bfloat16
    )
    frames, pixels = intensity.shape
    tm, pix = lax.axis_size("tm"), lax.axis_size("pix")
    inner = inner_extent(tm)
    outer = tm // inner
    cores = 2 if pix % 2 == 0 else 1
    across = pix // cores
    owned = CYCLES // pix
    at_tm, at_pix = lax.axis_index("tm"), lax.axis_index("pix")
    z, y = at_tm // inner, at_tm % inner
    x, core = at_pix // cores, at_pix % cores

    def shift_z(value, k=1):
        return lax.ppermute(
            value, "tm", [(i, (i // inner + k) % outer * inner + i % inner) for i in range(tm)]
        )

    def shift_y(value, k):
        return lax.ppermute(
            value, "tm", [(i, i // inner * inner + (i % inner + k) % inner) for i in range(tm)]
        )

    def shift_x(value, k):
        return lax.ppermute(
            value, "pix", [(i, (i // cores + k) % across * cores + i % cores) for i in range(pix)]
        )

    def swap_core(value):
        return lax.ppermute(
            value, "pix", [(i, i // cores * cores + (i % cores + 1) % cores) for i in range(pix)]
        )

    half = outer // 2
    remote = {0: intensity}
    for s in range(1, half + 1):
        remote[s] = shift_z(remote[s - 1])
    beside = [intensity]
    for k in range(1, inner):
        beside.append(shift_y(intensity, k))

    def onehot_of(owner_core, ks):
        ids = jnp.concatenate(
            [
                ((x + k) % across * cores + owner_core) * owned
                + jnp.arange(owned, dtype=jnp.int32)
                for k in ks
            ]
        )
        return (cycle_map[None, :] == ids[:, None]).astype(jnp.bfloat16)

    other = (core + 1) % cores
    away_ks, own_ks = range(1, across), range(1)
    rows = frames + 8

    def gram(onehot, left, right, sums):
        masked = (onehot[:, None, :] * left[None, :, :]).reshape(-1, pixels)
        value = lax.dot_general(
            masked, right, (((1,), (1,)), ((), ())), preferred_element_type=jnp.float32
        ).reshape(onehot.shape[0], rows, right.shape[0])
        if sums is not None:
            own = lax.dot_general(
                onehot, sums, (((1,), (1,)), ((), ())), preferred_element_type=jnp.float32
            )
            value = value + jnp.pad(
                own[:, None, :], ((0, 0), (frames, 7), (0, right.shape[0] - frames))
            )
        return value

    partials = LogCode(0.0218, 6800.0 * pixels * cores, True)
    results = LogCode(1 / 140.0, 140.0, False)

    def reduce_owned(left, right, sums=None, exact=False):
        def part(owner_core, ks):
            return gram(onehot_of(owner_core, ks), left, right, sums)

        theirs = {}
        for name, ks in (("o", away_ks), ("x", own_ks)):
            if cores > 1 and len(ks):
                theirs[name] = swap_core(part(other, ks))
        total = None
        if across > 1:
            sent = part(core, away_ks)
            if cores > 1:
                sent = sent + theirs["o"]
            got = []
            for k in range(1, across):
                value = sent[(k - 1) * owned : k * owned]
                if not exact:
                    value = partials.encode(value)
                value = shift_x(value, k)
                got.append(value if exact else partials.decode(value))
            total = sum(got[1:], got[0])
        here = part(core, own_ks)
        if cores > 1:
            here = here + theirs["x"]
        here = lax.optimization_barrier(here)
        return here if total is None else here + total

    out = jnp.zeros((owned, frames, tm * frames), jnp.float32)

    def place(out, value, zs, ys):
        at = (zs % outer * inner + ys % inner) * frames
        return lax.dynamic_update_slice_in_dim(out, value, at, 2)

    ones = jnp.ones((8, pixels), jnp.bfloat16)
    extended = jnp.concatenate([intensity, ones], axis=0)
    total = reduce_owned(extended, extended, exact=True)
    row_sums = total[:, :frames, frames]
    scale = total[:, frames, frames][:, None, None] / row_sums[:, :, None]
    column_sums = [total[:, frames : frames + 1, :frames]]
    size = total[:, frames : frames + 1, frames : frames + 1]
    out = place(out, total[:, :frames, :frames] * scale / column_sums[0], z, y)
    group = jnp.concatenate(beside, axis=0)

    def beside_group(out):
        if inner == 1:
            return out
        total = reduce_owned(extended, group[frames:])
        for k in range(1, inner):
            part = total[:, :, (k - 1) * frames : k * frames]
            column_sums.append(part[:, frames : frames + 1])
            out = place(out, part[:, :frames] * scale / column_sums[k], z, y - k)
        return out

    def remote_group(s, out):
        left = jnp.concatenate([remote[s], jnp.zeros((8, pixels), jnp.bfloat16)], axis=0)
        total = reduce_owned(left, group, sums=remote[s])
        left_sums = jnp.transpose(total[:, frames : frames + 1, :frames], (0, 2, 1))
        value = total[:, :frames] * (size / left_sums) / jnp.concatenate(column_sums, axis=2)
        if 2 * s != outer:
            back = shift_z(results.encode(value), -s)
            back = results.decode(back)
            for k in range(inner):
                out = place(out, back[:, :, k * frames : (k + 1) * frames], z + s, y - k)
        for k in range(inner):
            block = jnp.transpose(value[:, :, k * frames : (k + 1) * frames], (0, 2, 1))
            if k > 0:
                block = results.decode(shift_y(results.encode(block), -k))
            out = place(out, block, z - s, y + k)
        return out

    out = beside_group(out)
    for s in range(1, half + 1):
        out = remote_group(s, out)
    return out


MESH = pl.DeviceIdType.MESH
TILE = 16
CHUNKS = 2


def fits_kernel(shape):
    inner = inner_extent(shape["tm"])
    return shape["tm"] // inner == 4 and inner == 2 and shape["pix"] == 4


def exchange(owned, partials, results, *refs):
    (counts, dead_time, flat_field, cycle_map,
     diagonal, pair, local, side_in, back_in,
     wide, right, ring, swap_out, swap_in, x_out, x_in, here, side_out, back_out,
     diag_out, diag_in, diag_x_out, diag_x_in, diag_here,
     pair_out, pair_in, pair_x_out, pair_x_in, pair_here,
     sums_out, sums_core, sums_chip, sums_x, scale_own, scale_side, scale_first, scale_second,
     columns, pair_columns,
     core_send, core_recv, x_send, x_recv, up_send, up_recv, back_send, back_recv,
     side_send, side_recv, diag_send, diag_recv, pair_send, pair_recv, sum_send, sum_recv) = refs
    frames, pixels = counts.shape
    step, last = frames // CHUNKS, 2 * CHUNKS - 1
    at_tm, at_pix = lax.axis_index("tm"), lax.axis_index("pix")
    z, y = at_tm // 2, at_tm % 2
    x, core = at_pix // 2, at_pix % 2
    to_y = {"tm": z * 2 + 1 - y}
    to_up = {"tm": (z + 1) % 4 * 2 + y}
    to_down = {"tm": (z + 3) % 4 * 2 + y}
    to_core = {"pix": x * 2 + 1 - core}
    to_x = {"pix": (1 - x) * 2 + core}
    own, beside, every = pl.ds(0, frames), pl.ds(frames, frames), pl.ds(0, 2 * frames)

    barrier = pltpu.get_barrier_semaphore()
    for target in (to_y, to_up, to_down, to_core, to_x):
        pl.semaphore_signal(barrier, inc=1, device_id=target, device_id_type=MESH)

    def correct(i, carry):
        rows = pl.ds(pl.multiple_of(i * TILE, TILE), TILE)
        raw = counts[rows, :]
        value = raw / (1.0 - dead_time[...] * raw) * flat_field[...]
        right[rows, :] = value.astype(jnp.bfloat16)
        return carry

    lax.fori_loop(0, frames // TILE, correct, 0)
    pl.semaphore_wait(barrier, 5)

    def remote(source, target, send, recv, device):
        return pltpu.make_async_remote_copy(
            src_ref=source, dst_ref=target, send_sem=send, recv_sem=recv,
            device_id=device, device_id_type=MESH,
        )

    copies = []

    def start(*args):
        copy = remote(*args)
        copy.start()
        copies.append(copy)
        return copy

    def chunk(n):
        return pl.ds(pl.multiple_of(n * step, step), step)

    by_side = start(right.at[own], right.at[beside], side_send.at[0], side_recv.at[0], to_y)
    for n in range(CHUNKS):
        start(right.at[chunk(n)], ring.at[chunk(n)], up_send.at[n], up_recv.at[n], to_up)

    def forward(n):
        copy = remote(ring.at[chunk(n)], ring.at[chunk(n + CHUNKS)],
                      up_send.at[n + CHUNKS], up_recv.at[n + CHUNKS], to_up)
        return copy

    def landed(n):
        remote(ring.at[chunk(n)], ring.at[chunk(n)], up_send.at[n], up_recv.at[n], to_up).wait_recv()

    ids = lax.broadcasted_iota(jnp.int32, (CYCLES, pixels), 0)
    onehot = jnp.where(jnp.broadcast_to(cycle_map[...], (CYCLES, pixels)) == ids, 1.0, 0.0)
    counted = lax.dot_general(
        onehot.astype(jnp.bfloat16), right[own, :], (((1,), (1,)), ((), ())),
        preferred_element_type=jnp.float32,
    )
    size = jnp.sum(onehot, axis=1, keepdims=True)
    sums_out[:, own] = counted
    sums_out[:, beside] = jnp.broadcast_to(size, counted.shape)
    by_core = start(sums_out, sums_core, sum_send.at[0], sum_recv.at[0], to_core)

    def fill(r, carry):
        hit = jnp.broadcast_to(cycle_map[...], (TILE, pixels)) == r
        wide[r] = jnp.where(hit, 1.0, 0.0).astype(jnp.bfloat16)
        return carry

    lax.fori_loop(0, CYCLES // 2, fill, 0)
    by_core.wait_recv()
    sums_chip[...] = sums_out[...] + sums_core[...]
    by_x = start(sums_chip, sums_x, sum_send.at[1], sum_recv.at[1], to_x)
    lax.fori_loop(CYCLES // 2, CYCLES, fill, 0)

    bases = [((1 - x) * 2 + 1 - core) * owned, (x * 2 + 1 - core) * owned,
             ((1 - x) * 2 + core) * owned, at_pix * owned]

    def reduce_unit(left, rows, count, cols, out, inn, code_out, code_in, kept, csem, xsem):
        def product(group):
            block = left[rows, :].reshape(count // TILE, TILE, pixels)
            masked = jnp.concatenate(
                [(block * wide[bases[group] + i][None]).reshape(count, pixels) for i in range(owned)],
                axis=0,
            )
            value = lax.dot_general(
                masked, right[cols, :], (((1,), (1,)), ((), ())), preferred_element_type=jnp.float32
            )
            return value.reshape(owned, count, cols.size)

        away = []
        for g in range(2):
            out[g] = product(g)
            copy = remote(out.at[g], inn.at[g], csem[0].at[g], csem[1].at[g], to_core)
            copy.start()
            away.append(copy)
        value = product(2)
        away[0].wait_recv()
        code_out[...] = partials.encode(value + inn[0])
        across = remote(code_out, code_in, xsem[0], xsem[1], to_x)
        across.start()
        value = product(3)
        away[1].wait_recv()
        kept[...] = value + inn[1]
        return [*away, across]

    def part(refs, n):
        return [ref.at[n] for ref in refs]

    diag_sems = (diag_send, diag_recv)
    sent = reduce_unit(right, own, frames, own, diag_out, diag_in, diag_x_out, diag_x_in, diag_here,
                       diag_sems, part(diag_sems, 2))
    copies += sent
    by_x.wait_recv()
    mine = pl.ds(pl.multiple_of(at_pix * owned, owned), owned)
    scale_own[...] = sums_chip[mine, :] + sums_x[mine, :]
    by_y = start(scale_own, scale_side, sum_send.at[2], sum_recv.at[2], to_y)
    by_up = start(scale_own, scale_first, sum_send.at[3], sum_recv.at[3], to_up)

    def pass_on(n):
        landed(n)
        copy = forward(n)
        copy.start()
        copies.append(copy)

    for n in range(CHUNKS - 1):
        pass_on(n)
    by_up.wait_recv()
    by_up2 = start(scale_first, scale_second, sum_send.at[4], sum_recv.at[4], to_up)
    size = scale_own[:, beside]
    own_sums = scale_own[:, own]
    own_columns = jnp.transpose(size / own_sums, (1, 0))
    sent[2].wait_recv()
    for r in range(owned):
        value = diag_here[r] + partials.decode(diag_x_in[r])
        diagonal[r] = value * own_columns[:, r : r + 1] * (1.0 / own_sums[r : r + 1])

    by_y.wait_recv()
    side_sums = scale_side[:, own]
    lower = y == 0
    pair_columns[...] = jnp.transpose(size / jnp.where(lower, own_sums, side_sums), (1, 0))
    pair_lanes = 1.0 / jnp.where(lower, side_sums, own_sums)
    lanes = 1.0 / jnp.concatenate([own_sums, side_sums], axis=1)
    columns[own, :] = jnp.transpose(size / scale_first[:, own], (1, 0))
    by_up2.wait_recv()
    columns[beside, :] = jnp.transpose(size / scale_second[:, own], (1, 0))

    by_side.wait_recv()
    pass_on(CHUNKS - 1)
    half = frames // 2
    half_rows = pl.ds(pl.multiple_of(y * half, half), half)
    pair_sems = (pair_send, pair_recv)
    sent = reduce_unit(right, pl.ds(pl.multiple_of(y * (frames + half), half), half), half,
                       pl.ds(pl.multiple_of((1 - y) * frames, frames), frames),
                       pair_out, pair_in, pair_x_out, pair_x_in, pair_here,
                       pair_sems, part(pair_sems, 2))
    copies += sent

    core_sems, x_sems = (core_send, core_recv), (x_send, x_recv)

    def unit(n):
        return reduce_unit(ring, chunk(n), step, every, swap_out.at[n], swap_in.at[n],
                           x_out.at[n], x_in.at[n], here.at[n], part(core_sems, n), part(x_sems, n))

    def to_side(n):
        return remote(side_out.at[n], side_in.at[:, chunk(n)],
                      side_send.at[1 + n], side_recv.at[1 + n], to_y)

    def to_back(n):
        return remote(back_out.at[n], back_in.at[:, chunk(n)], back_send.at[n], back_recv.at[n], to_down)

    def finish(n, back):
        remote(x_out.at[n], x_in.at[n], x_send.at[n], x_recv.at[n], to_x).wait_recv()
        for r in range(owned):
            value = here[n, r] + partials.decode(x_in[n, r])
            value = value * columns[chunk(n), r : r + 1] * lanes[r : r + 1]
            local[r, chunk(n), :] = value[:, :frames]
            code = results.encode(value)
            side_out[n, r] = code[:, frames:]
            if back:
                back_out[n, r] = code
        if back:
            to_back(n).start()
        to_side(n).start()

    copies += unit(0)
    sent[2].wait_recv()
    for r in range(owned):
        value = pair_here[r] + partials.decode(pair_x_in[r])
        value = value * pair_columns[half_rows, r : r + 1] * pair_lanes[r : r + 1]
        pair[r, half_rows, :] = results.encode(value)
    by_pair = start(pair.at[:, half_rows], pair.at[:, half_rows], pair_send.at[3], pair_recv.at[3], to_y)
    for n in range(1, 2 * CHUNKS):
        if n >= CHUNKS:
            landed(n)
        copies += unit(n)
        finish(n - 1, n - 1 < CHUNKS)
    finish(last, False)
    by_pair.wait_recv()
    for n in range(2 * CHUNKS):
        copies.append(to_side(n))
        copies[-1].wait_recv()
    for n in range(CHUNKS):
        copies.append(to_back(n))
        copies[-1].wait_recv()
    for copy in copies:
        copy.wait_send()


def assemble(results, diagonal, pair, local, side, back, out):
    frames = diagonal.shape[1]
    at_tm = lax.axis_index("tm")
    z, y = at_tm // 2, at_tm % 2

    def put(dz, dy, value):
        block = (z + dz + 4) % 4 * 2 + (y + dy) % 2
        out[0, :, pl.ds(pl.multiple_of(block * frames, frames), frames)] = value

    def turn(value):
        return jnp.transpose(value, (1, 0))

    put(0, 0, diagonal[0])
    value = results.decode(pair[0])
    put(0, 1, jnp.where(y == 0, value, turn(value)))
    for s in range(2):
        rows = pl.ds(s * frames, frames)
        put(-1 - s, 0, turn(local[0, rows, :]))
        put(-1 - s, 1, turn(results.decode(side[0, rows, :])))
    value = results.decode(back[0])
    put(1, 0, value[:, :frames])
    put(1, 1, value[:, frames:])


def per_device_kernel(counts, dead_time, flat_field, cycle_map):
    frames, pixels = counts.shape
    tm, pix = lax.axis_size("tm"), lax.axis_size("pix")
    owned = CYCLES // pix
    partials = LogCode(0.0218, 6800.0 * pixels * 2, True)
    results = LogCode(1 / 140.0, 140.0, False)
    f32, bf16, i16 = jnp.float32, jnp.bfloat16, jnp.int16
    vmem, dma = pltpu.VMEM, pltpu.SemaphoreType.DMA
    both, half, step, units = 2 * frames, frames // 2, frames // CHUNKS, 2 * CHUNKS
    small = (owned, both)
    scratch = [
        vmem((CYCLES, TILE, pixels), bf16),
        vmem((both, pixels), bf16),
        vmem((both, pixels), bf16),
        *[vmem((units, 2, owned, step, both), f32)] * 2,
        *[vmem((units, owned, step, both), i16)] * 2,
        vmem((units, owned, step, both), f32),
        vmem((units, owned, step, frames), i16),
        vmem((CHUNKS, owned, step, both), i16),
        *[vmem((2, owned, frames, frames), f32)] * 2,
        *[vmem((owned, frames, frames), i16)] * 2,
        vmem((owned, frames, frames), f32),
        *[vmem((2, owned, half, frames), f32)] * 2,
        *[vmem((owned, half, frames), i16)] * 2,
        vmem((owned, half, frames), f32),
        *[vmem((CYCLES, both), f32)] * 4,
        *[vmem(small, f32)] * 4,
        vmem((both, owned), f32),
        vmem((frames, owned), f32),
        dma((units, 2)), dma((units, 2)), dma((units,)), dma((units,)),
        dma((units,)), dma((units,)), dma((CHUNKS,)), dma((CHUNKS,)),
        dma((1 + units,)), dma((1 + units,)), dma((3,)), dma((3,)), dma((4,)), dma((4,)),
        dma((5,)), dma((5,)),
    ]
    shapes = [
        ((owned, frames, frames), f32), ((owned, frames, frames), i16),
        ((owned, both, frames), f32), ((owned, both, frames), i16), ((owned, frames, both), i16),
    ]
    pieces = pl.pallas_call(
        functools.partial(exchange, owned, partials, results),
        out_shape=[jax.ShapeDtypeStruct(*shape) for shape in shapes],
        in_specs=[pl.BlockSpec(memory_space=pltpu.VMEM)] * 4,
        out_specs=[pl.BlockSpec(memory_space=pltpu.VMEM)] * 5,
        scratch_shapes=scratch,
        compiler_params=pltpu.CompilerParams(
            collective_id=0, has_side_effects=True, vmem_limit_bytes=60 << 20
        ),
    )(counts, dead_time[None, :], flat_field[None, :], cycle_map[None, :])
    return pl.pallas_call(
        functools.partial(assemble, results),
        grid=(owned,),
        out_shape=jax.ShapeDtypeStruct((owned, frames, tm * frames), f32),
        in_specs=[pl.BlockSpec((1, *shape[1:]), lambda r: (r, 0, 0)) for shape, _ in shapes],
        out_specs=pl.BlockSpec((1, frames, tm * frames), lambda r: (r, 0, 0)),
    )(*pieces)


def solution(mesh):
    kernel_path = fits_kernel(mesh.shape)
    device_program = per_device_kernel if kernel_path else per_device
    placed = (P("tm", "pix"), P("pix"), P("pix"), P("pix"))

    return jax.shard_map(
        device_program, mesh=mesh, in_specs=placed, out_specs=P("pix", "tm", None), check_vma=False
    )
```

```python
import functools
import math

import jax
import jax.numpy as jnp
from jax import lax
from jax.experimental import pallas as pl
from jax.experimental.pallas import tpu as pltpu
from jax.sharding import PartitionSpec as P

CYCLES = 32


def inner_extent(count):
    return max(d for d in range(1, count + 1) if count % d == 0 and d * d <= count)


class LogCode:
    def __init__(self, low, high, zero):
        self.low, self.zero = low, zero
        low, high = math.log2(low), math.log2(high)
        self.centre, self.steps = (high + low) / 2, 65400 / (high - low)

    def encode(self, value):
        level = (jnp.log2(jnp.maximum(value, self.low)) - self.centre) * self.steps
        return jnp.round(level).astype(jnp.int16)

    def decode(self, code):
        level = code.astype(jnp.float32)
        value = jnp.exp2(level * (1.0 / self.steps) + self.centre)
        return jnp.where(level > -32700 + 32, value, 0.0) if self.zero else value


def per_device(counts, dead_time, flat_field, cycle_map):
    intensity = (counts / (1.0 - dead_time[None, :] * counts) * flat_field[None, :]).astype(
        jnp.bfloat16
    )
    frames, pixels = intensity.shape
    tm, pix = lax.axis_size("tm"), lax.axis_size("pix")
    inner = inner_extent(tm)
    outer = tm // inner
    cores = 2 if pix % 2 == 0 else 1
    across = pix // cores
    owned = CYCLES // pix
    at_tm, at_pix = lax.axis_index("tm"), lax.axis_index("pix")
    z, y = at_tm // inner, at_tm % inner
    x, core = at_pix // cores, at_pix % cores

    def shift_z(value, k=1):
        return lax.ppermute(
            value, "tm", [(i, (i // inner + k) % outer * inner + i % inner) for i in range(tm)]
        )

    def shift_y(value, k):
        return lax.ppermute(
            value, "tm", [(i, i // inner * inner + (i % inner + k) % inner) for i in range(tm)]
        )

    def shift_x(value, k):
        return lax.ppermute(
            value, "pix", [(i, (i // cores + k) % across * cores + i % cores) for i in range(pix)]
        )

    def swap_core(value):
        return lax.ppermute(
            value, "pix", [(i, i // cores * cores + (i % cores + 1) % cores) for i in range(pix)]
        )

    half = outer // 2
    remote = {0: intensity}
    for s in range(1, half + 1):
        remote[s] = shift_z(remote[s - 1])
    beside = [intensity]
    for k in range(1, inner):
        beside.append(shift_y(intensity, k))

    def onehot_of(owner_core, ks):
        ids = jnp.concatenate(
            [
                ((x + k) % across * cores + owner_core) * owned
                + jnp.arange(owned, dtype=jnp.int32)
                for k in ks
            ]
        )
        return (cycle_map[None, :] == ids[:, None]).astype(jnp.bfloat16)

    other = (core + 1) % cores
    away_ks, own_ks = range(1, across), range(1)
    rows = frames + 8

    def gram(onehot, left, right, sums):
        masked = (onehot[:, None, :] * left[None, :, :]).reshape(-1, pixels)
        value = lax.dot_general(
            masked, right, (((1,), (1,)), ((), ())), preferred_element_type=jnp.float32
        ).reshape(onehot.shape[0], rows, right.shape[0])
        if sums is not None:
            own = lax.dot_general(
                onehot, sums, (((1,), (1,)), ((), ())), preferred_element_type=jnp.float32
            )
            value = value + jnp.pad(
                own[:, None, :], ((0, 0), (frames, 7), (0, right.shape[0] - frames))
            )
        return value

    partials = LogCode(0.0218, 6800.0 * pixels * cores, True)
    results = LogCode(1 / 140.0, 140.0, False)

    def reduce_owned(left, right, sums=None, exact=False):
        def part(owner_core, ks):
            return gram(onehot_of(owner_core, ks), left, right, sums)

        theirs = {}
        for name, ks in (("o", away_ks), ("x", own_ks)):
            if cores > 1 and len(ks):
                theirs[name] = swap_core(part(other, ks))
        total = None
        if across > 1:
            sent = part(core, away_ks)
            if cores > 1:
                sent = sent + theirs["o"]
            got = []
            for k in range(1, across):
                value = sent[(k - 1) * owned : k * owned]
                if not exact:
                    value = partials.encode(value)
                value = shift_x(value, k)
                got.append(value if exact else partials.decode(value))
            total = sum(got[1:], got[0])
        here = part(core, own_ks)
        if cores > 1:
            here = here + theirs["x"]
        here = lax.optimization_barrier(here)
        return here if total is None else here + total

    out = jnp.zeros((owned, frames, tm * frames), jnp.float32)

    def place(out, value, zs, ys):
        at = (zs % outer * inner + ys % inner) * frames
        return lax.dynamic_update_slice_in_dim(out, value, at, 2)

    ones = jnp.ones((8, pixels), jnp.bfloat16)
    extended = jnp.concatenate([intensity, ones], axis=0)
    total = reduce_owned(extended, extended, exact=True)
    row_sums = total[:, :frames, frames]
    scale = total[:, frames, frames][:, None, None] / row_sums[:, :, None]
    column_sums = [total[:, frames : frames + 1, :frames]]
    size = total[:, frames : frames + 1, frames : frames + 1]
    out = place(out, total[:, :frames, :frames] * scale / column_sums[0], z, y)
    group = jnp.concatenate(beside, axis=0)

    def beside_group(out):
        if inner == 1:
            return out
        total = reduce_owned(extended, group[frames:])
        for k in range(1, inner):
            part = total[:, :, (k - 1) * frames : k * frames]
            column_sums.append(part[:, frames : frames + 1])
            out = place(out, part[:, :frames] * scale / column_sums[k], z, y - k)
        return out

    def remote_group(s, out):
        left = jnp.concatenate([remote[s], jnp.zeros((8, pixels), jnp.bfloat16)], axis=0)
        total = reduce_owned(left, group, sums=remote[s])
        left_sums = jnp.transpose(total[:, frames : frames + 1, :frames], (0, 2, 1))
        value = total[:, :frames] * (size / left_sums) / jnp.concatenate(column_sums, axis=2)
        if 2 * s != outer:
            back = shift_z(results.encode(value), -s)
            back = results.decode(back)
            for k in range(inner):
                out = place(out, back[:, :, k * frames : (k + 1) * frames], z + s, y - k)
        for k in range(inner):
            block = jnp.transpose(value[:, :, k * frames : (k + 1) * frames], (0, 2, 1))
            if k > 0:
                block = results.decode(shift_y(results.encode(block), -k))
            out = place(out, block, z - s, y + k)
        return out

    out = beside_group(out)
    for s in range(1, half + 1):
        out = remote_group(s, out)
    return out


MESH = pl.DeviceIdType.MESH
TILE = 16
CHUNKS = 2


def fits_kernel(shape):
    inner = inner_extent(shape["tm"])
    return shape["tm"] // inner == 4 and inner == 2 and shape["pix"] == 4


def exchange(owned, partials, results, *refs):
    (counts, dead_time, flat_field, cycle_map,
     diagonal, pair, local, side_in, back_in,
     wide, right, ring, swap_out, swap_in, x_out, x_in, here, side_out, back_out,
     diag_out, diag_in, diag_x_out, diag_x_in, diag_here,
     pair_out, pair_in, pair_x_out, pair_x_in, pair_here,
     sums_out, sums_core, sums_chip, sums_x, scale_own, scale_side, scale_first, scale_second,
     columns, pair_columns, lanes,
     core_send, core_recv, x_send, x_recv, up_send, up_recv, back_send, back_recv,
     side_send, side_recv, diag_send, diag_recv, pair_send, pair_recv, sum_send, sum_recv) = refs
    frames, pixels = counts.shape
    step, last = frames // CHUNKS, 2 * CHUNKS - 1
    at_tm, at_pix = lax.axis_index("tm"), lax.axis_index("pix")
    z, y = at_tm // 2, at_tm % 2
    x, core = at_pix // 2, at_pix % 2
    to_y = {"tm": z * 2 + 1 - y}
    to_up = {"tm": (z + 1) % 4 * 2 + y}
    to_down = {"tm": (z + 3) % 4 * 2 + y}
    to_core = {"pix": x * 2 + 1 - core}
    to_x = {"pix": (1 - x) * 2 + core}
    own, beside, every = pl.ds(0, frames), pl.ds(frames, frames), pl.ds(0, 2 * frames)

    barrier = pltpu.get_barrier_semaphore()
    for target in (to_y, to_up, to_down, to_core, to_x):
        pl.semaphore_signal(barrier, inc=1, device_id=target, device_id_type=MESH)

    def correct(i, carry):
        rows = pl.ds(pl.multiple_of(i * TILE, TILE), TILE)
        raw = counts[rows, :]
        value = raw / (1.0 - dead_time[...] * raw) * flat_field[...]
        right[rows, :] = value.astype(jnp.bfloat16)
        return carry

    lax.fori_loop(0, frames // TILE, correct, 0)
    pl.semaphore_wait(barrier, 5)

    def remote(source, target, send, recv, device):
        return pltpu.make_async_remote_copy(
            src_ref=source, dst_ref=target, send_sem=send, recv_sem=recv,
            device_id=device, device_id_type=MESH,
        )

    copies = []

    def start(*args):
        copy = remote(*args)
        copy.start()
        copies.append(copy)
        return copy

    def chunk(n):
        return pl.ds(pl.multiple_of(n * step, step), step)

    by_side = start(right.at[own], right.at[beside], side_send.at[0], side_recv.at[0], to_y)

    def to_ring(n):
        return remote(right.at[chunk(n)], ring.at[chunk(n)], up_send.at[n], up_recv.at[n], to_up)

    def forward(n):
        return remote(ring.at[chunk(n)], ring.at[chunk(n + CHUNKS)],
                      up_send.at[n + CHUNKS], up_recv.at[n + CHUNKS], to_up)

    copies += [to_ring(n) for n in range(CHUNKS)] + [forward(n) for n in range(CHUNKS)]
    to_ring(0).start()

    ids = lax.broadcasted_iota(jnp.int32, (CYCLES, pixels), 0)
    onehot = jnp.where(jnp.broadcast_to(cycle_map[...], (CYCLES, pixels)) == ids, 1.0, 0.0)
    counted = lax.dot_general(
        onehot.astype(jnp.bfloat16), right[own, :], (((1,), (1,)), ((), ())),
        preferred_element_type=jnp.float32,
    )
    size = jnp.sum(onehot, axis=1, keepdims=True)
    sums_out[:, own] = counted
    sums_out[:, beside] = jnp.broadcast_to(size, counted.shape)
    by_core = start(sums_out, sums_core, sum_send.at[0], sum_recv.at[0], to_core)

    def fill(r, carry):
        hit = jnp.broadcast_to(cycle_map[...], (TILE, pixels)) == r
        wide[r] = jnp.where(hit, 1.0, 0.0).astype(jnp.bfloat16)
        return carry

    lax.fori_loop(0, CYCLES // 2, fill, 0)
    by_core.wait_recv()
    sums_chip[...] = sums_out[...] + sums_core[...]
    by_x = start(sums_chip, sums_x, sum_send.at[1], sum_recv.at[1], to_x)
    lax.fori_loop(CYCLES // 2, CYCLES, fill, 0)
    by_x.wait_recv()
    mine = pl.ds(pl.multiple_of(at_pix * owned, owned), owned)
    scale_own[...] = sums_chip[mine, :] + sums_x[mine, :]
    by_y = start(scale_own, scale_side, sum_send.at[2], sum_recv.at[2], to_y)
    by_up = start(scale_own, scale_first, sum_send.at[3], sum_recv.at[3], to_up)
    for n in range(1, CHUNKS):
        to_ring(n).start()

    away_base, own_base = (1 - x) * 2 * owned, x * 2 * owned

    def reduce_unit(left, rows, count, cols, made, to_other, inn, code_out, to_across, kept):
        def product(j, carry):
            owner_core = lax.rem(core + 1 + j, 2)
            block = left[rows, :].reshape(count // TILE, TILE, pixels)
            masked = jnp.concatenate(
                [
                    (block * wide[base + owner_core * owned + i][None]).reshape(count, pixels)
                    for base in (away_base, own_base)
                    for i in range(owned)
                ],
                axis=0,
            )
            value = lax.dot_general(
                masked, right[cols, :], (((1,), (1,)), ((), ())), preferred_element_type=jnp.float32
            )
            made[j] = value.reshape(2, owned, count, cols.size)

            @pl.when(j == 0)
            def _():
                to_other.start()

            return carry

        lax.fori_loop(0, 2, product, 0)
        to_other.wait_recv()
        code_out[...] = partials.encode(made[1, 0] + inn[0])
        to_across.start()
        kept[...] = made[1, 1] + inn[1]

    half = frames // 2

    def diag_core(n):
        return remote(diag_out.at[n, 0], diag_in.at[n], diag_send.at[n], diag_recv.at[n], to_core)

    def diag_across(n):
        return remote(diag_x_out.at[n], diag_x_in.at[n],
                      diag_send.at[2 + n], diag_recv.at[2 + n], to_x)

    def diag_unit(n, carry):
        rows = pl.ds(pl.multiple_of(n * half, half), half)
        reduce_unit(right, rows, half, own, diag_out.at[n], diag_core(n), diag_in.at[n],
                    diag_x_out.at[n], diag_across(n), diag_here.at[n])
        return carry

    lax.fori_loop(0, 2, diag_unit, 0)
    copies += [diag_core(0), diag_core(1), diag_across(0), diag_across(1)]

    def pass_on(n):
        remote(ring.at[chunk(n)], ring.at[chunk(n)], up_send.at[n], up_recv.at[n], to_up).wait_recv()
        forward(n).start()

    by_up.wait_recv()
    by_up2 = start(scale_first, scale_second, sum_send.at[4], sum_recv.at[4], to_up)
    for n in range(CHUNKS - 1):
        pass_on(n)
    size = scale_own[:, beside]
    own_sums = scale_own[:, own]
    own_columns = jnp.transpose(size / own_sums, (1, 0))
    columns[own, :] = jnp.transpose(size / scale_first[:, own], (1, 0))
    for n in range(2):
        rows = pl.ds(n * half, half)
        diag_across(n).wait_recv()
        for r in range(owned):
            value = diag_here[n, r] + partials.decode(diag_x_in[n, r])
            value = value * own_columns[n * half : (n + 1) * half, r : r + 1]
            diagonal[r, rows, :] = value * (1.0 / own_sums[r : r + 1])

    by_side.wait_recv()
    pass_on(CHUNKS - 1)
    half_rows = pl.ds(pl.multiple_of(y * half, half), half)
    pair_core = remote(pair_out.at[0], pair_in, pair_send.at[0], pair_recv.at[0], to_core)
    pair_across = remote(pair_x_out, pair_x_in, pair_send.at[1], pair_recv.at[1], to_x)
    reduce_unit(right, pl.ds(pl.multiple_of(y * (frames + half), half), half), half,
                pl.ds(pl.multiple_of((1 - y) * frames, frames), frames),
                pair_out, pair_core, pair_in, pair_x_out, pair_across, pair_here)
    copies += [pair_core, pair_across]

    by_y.wait_recv()
    side_sums = scale_side[:, own]
    lower = y == 0
    pair_columns[...] = jnp.transpose(size / jnp.where(lower, own_sums, side_sums), (1, 0))
    pair_lanes = 1.0 / jnp.where(lower, side_sums, own_sums)
    lanes[...] = 1.0 / jnp.concatenate([own_sums, side_sums], axis=1)

    def to_other(n):
        return remote(swap_out.at[n, 0], swap_in.at[n], core_send.at[n], core_recv.at[n], to_core)

    def to_across(n):
        return remote(x_out.at[n], x_in.at[n], x_send.at[n], x_recv.at[n], to_x)

    def to_side(n):
        return remote(side_out.at[n], side_in.at[n], side_send.at[1 + n], side_recv.at[1 + n], to_y)

    def to_back(n):
        return remote(back_out.at[n], back_in.at[:, chunk(n)], back_send.at[n], back_recv.at[n], to_down)

    by_pair = remote(pair.at[:, half_rows], pair.at[:, half_rows],
                     pair_send.at[2], pair_recv.at[2], to_y)

    def finish(n):
        to_across(n).wait_recv()

        for r in range(owned):
            value = here[n, r] + partials.decode(x_in[n, r])
            value = value * columns[chunk(n), r : r + 1] * lanes[r : r + 1, :]
            back_out[n, r] = results.encode(value)
            turned = jnp.transpose(value, (1, 0))
            side_out[n, r] = results.encode(turned[frames:])
            local[n, r] = turned[:frames]

        @pl.when(n < CHUNKS)
        def _():
            to_back(n).start()

        to_side(n).start()

    def unit(n, carry):
        @pl.when(n >= CHUNKS)
        def _():
            remote(ring.at[chunk(n)], ring.at[chunk(n)],
                   up_send.at[n], up_recv.at[n], to_up).wait_recv()

        reduce_unit(ring, chunk(n), step, every, swap_out.at[n], to_other(n), swap_in.at[n],
                    x_out.at[n], to_across(n), here.at[n])

        @pl.when(n == 0)
        def _():
            pair_across.wait_recv()
            for r in range(owned):
                value = pair_here[r] + partials.decode(pair_x_in[r])
                value = value * pair_columns[half_rows, r : r + 1] * pair_lanes[r : r + 1]
                pair[r, half_rows, :] = results.encode(value)
            by_pair.start()

        @pl.when(n == 1)
        def _():
            by_up2.wait_recv()
            columns[beside, :] = jnp.transpose(size / scale_second[:, own], (1, 0))

        @pl.when(n > 0)
        def _():
            finish(n - 1)

        return carry

    lax.fori_loop(0, 2 * CHUNKS, unit, 0)
    finish(jnp.int32(last))
    by_pair.wait_recv()
    copies.append(by_pair)
    for n in range(2 * CHUNKS):
        copies += [to_other(n), to_across(n), to_side(n)]
        to_side(n).wait_recv()
    for n in range(CHUNKS):
        copies.append(to_back(n))
        to_back(n).wait_recv()
    for copy in copies:
        copy.wait_send()


def assemble(results, diagonal, pair, local, side, back, out):
    frames = diagonal.shape[1]
    at_tm = lax.axis_index("tm")
    z, y = at_tm // 2, at_tm % 2

    def put(dz, dy, value):
        block = (z + dz + 4) % 4 * 2 + (y + dy) % 2
        out[0, :, pl.ds(pl.multiple_of(block * frames, frames), frames)] = value

    def turn(value):
        return jnp.transpose(value, (1, 0))

    put(0, 0, diagonal[0])

    @pl.when(y == 0)
    def _():
        put(0, 1, results.decode(pair[0]))

    @pl.when(y == 1)
    def _():
        put(0, 1, turn(results.decode(pair[0])))

    for s in range(2):
        chunks = range(s * CHUNKS, (s + 1) * CHUNKS)
        put(-1 - s, 0, jnp.concatenate([local[n, 0] for n in chunks], axis=1))
        put(-1 - s, 1, results.decode(jnp.concatenate([side[n, 0] for n in chunks], axis=1)))
    value = results.decode(back[0])
    put(1, 0, value[:, :frames])
    put(1, 1, value[:, frames:])


def per_device_kernel(counts, dead_time, flat_field, cycle_map):
    frames, pixels = counts.shape
    tm, pix = lax.axis_size("tm"), lax.axis_size("pix")
    owned = CYCLES // pix
    partials = LogCode(0.0218, 6800.0 * pixels * 2, True)
    results = LogCode(1 / 140.0, 140.0, False)
    f32, bf16, i16 = jnp.float32, jnp.bfloat16, jnp.int16
    vmem, dma = pltpu.VMEM, pltpu.SemaphoreType.DMA
    both, half, step, units = 2 * frames, frames // 2, frames // CHUNKS, 2 * CHUNKS
    small = (owned, both)
    scratch = [
        vmem((CYCLES, TILE, pixels), bf16),
        vmem((both, pixels), bf16),
        vmem((both, pixels), bf16),
        vmem((units, 2, 2, owned, step, both), f32),
        vmem((units, 2, owned, step, both), f32),
        *[vmem((units, owned, step, both), i16)] * 2,
        vmem((units, owned, step, both), f32),
        vmem((units, owned, frames, step), i16),
        vmem((units, owned, step, both), i16),
        vmem((2, 2, 2, owned, half, frames), f32),
        vmem((2, 2, owned, half, frames), f32),
        *[vmem((2, owned, half, frames), i16)] * 2,
        vmem((2, owned, half, frames), f32),
        vmem((2, 2, owned, half, frames), f32),
        vmem((2, owned, half, frames), f32),
        *[vmem((owned, half, frames), i16)] * 2,
        vmem((owned, half, frames), f32),
        *[vmem((CYCLES, both), f32)] * 4,
        *[vmem(small, f32)] * 4,
        vmem((both, owned), f32),
        vmem((frames, owned), f32),
        vmem(small, f32),
        dma((units,)), dma((units,)), dma((units,)), dma((units,)),
        dma((units,)), dma((units,)), dma((CHUNKS,)), dma((CHUNKS,)),
        dma((1 + units,)), dma((1 + units,)), dma((4,)), dma((4,)), dma((3,)), dma((3,)),
        dma((5,)), dma((5,)),
    ]
    shapes = [
        ((owned, frames, frames), f32), ((owned, frames, frames), i16),
        ((units, owned, frames, step), f32), ((units, owned, frames, step), i16),
        ((owned, frames, both), i16),
    ]
    pieces = pl.pallas_call(
        functools.partial(exchange, owned, partials, results),
        out_shape=[jax.ShapeDtypeStruct(*shape) for shape in shapes],
        in_specs=[pl.BlockSpec(memory_space=pltpu.VMEM)] * 4,
        out_specs=[pl.BlockSpec(memory_space=pltpu.VMEM)] * 5,
        scratch_shapes=scratch,
        compiler_params=pltpu.CompilerParams(
            collective_id=0, has_side_effects=True, vmem_limit_bytes=60 << 20
        ),
    )(counts, dead_time[None, :], flat_field[None, :], cycle_map[None, :])
    return pl.pallas_call(
        functools.partial(assemble, results),
        grid=(owned,),
        out_shape=jax.ShapeDtypeStruct((owned, frames, tm * frames), f32),
        in_specs=[
            pl.BlockSpec((1, *shape[1:]), lambda r: (r, 0, 0))
            if len(shape) == 3
            else pl.BlockSpec((shape[0], 1, *shape[2:]), lambda r: (0, r, 0, 0))
            for shape, _ in shapes
        ],
        out_specs=pl.BlockSpec((1, frames, tm * frames), lambda r: (r, 0, 0)),
    )(*pieces)


def solution(mesh):
    kernel_path = fits_kernel(mesh.shape)
    device_program = per_device_kernel if kernel_path else per_device
    placed = (P("tm", "pix"), P("pix"), P("pix"), P("pix"))

    return jax.shard_map(
        device_program, mesh=mesh, in_specs=placed, out_specs=P("pix", "tm", None), check_vma=False
    )
```

```python
import functools
import math

import jax
import jax.numpy as jnp
from jax import lax
from jax.experimental import pallas as pl
from jax.experimental.pallas import tpu as pltpu
from jax.sharding import PartitionSpec as P

CYCLES = 32


def inner_extent(count):
    return max(d for d in range(1, count + 1) if count % d == 0 and d * d <= count)


class LogCode:
    def __init__(self, low, high, zero):
        self.low, self.zero = low, zero
        low, high = math.log2(low), math.log2(high)
        self.centre, self.steps = (high + low) / 2, 65400 / (high - low)

    def encode(self, value):
        level = (jnp.log2(jnp.maximum(value, self.low)) - self.centre) * self.steps
        return jnp.round(level).astype(jnp.int16)

    def decode(self, code):
        level = code.astype(jnp.float32)
        value = jnp.exp2(level * (1.0 / self.steps) + self.centre)
        return jnp.where(level > -32700 + 32, value, 0.0) if self.zero else value


def per_device(counts, dead_time, flat_field, cycle_map):
    intensity = (counts / (1.0 - dead_time[None, :] * counts) * flat_field[None, :]).astype(
        jnp.bfloat16
    )
    frames, pixels = intensity.shape
    tm, pix = lax.axis_size("tm"), lax.axis_size("pix")
    inner = inner_extent(tm)
    outer = tm // inner
    cores = 2 if pix % 2 == 0 else 1
    across = pix // cores
    owned = CYCLES // pix
    at_tm, at_pix = lax.axis_index("tm"), lax.axis_index("pix")
    z, y = at_tm // inner, at_tm % inner
    x, core = at_pix // cores, at_pix % cores

    def shift_z(value, k=1):
        return lax.ppermute(
            value, "tm", [(i, (i // inner + k) % outer * inner + i % inner) for i in range(tm)]
        )

    def shift_y(value, k):
        return lax.ppermute(
            value, "tm", [(i, i // inner * inner + (i % inner + k) % inner) for i in range(tm)]
        )

    def shift_x(value, k):
        return lax.ppermute(
            value, "pix", [(i, (i // cores + k) % across * cores + i % cores) for i in range(pix)]
        )

    def swap_core(value):
        return lax.ppermute(
            value, "pix", [(i, i // cores * cores + (i % cores + 1) % cores) for i in range(pix)]
        )

    half = outer // 2
    remote = {0: intensity}
    for s in range(1, half + 1):
        remote[s] = shift_z(remote[s - 1])
    beside = [intensity]
    for k in range(1, inner):
        beside.append(shift_y(intensity, k))

    def onehot_of(owner_core, ks):
        ids = jnp.concatenate(
            [
                ((x + k) % across * cores + owner_core) * owned
                + jnp.arange(owned, dtype=jnp.int32)
                for k in ks
            ]
        )
        return (cycle_map[None, :] == ids[:, None]).astype(jnp.bfloat16)

    other = (core + 1) % cores
    away_ks, own_ks = range(1, across), range(1)
    rows = frames + 8

    def gram(onehot, left, right, sums):
        masked = (onehot[:, None, :] * left[None, :, :]).reshape(-1, pixels)
        value = lax.dot_general(
            masked, right, (((1,), (1,)), ((), ())), preferred_element_type=jnp.float32
        ).reshape(onehot.shape[0], rows, right.shape[0])
        if sums is not None:
            own = lax.dot_general(
                onehot, sums, (((1,), (1,)), ((), ())), preferred_element_type=jnp.float32
            )
            value = value + jnp.pad(
                own[:, None, :], ((0, 0), (frames, 7), (0, right.shape[0] - frames))
            )
        return value

    partials = LogCode(0.0218, 6800.0 * pixels * cores, True)
    results = LogCode(1 / 140.0, 140.0, False)

    def reduce_owned(left, right, sums=None, exact=False):
        def part(owner_core, ks):
            return gram(onehot_of(owner_core, ks), left, right, sums)

        theirs = {}
        for name, ks in (("o", away_ks), ("x", own_ks)):
            if cores > 1 and len(ks):
                theirs[name] = swap_core(part(other, ks))
        total = None
        if across > 1:
            sent = part(core, away_ks)
            if cores > 1:
                sent = sent + theirs["o"]
            got = []
            for k in range(1, across):
                value = sent[(k - 1) * owned : k * owned]
                if not exact:
                    value = partials.encode(value)
                value = shift_x(value, k)
                got.append(value if exact else partials.decode(value))
            total = sum(got[1:], got[0])
        here = part(core, own_ks)
        if cores > 1:
            here = here + theirs["x"]
        here = lax.optimization_barrier(here)
        return here if total is None else here + total

    out = jnp.zeros((owned, frames, tm * frames), jnp.float32)

    def place(out, value, zs, ys):
        at = (zs % outer * inner + ys % inner) * frames
        return lax.dynamic_update_slice_in_dim(out, value, at, 2)

    ones = jnp.ones((8, pixels), jnp.bfloat16)
    extended = jnp.concatenate([intensity, ones], axis=0)
    total = reduce_owned(extended, extended, exact=True)
    row_sums = total[:, :frames, frames]
    scale = total[:, frames, frames][:, None, None] / row_sums[:, :, None]
    column_sums = [total[:, frames : frames + 1, :frames]]
    size = total[:, frames : frames + 1, frames : frames + 1]
    out = place(out, total[:, :frames, :frames] * scale / column_sums[0], z, y)
    group = jnp.concatenate(beside, axis=0)

    def beside_group(out):
        if inner == 1:
            return out
        total = reduce_owned(extended, group[frames:])
        for k in range(1, inner):
            part = total[:, :, (k - 1) * frames : k * frames]
            column_sums.append(part[:, frames : frames + 1])
            out = place(out, part[:, :frames] * scale / column_sums[k], z, y - k)
        return out

    def remote_group(s, out):
        left = jnp.concatenate([remote[s], jnp.zeros((8, pixels), jnp.bfloat16)], axis=0)
        total = reduce_owned(left, group, sums=remote[s])
        left_sums = jnp.transpose(total[:, frames : frames + 1, :frames], (0, 2, 1))
        value = total[:, :frames] * (size / left_sums) / jnp.concatenate(column_sums, axis=2)
        if 2 * s != outer:
            back = shift_z(results.encode(value), -s)
            back = results.decode(back)
            for k in range(inner):
                out = place(out, back[:, :, k * frames : (k + 1) * frames], z + s, y - k)
        for k in range(inner):
            block = jnp.transpose(value[:, :, k * frames : (k + 1) * frames], (0, 2, 1))
            if k > 0:
                block = results.decode(shift_y(results.encode(block), -k))
            out = place(out, block, z - s, y + k)
        return out

    out = beside_group(out)
    for s in range(1, half + 1):
        out = remote_group(s, out)
    return out


MESH = pl.DeviceIdType.MESH
TILE = 16
CHUNKS = 2


def fits_kernel(shape):
    inner = inner_extent(shape["tm"])
    return shape["tm"] // inner == 4 and inner == 2 and shape["pix"] == 4


def exchange(owned, partials, results, *refs):
    (counts, dead_time, flat_field, cycle_map,
     diagonal, pair, local, side_in, back_in, diag_rows, pair_rows, local_rows, local_turned,
     wide, right, ring, swap_out, swap_in, x_out, x_in, here, side_out, back_out,
     diag_out, diag_in, diag_x_out, diag_x_in, diag_here,
     pair_out, pair_in, pair_x_out, pair_x_in, pair_here,
     sums_out, sums_core, sums_chip, sums_x, scale_own, scale_side, scale_first, scale_second,
     columns, pair_columns, lanes,
     core_send, core_recv, x_send, x_recv, up_send, up_recv, back_send, back_recv,
     side_send, side_recv, diag_send, diag_recv, pair_send, pair_recv, sum_send, sum_recv, keep_sem) = refs
    frames, pixels = counts.shape
    step, last = frames // CHUNKS, 2 * CHUNKS - 1
    at_tm, at_pix = lax.axis_index("tm"), lax.axis_index("pix")
    z, y = at_tm // 2, at_tm % 2
    x, core = at_pix // 2, at_pix % 2
    to_y = {"tm": z * 2 + 1 - y}
    to_up = {"tm": (z + 1) % 4 * 2 + y}
    to_down = {"tm": (z + 3) % 4 * 2 + y}
    to_core = {"pix": x * 2 + 1 - core}
    to_x = {"pix": (1 - x) * 2 + core}
    own, beside, every = pl.ds(0, frames), pl.ds(frames, frames), pl.ds(0, 2 * frames)

    barrier = pltpu.get_barrier_semaphore()
    for target in (to_y, to_up, to_down, to_core, to_x):
        pl.semaphore_signal(barrier, inc=1, device_id=target, device_id_type=MESH)

    def correct(i, carry):
        rows = pl.ds(pl.multiple_of(i * TILE, TILE), TILE)
        raw = counts[rows, :]
        value = raw / (1.0 - dead_time[...] * raw) * flat_field[...]
        right[rows, :] = value.astype(jnp.bfloat16)
        return carry

    lax.fori_loop(0, frames // TILE, correct, 0)
    pl.semaphore_wait(barrier, 5)

    def remote(source, target, send, recv, device):
        return pltpu.make_async_remote_copy(
            src_ref=source, dst_ref=target, send_sem=send, recv_sem=recv,
            device_id=device, device_id_type=MESH,
        )

    copies = []

    def start(*args):
        copy = remote(*args)
        copy.start()
        copies.append(copy)
        return copy

    def chunk(n):
        return pl.ds(pl.multiple_of(n * step, step), step)

    by_side = start(right.at[own], right.at[beside], side_send.at[0], side_recv.at[0], to_y)

    def to_ring(n):
        return remote(right.at[chunk(n)], ring.at[chunk(n)], up_send.at[n], up_recv.at[n], to_up)

    def forward(n):
        return remote(ring.at[chunk(n)], ring.at[chunk(n + CHUNKS)],
                      up_send.at[n + CHUNKS], up_recv.at[n + CHUNKS], to_up)

    copies += [to_ring(n) for n in range(CHUNKS)] + [forward(n) for n in range(CHUNKS)]
    to_ring(0).start()

    ids = lax.broadcasted_iota(jnp.int32, (CYCLES, pixels), 0)
    onehot = jnp.where(jnp.broadcast_to(cycle_map[...], (CYCLES, pixels)) == ids, 1.0, 0.0)
    counted = lax.dot_general(
        onehot.astype(jnp.bfloat16), right[own, :], (((1,), (1,)), ((), ())),
        preferred_element_type=jnp.float32,
    )
    size = jnp.sum(onehot, axis=1, keepdims=True)
    sums_out[:, own] = counted
    sums_out[:, beside] = jnp.broadcast_to(size, counted.shape)
    by_core = start(sums_out, sums_core, sum_send.at[0], sum_recv.at[0], to_core)

    def fill(r, carry):
        hit = jnp.broadcast_to(cycle_map[...], (TILE, pixels)) == r
        wide[r] = jnp.where(hit, 1.0, 0.0).astype(jnp.bfloat16)
        return carry

    lax.fori_loop(0, CYCLES // 2, fill, 0)
    by_core.wait_recv()
    sums_chip[...] = sums_out[...] + sums_core[...]
    by_x = start(sums_chip, sums_x, sum_send.at[1], sum_recv.at[1], to_x)
    lax.fori_loop(CYCLES // 2, CYCLES, fill, 0)
    by_x.wait_recv()
    mine = pl.ds(pl.multiple_of(at_pix * owned, owned), owned)
    scale_own[...] = sums_chip[mine, :] + sums_x[mine, :]
    by_y = start(scale_own, scale_side, sum_send.at[2], sum_recv.at[2], to_y)
    by_up = start(scale_own, scale_first, sum_send.at[3], sum_recv.at[3], to_up)
    for n in range(1, CHUNKS):
        to_ring(n).start()

    away_base, own_base = (1 - x) * 2 * owned, x * 2 * owned

    def reduce_unit(left, rows, count, cols, made, to_other, inn, code_out, to_across, kept):
        def product(j, carry):
            owner_core = lax.rem(core + 1 + j, 2)
            block = left[rows, :].reshape(count // TILE, TILE, pixels)
            masked = jnp.concatenate(
                [
                    (block * wide[base + owner_core * owned + i][None]).reshape(count, pixels)
                    for base in (away_base, own_base)
                    for i in range(owned)
                ],
                axis=0,
            )
            value = lax.dot_general(
                masked, right[cols, :], (((1,), (1,)), ((), ())), preferred_element_type=jnp.float32
            )
            made[j] = value.reshape(2, owned, count, cols.size)

            @pl.when(j == 0)
            def _():
                to_other.start()

            return carry

        lax.fori_loop(0, 2, product, 0)
        to_other.wait_recv()
        code_out[...] = partials.encode(made[1, 0] + inn[0])
        to_across.start()
        kept[...] = made[1, 1] + inn[1]

    half = frames // 2

    def keep(source, target, n):
        return pltpu.make_async_copy(source, target, keep_sem.at[n])

    def diag_core(n):
        return remote(diag_out.at[n, 0], diag_in.at[n], diag_send.at[n], diag_recv.at[n], to_core)

    def diag_across(n):
        return remote(diag_x_out.at[n], diag_x_in.at[n],
                      diag_send.at[2 + n], diag_recv.at[2 + n], to_x)

    def diag_unit(n, carry):
        rows = pl.ds(pl.multiple_of(n * half, half), half)
        reduce_unit(right, rows, half, own, diag_out.at[n], diag_core(n), diag_in.at[n],
                    diag_x_out.at[n], diag_across(n), diag_here.at[n])
        return carry

    lax.fori_loop(0, 2, diag_unit, 0)
    copies += [diag_core(0), diag_core(1), diag_across(0), diag_across(1)]

    def pass_on(n):
        remote(ring.at[chunk(n)], ring.at[chunk(n)], up_send.at[n], up_recv.at[n], to_up).wait_recv()
        forward(n).start()

    by_up.wait_recv()
    by_up2 = start(scale_first, scale_second, sum_send.at[4], sum_recv.at[4], to_up)
    for n in range(CHUNKS - 1):
        pass_on(n)
    size = scale_own[:, beside]
    own_sums = scale_own[:, own]
    own_columns = jnp.transpose(size / own_sums, (1, 0))
    columns[own, :] = jnp.transpose(size / scale_first[:, own], (1, 0))
    for n in range(2):
        rows = pl.ds(n * half, half)
        diag_across(n).wait_recv()
        for r in range(owned):
            value = diag_here[n, r] + partials.decode(diag_x_in[n, r])
            value = value * own_columns[n * half : (n + 1) * half, r : r + 1]
            diag_rows[r, rows, :] = value * (1.0 / own_sums[r : r + 1])
    keep(diag_rows, diagonal, 0).start()

    by_side.wait_recv()
    pass_on(CHUNKS - 1)
    half_rows = pl.ds(pl.multiple_of(y * half, half), half)
    pair_core = remote(pair_out.at[0], pair_in, pair_send.at[0], pair_recv.at[0], to_core)
    pair_across = remote(pair_x_out, pair_x_in, pair_send.at[1], pair_recv.at[1], to_x)
    reduce_unit(right, pl.ds(pl.multiple_of(y * (frames + half), half), half), half,
                pl.ds(pl.multiple_of((1 - y) * frames, frames), frames),
                pair_out, pair_core, pair_in, pair_x_out, pair_across, pair_here)
    copies += [pair_core, pair_across]

    by_y.wait_recv()
    side_sums = scale_side[:, own]
    lower = y == 0
    pair_columns[...] = jnp.transpose(size / jnp.where(lower, own_sums, side_sums), (1, 0))
    pair_lanes = 1.0 / jnp.where(lower, side_sums, own_sums)
    lanes[...] = 1.0 / jnp.concatenate([own_sums, side_sums], axis=1)

    def to_other(n):
        return remote(swap_out.at[n, 0], swap_in.at[n], core_send.at[n], core_recv.at[n], to_core)

    def to_across(n):
        return remote(x_out.at[n], x_in.at[n], x_send.at[n], x_recv.at[n], to_x)

    def to_side(n):
        return remote(side_out.at[n], side_in.at[:, chunk(n)], side_send.at[1 + n], side_recv.at[1 + n], to_y)

    def to_back(n):
        return remote(back_out.at[n], back_in.at[:, chunk(n)], back_send.at[n], back_recv.at[n], to_down)

    by_pair = remote(pair_rows, pair.at[:, half_rows], pair_send.at[2], pair_recv.at[2], to_y)

    def finish(n):
        to_across(n).wait_recv()

        for r in range(owned):
            value = here[n, r] + partials.decode(x_in[n, r])
            value = value * columns[chunk(n), r : r + 1] * lanes[r : r + 1, :]
            back_out[n, r] = results.encode(value)
            side_out[n, r] = results.encode(value[:, frames:])
            local_rows[r, chunk(n), :] = value[:, :frames]

        @pl.when(n < CHUNKS)
        def _():
            to_back(n).start()

        to_side(n).start()

    def turn(s):
        for r in range(owned):
            local_turned[s, r] = jnp.transpose(local_rows[r, pl.ds(s * frames, frames), :], (1, 0))
        keep(local_turned.at[s], local.at[s], 1 + s).start()

    def unit(n, carry):
        @pl.when(n >= CHUNKS)
        def _():
            remote(ring.at[chunk(n)], ring.at[chunk(n)],
                   up_send.at[n], up_recv.at[n], to_up).wait_recv()

        reduce_unit(ring, chunk(n), step, every, swap_out.at[n], to_other(n), swap_in.at[n],
                    x_out.at[n], to_across(n), here.at[n])

        @pl.when(n == 0)
        def _():
            pair_across.wait_recv()
            for r in range(owned):
                value = pair_here[r] + partials.decode(pair_x_in[r])
                value = value * pair_columns[half_rows, r : r + 1] * pair_lanes[r : r + 1]
                pair_rows[r] = results.encode(value)
            by_pair.start()
            keep(pair_rows, pair.at[:, half_rows], 3).start()

        @pl.when(n == 1)
        def _():
            by_up2.wait_recv()
            columns[beside, :] = jnp.transpose(size / scale_second[:, own], (1, 0))

        @pl.when(n > 0)
        def _():
            finish(n - 1)

        @pl.when(n == CHUNKS)
        def _():
            turn(0)

        return carry

    lax.fori_loop(0, 2 * CHUNKS, unit, 0)
    finish(jnp.int32(last))
    turn(1)
    by_pair.wait_recv()
    copies.append(by_pair)
    for n in range(2 * CHUNKS):
        copies += [to_other(n), to_across(n), to_side(n)]
        to_side(n).wait_recv()
    for n in range(CHUNKS):
        copies.append(to_back(n))
        to_back(n).wait_recv()
    keep(diag_rows, diagonal, 0).wait()
    for s in range(2):
        keep(local_turned.at[s], local.at[s], 1 + s).wait()
    keep(pair_rows, pair.at[:, half_rows], 3).wait()
    for copy in copies:
        copy.wait_send()


def assemble(results, diagonal, pair, local, side, back, out):
    frames = diagonal.shape[1]
    at_tm = lax.axis_index("tm")
    z, y = at_tm // 2, at_tm % 2

    def put(dz, dy, value):
        block = (z + dz + 4) % 4 * 2 + (y + dy) % 2
        out[0, :, pl.ds(pl.multiple_of(block * frames, frames), frames)] = value

    def turn(value):
        return jnp.transpose(value, (1, 0))

    put(0, 0, diagonal[0])

    @pl.when(y == 0)
    def _():
        put(0, 1, results.decode(pair[0]))

    @pl.when(y == 1)
    def _():
        put(0, 1, turn(results.decode(pair[0])))

    for s in range(2):
        put(-1 - s, 0, local[s, 0])
        put(-1 - s, 1, turn(results.decode(side[0, pl.ds(s * frames, frames), :])))
    value = results.decode(back[0])
    put(1, 0, value[:, :frames])
    put(1, 1, value[:, frames:])


def per_device_kernel(counts, dead_time, flat_field, cycle_map):
    frames, pixels = counts.shape
    tm, pix = lax.axis_size("tm"), lax.axis_size("pix")
    owned = CYCLES // pix
    partials = LogCode(0.0218, 6800.0 * pixels * 2, True)
    results = LogCode(1 / 140.0, 140.0, False)
    f32, bf16, i16 = jnp.float32, jnp.bfloat16, jnp.int16
    vmem, dma = pltpu.VMEM, pltpu.SemaphoreType.DMA
    both, half, step, units = 2 * frames, frames // 2, frames // CHUNKS, 2 * CHUNKS
    small = (owned, both)
    scratch = [
        vmem((owned, frames, frames), f32),
        vmem((owned, half, frames), i16),
        vmem((owned, both, frames), f32),
        vmem((2, owned, frames, frames), f32),
        vmem((CYCLES, TILE, pixels), bf16),
        vmem((both, pixels), bf16),
        vmem((both, pixels), bf16),
        vmem((units, 2, 2, owned, step, both), f32),
        vmem((units, 2, owned, step, both), f32),
        *[vmem((units, owned, step, both), i16)] * 2,
        vmem((units, owned, step, both), f32),
        vmem((units, owned, step, frames), i16),
        vmem((units, owned, step, both), i16),
        vmem((2, 2, 2, owned, half, frames), f32),
        vmem((2, 2, owned, half, frames), f32),
        *[vmem((2, owned, half, frames), i16)] * 2,
        vmem((2, owned, half, frames), f32),
        vmem((2, 2, owned, half, frames), f32),
        vmem((2, owned, half, frames), f32),
        *[vmem((owned, half, frames), i16)] * 2,
        vmem((owned, half, frames), f32),
        *[vmem((CYCLES, both), f32)] * 4,
        *[vmem(small, f32)] * 4,
        vmem((both, owned), f32),
        vmem((frames, owned), f32),
        vmem(small, f32),
        dma((units,)), dma((units,)), dma((units,)), dma((units,)),
        dma((units,)), dma((units,)), dma((CHUNKS,)), dma((CHUNKS,)),
        dma((1 + units,)), dma((1 + units,)), dma((4,)), dma((4,)), dma((3,)), dma((3,)),
        dma((5,)), dma((5,)), dma((4,)),
    ]
    shapes = [
        ((owned, frames, frames), f32), ((owned, frames, frames), i16),
        ((2, owned, frames, frames), f32), ((owned, both, frames), i16), ((owned, frames, both), i16),
    ]
    pieces = pl.pallas_call(
        functools.partial(exchange, owned, partials, results),
        out_shape=[jax.ShapeDtypeStruct(*shape) for shape in shapes],
        in_specs=[pl.BlockSpec(memory_space=pltpu.VMEM)] * 4,
        out_specs=[pl.BlockSpec(memory_space=pl.ANY)] * 5,
        scratch_shapes=scratch,
        compiler_params=pltpu.CompilerParams(
            collective_id=0, has_side_effects=True, vmem_limit_bytes=60 << 20
        ),
    )(counts, dead_time[None, :], flat_field[None, :], cycle_map[None, :])
    return pl.pallas_call(
        functools.partial(assemble, results),
        grid=(owned,),
        out_shape=jax.ShapeDtypeStruct((owned, frames, tm * frames), f32),
        in_specs=[
            pl.BlockSpec((1, *shape[1:]), lambda r: (r, 0, 0))
            if len(shape) == 3
            else pl.BlockSpec((shape[0], 1, *shape[2:]), lambda r: (0, r, 0, 0))
            for shape, _ in shapes
        ],
        out_specs=pl.BlockSpec((1, frames, tm * frames), lambda r: (r, 0, 0)),
    )(*pieces)


def solution(mesh):
    kernel_path = fits_kernel(mesh.shape)
    device_program = per_device_kernel if kernel_path else per_device
    placed = (P("tm", "pix"), P("pix"), P("pix"), P("pix"))

    return jax.shard_map(
        device_program, mesh=mesh, in_specs=placed, out_specs=P("pix", "tm", None), check_vma=False
    )
```

```python
import functools
import math

import jax
import jax.numpy as jnp
from jax import lax
from jax.experimental import pallas as pl
from jax.experimental.pallas import tpu as pltpu
from jax.sharding import PartitionSpec as P

CYCLES = 32


def inner_extent(count):
    return max(d for d in range(1, count + 1) if count % d == 0 and d * d <= count)


class LogCode:
    def __init__(self, low, high, zero):
        self.low, self.zero = low, zero
        low, high = math.log2(low), math.log2(high)
        self.centre, self.steps = (high + low) / 2, 65400 / (high - low)

    def encode(self, value):
        level = (jnp.log2(jnp.maximum(value, self.low)) - self.centre) * self.steps
        return jnp.round(level).astype(jnp.int16)

    def decode(self, code):
        level = code.astype(jnp.float32)
        value = jnp.exp2(level * (1.0 / self.steps) + self.centre)
        return jnp.where(level > -32700 + 32, value, 0.0) if self.zero else value


def per_device(counts, dead_time, flat_field, cycle_map):
    intensity = (counts / (1.0 - dead_time[None, :] * counts) * flat_field[None, :]).astype(
        jnp.bfloat16
    )
    frames, pixels = intensity.shape
    tm, pix = lax.axis_size("tm"), lax.axis_size("pix")
    inner = inner_extent(tm)
    outer = tm // inner
    cores = 2 if pix % 2 == 0 else 1
    across = pix // cores
    owned = CYCLES // pix
    at_tm, at_pix = lax.axis_index("tm"), lax.axis_index("pix")
    z, y = at_tm // inner, at_tm % inner
    x, core = at_pix // cores, at_pix % cores

    def shift_z(value, k=1):
        return lax.ppermute(
            value, "tm", [(i, (i // inner + k) % outer * inner + i % inner) for i in range(tm)]
        )

    def shift_y(value, k):
        return lax.ppermute(
            value, "tm", [(i, i // inner * inner + (i % inner + k) % inner) for i in range(tm)]
        )

    def shift_x(value, k):
        return lax.ppermute(
            value, "pix", [(i, (i // cores + k) % across * cores + i % cores) for i in range(pix)]
        )

    def swap_core(value):
        return lax.ppermute(
            value, "pix", [(i, i // cores * cores + (i % cores + 1) % cores) for i in range(pix)]
        )

    half = outer // 2
    remote = {0: intensity}
    for s in range(1, half + 1):
        remote[s] = shift_z(remote[s - 1])
    beside = [intensity]
    for k in range(1, inner):
        beside.append(shift_y(intensity, k))

    def onehot_of(owner_core, ks):
        ids = jnp.concatenate(
            [
                ((x + k) % across * cores + owner_core) * owned
                + jnp.arange(owned, dtype=jnp.int32)
                for k in ks
            ]
        )
        return (cycle_map[None, :] == ids[:, None]).astype(jnp.bfloat16)

    other = (core + 1) % cores
    away_ks, own_ks = range(1, across), range(1)
    rows = frames + 8

    def gram(onehot, left, right, sums):
        masked = (onehot[:, None, :] * left[None, :, :]).reshape(-1, pixels)
        value = lax.dot_general(
            masked, right, (((1,), (1,)), ((), ())), preferred_element_type=jnp.float32
        ).reshape(onehot.shape[0], rows, right.shape[0])
        if sums is not None:
            own = lax.dot_general(
                onehot, sums, (((1,), (1,)), ((), ())), preferred_element_type=jnp.float32
            )
            value = value + jnp.pad(
                own[:, None, :], ((0, 0), (frames, 7), (0, right.shape[0] - frames))
            )
        return value

    partials = LogCode(0.0218, 6800.0 * pixels * cores, True)
    results = LogCode(1 / 140.0, 140.0, False)

    def reduce_owned(left, right, sums=None, exact=False):
        def part(owner_core, ks):
            return gram(onehot_of(owner_core, ks), left, right, sums)

        theirs = {}
        for name, ks in (("o", away_ks), ("x", own_ks)):
            if cores > 1 and len(ks):
                theirs[name] = swap_core(part(other, ks))
        total = None
        if across > 1:
            sent = part(core, away_ks)
            if cores > 1:
                sent = sent + theirs["o"]
            got = []
            for k in range(1, across):
                value = sent[(k - 1) * owned : k * owned]
                if not exact:
                    value = partials.encode(value)
                value = shift_x(value, k)
                got.append(value if exact else partials.decode(value))
            total = sum(got[1:], got[0])
        here = part(core, own_ks)
        if cores > 1:
            here = here + theirs["x"]
        here = lax.optimization_barrier(here)
        return here if total is None else here + total

    out = jnp.zeros((owned, frames, tm * frames), jnp.float32)

    def place(out, value, zs, ys):
        at = (zs % outer * inner + ys % inner) * frames
        return lax.dynamic_update_slice_in_dim(out, value, at, 2)

    ones = jnp.ones((8, pixels), jnp.bfloat16)
    extended = jnp.concatenate([intensity, ones], axis=0)
    total = reduce_owned(extended, extended, exact=True)
    row_sums = total[:, :frames, frames]
    scale = total[:, frames, frames][:, None, None] / row_sums[:, :, None]
    column_sums = [total[:, frames : frames + 1, :frames]]
    size = total[:, frames : frames + 1, frames : frames + 1]
    out = place(out, total[:, :frames, :frames] * scale / column_sums[0], z, y)
    group = jnp.concatenate(beside, axis=0)

    def beside_group(out):
        if inner == 1:
            return out
        total = reduce_owned(extended, group[frames:])
        for k in range(1, inner):
            part = total[:, :, (k - 1) * frames : k * frames]
            column_sums.append(part[:, frames : frames + 1])
            out = place(out, part[:, :frames] * scale / column_sums[k], z, y - k)
        return out

    def remote_group(s, out):
        left = jnp.concatenate([remote[s], jnp.zeros((8, pixels), jnp.bfloat16)], axis=0)
        total = reduce_owned(left, group, sums=remote[s])
        left_sums = jnp.transpose(total[:, frames : frames + 1, :frames], (0, 2, 1))
        value = total[:, :frames] * (size / left_sums) / jnp.concatenate(column_sums, axis=2)
        if 2 * s != outer:
            back = shift_z(results.encode(value), -s)
            back = results.decode(back)
            for k in range(inner):
                out = place(out, back[:, :, k * frames : (k + 1) * frames], z + s, y - k)
        for k in range(inner):
            block = jnp.transpose(value[:, :, k * frames : (k + 1) * frames], (0, 2, 1))
            if k > 0:
                block = results.decode(shift_y(results.encode(block), -k))
            out = place(out, block, z - s, y + k)
        return out

    out = beside_group(out)
    for s in range(1, half + 1):
        out = remote_group(s, out)
    return out


MESH = pl.DeviceIdType.MESH
TILE = 16
CHUNKS = 2


def fits_kernel(shape):
    inner = inner_extent(shape["tm"])
    return shape["tm"] // inner == 4 and inner == 2 and shape["pix"] == 4


def exchange(owned, partials, results, *refs):
    (counts, dead_time, flat_field, cycle_map,
     diagonal, pair, local, side_in, back_in, diag_rows, pair_rows, local_rows, local_turned,
     wide, right, ring, swap_out, swap_in, x_out, x_in, here, side_out, back_out,
     diag_out, diag_in, diag_x_out, diag_x_in, diag_here,
     pair_out, pair_in, pair_x_out, pair_x_in, pair_here,
     sums_out, sums_core, sums_chip, sums_x, scale_own, scale_side, scale_first, scale_second,
     columns, pair_columns, lanes,
     core_send, core_recv, x_send, x_recv, up_send, up_recv, back_send, back_recv,
     side_send, side_recv, diag_send, diag_recv, pair_send, pair_recv, sum_send, sum_recv, keep_sem,
     y_send, y_recv, diag_core_send, diag_core_recv, pair_core_send, pair_core_recv) = refs
    frames, pixels = counts.shape
    step, last = frames // CHUNKS, 2 * CHUNKS - 1
    at_tm, at_pix = lax.axis_index("tm"), lax.axis_index("pix")
    z, y = at_tm // 2, at_tm % 2
    x, core = at_pix // 2, at_pix % 2
    to_y = {"tm": z * 2 + 1 - y}
    to_up = {"tm": (z + 1) % 4 * 2 + y}
    to_down = {"tm": (z + 3) % 4 * 2 + y}
    to_core = {"pix": x * 2 + 1 - core}
    to_x = {"pix": (1 - x) * 2 + core}
    own, beside, every = pl.ds(0, frames), pl.ds(frames, frames), pl.ds(0, 2 * frames)

    barrier = pltpu.get_barrier_semaphore()
    for target in (to_y, to_up, to_down, to_core, to_x):
        pl.semaphore_signal(barrier, inc=1, device_id=target, device_id_type=MESH)

    def correct(i, carry):
        rows = pl.ds(pl.multiple_of(i * TILE, TILE), TILE)
        raw = counts[rows, :]
        value = raw / (1.0 - dead_time[...] * raw) * flat_field[...]
        right[rows, :] = value.astype(jnp.bfloat16)
        return carry

    lax.fori_loop(0, frames // TILE, correct, 0)
    pl.semaphore_wait(barrier, 5)

    def remote(source, target, send, recv, device):
        return pltpu.make_async_remote_copy(
            src_ref=source, dst_ref=target, send_sem=send, recv_sem=recv,
            device_id=device, device_id_type=MESH,
        )

    copies = []

    def start(*args):
        copy = remote(*args)
        copy.start()
        copies.append(copy)
        return copy

    def chunk(n):
        return pl.ds(pl.multiple_of(n * step, step), step)

    deep = pixels // 2

    def depth(h):
        return pl.ds(h * deep, deep)

    by_side = [
        start(right.at[own, depth(h)], right.at[beside, depth(h)], y_send.at[h], y_recv.at[h], to_y)
        for h in range(2)
    ]

    def to_ring(n):
        return remote(right.at[chunk(n)], ring.at[chunk(n)], up_send.at[n], up_recv.at[n], to_up)

    def forward(n):
        return remote(ring.at[chunk(n)], ring.at[chunk(n + CHUNKS)],
                      up_send.at[n + CHUNKS], up_recv.at[n + CHUNKS], to_up)

    copies += [to_ring(n) for n in range(CHUNKS)] + [forward(n) for n in range(CHUNKS)]
    to_ring(0).start()

    ids = lax.broadcasted_iota(jnp.int32, (CYCLES, pixels), 0)
    onehot = jnp.where(jnp.broadcast_to(cycle_map[...], (CYCLES, pixels)) == ids, 1.0, 0.0)
    counted = lax.dot_general(
        onehot.astype(jnp.bfloat16), right[own, :], (((1,), (1,)), ((), ())),
        preferred_element_type=jnp.float32,
    )
    size = jnp.sum(onehot, axis=1, keepdims=True)
    sums_out[:, own] = counted
    sums_out[:, beside] = jnp.broadcast_to(size, counted.shape)
    by_core = start(sums_out, sums_core, sum_send.at[0], sum_recv.at[0], to_core)

    def fill(r, carry):
        hit = jnp.broadcast_to(cycle_map[...], (TILE, pixels)) == r
        wide[r] = jnp.where(hit, 1.0, 0.0).astype(jnp.bfloat16)
        return carry

    lax.fori_loop(0, CYCLES // 2, fill, 0)
    by_core.wait_recv()
    sums_chip[...] = sums_out[...] + sums_core[...]
    by_x = start(sums_chip, sums_x, sum_send.at[1], sum_recv.at[1], to_x)
    lax.fori_loop(CYCLES // 2, CYCLES, fill, 0)
    by_x.wait_recv()
    mine = pl.ds(pl.multiple_of(at_pix * owned, owned), owned)
    scale_own[...] = sums_chip[mine, :] + sums_x[mine, :]
    by_y = start(scale_own, scale_side, sum_send.at[2], sum_recv.at[2], to_y)
    by_up = start(scale_own, scale_first, sum_send.at[3], sum_recv.at[3], to_up)
    for n in range(1, CHUNKS):
        to_ring(n).start()

    def product(left, rows, count, cols, made, j, ks, add):
        base = (lax.rem(x + 1 + j, 2) * 2 + lax.rem(core + 1 + j // 2, 2)) * owned
        block = left[rows, ks].reshape(count // TILE, TILE, ks.size)
        masked = jnp.concatenate(
            [(block * wide[base + i, :, ks][None]).reshape(count, ks.size) for i in range(owned)],
            axis=0,
        )
        value = lax.dot_general(
            masked, right[cols, ks], (((1,), (1,)), ((), ())), preferred_element_type=jnp.float32
        ).reshape(owned, count, cols.size)
        made[j] = made[j] + value if add else value

    def early(left, rows, count, cols, made):
        def body(j, carry):
            product(left, rows, count, cols, made, j, depth(0), False)
            return carry

        lax.fori_loop(0, 4, body, 0)

    def reduce_unit(left, rows, count, cols, made, others, inn, code_out, across, kept, late=False):
        ks = depth(1) if late else pl.ds(0, pixels)

        def body(j, carry):
            product(left, rows, count, cols, made, j, ks, late)

            @pl.when(j == 0)
            def _():
                others[0].start()

            @pl.when(j == 1)
            def _():
                others[1].start()

            @pl.when(j == 2)
            def _():
                others[0].wait_recv()
                code_out[...] = partials.encode(made[2] + inn[0])
                across.start()

            return carry

        lax.fori_loop(0, 4, body, 0)
        others[1].wait_recv()
        kept[...] = made[3] + inn[1]

    half = frames // 2

    def keep(source, target, n):
        return pltpu.make_async_copy(source, target, keep_sem.at[n])

    def diag_core(n):
        return [
            remote(diag_out.at[n, g], diag_in.at[n, g],
                   diag_core_send.at[n, g], diag_core_recv.at[n, g], to_core)
            for g in range(2)
        ]

    def diag_across(n):
        return remote(diag_x_out.at[n], diag_x_in.at[n],
                      diag_send.at[n], diag_recv.at[n], to_x)

    def diag_unit(n, carry):
        rows = pl.ds(pl.multiple_of(n * half, half), half)
        reduce_unit(right, rows, half, own, diag_out.at[n], diag_core(n), diag_in.at[n],
                    diag_x_out.at[n], diag_across(n), diag_here.at[n])
        return carry

    lax.fori_loop(0, 2, diag_unit, 0)
    copies += [*diag_core(0), *diag_core(1), diag_across(0), diag_across(1)]

    def pass_on(n):
        remote(ring.at[chunk(n)], ring.at[chunk(n)], up_send.at[n], up_recv.at[n], to_up).wait_recv()
        forward(n).start()

    by_up.wait_recv()
    by_up2 = start(scale_first, scale_second, sum_send.at[4], sum_recv.at[4], to_up)
    for n in range(CHUNKS - 1):
        pass_on(n)
    half_rows = pl.ds(pl.multiple_of(y * half, half), half)
    pair_block = (right, pl.ds(pl.multiple_of(y * (frames + half), half), half), half,
                  pl.ds(pl.multiple_of((1 - y) * frames, frames), frames), pair_out)

    def unit_block(n):
        return ring, chunk(n), step, every, swap_out.at[n]

    by_side[0].wait_recv()
    early(*pair_block)
    early(*unit_block(0))
    size = scale_own[:, beside]
    own_sums = scale_own[:, own]
    own_columns = jnp.transpose(size / own_sums, (1, 0))
    columns[own, :] = jnp.transpose(size / scale_first[:, own], (1, 0))
    for n in range(2):
        rows = pl.ds(n * half, half)
        diag_across(n).wait_recv()
        for r in range(owned):
            value = diag_here[n, r] + partials.decode(diag_x_in[n, r])
            value = value * own_columns[n * half : (n + 1) * half, r : r + 1]
            diag_rows[r, rows, :] = value * (1.0 / own_sums[r : r + 1])
    keep(diag_rows, diagonal, 0).start()

    pair_across = remote(pair_x_out, pair_x_in, pair_send.at[1], pair_recv.at[1], to_x)
    pair_core = [
        remote(pair_out.at[g], pair_in.at[g], pair_core_send.at[g], pair_core_recv.at[g], to_core)
        for g in range(2)
    ]
    by_side[1].wait_recv()
    pass_on(CHUNKS - 1)
    reduce_unit(*pair_block, pair_core, pair_in, pair_x_out, pair_across, pair_here, late=True)
    copies += [*pair_core, pair_across]

    by_y.wait_recv()
    side_sums = scale_side[:, own]
    lower = y == 0
    pair_columns[...] = jnp.transpose(size / jnp.where(lower, own_sums, side_sums), (1, 0))
    pair_lanes = 1.0 / jnp.where(lower, side_sums, own_sums)
    lanes[...] = 1.0 / jnp.concatenate([own_sums, side_sums], axis=1)

    def to_other(n):
        return [
            remote(swap_out.at[n, g], swap_in.at[n, g],
                   core_send.at[n, g], core_recv.at[n, g], to_core)
            for g in range(2)
        ]

    def to_across(n):
        return remote(x_out.at[n], x_in.at[n], x_send.at[n], x_recv.at[n], to_x)

    def to_side(n):
        return remote(side_out.at[n], side_in.at[:, chunk(n)], side_send.at[n], side_recv.at[n], to_y)

    def to_back(n):
        return remote(back_out.at[n], back_in.at[:, chunk(n)], back_send.at[n], back_recv.at[n], to_down)

    by_pair = remote(pair_rows, pair.at[:, half_rows], pair_send.at[0], pair_recv.at[0], to_y)

    def finish(n):
        to_across(n).wait_recv()

        for r in range(owned):
            value = here[n, r] + partials.decode(x_in[n, r])
            value = value * columns[chunk(n), r : r + 1] * lanes[r : r + 1, :]
            back_out[n, r] = results.encode(value)
            side_out[n, r] = results.encode(value[:, frames:])
            local_rows[r, chunk(n), :] = value[:, :frames]

        @pl.when(n < CHUNKS)
        def _():
            to_back(n).start()

        to_side(n).start()

    def turn(s):
        for r in range(owned):
            local_turned[s, r] = jnp.transpose(local_rows[r, pl.ds(s * frames, frames), :], (1, 0))
        keep(local_turned.at[s], local.at[s], 1 + s).start()

    def reduce_block(n, late=False):
        reduce_unit(*unit_block(n), to_other(n), swap_in.at[n],
                    x_out.at[n], to_across(n), here.at[n], late)

    def unit(n, carry):
        @pl.when(n >= CHUNKS)
        def _():
            remote(ring.at[chunk(n)], ring.at[chunk(n)],
                   up_send.at[n], up_recv.at[n], to_up).wait_recv()

        reduce_block(n)

        @pl.when(n == CHUNKS)
        def _():
            by_up2.wait_recv()
            columns[beside, :] = jnp.transpose(size / scale_second[:, own], (1, 0))

        finish(n - 1)

        @pl.when(n == CHUNKS)
        def _():
            turn(0)

        return carry

    reduce_block(0, late=True)
    pair_across.wait_recv()
    for r in range(owned):
        value = pair_here[r] + partials.decode(pair_x_in[r])
        value = value * pair_columns[half_rows, r : r + 1] * pair_lanes[r : r + 1]
        pair_rows[r] = results.encode(value)
    by_pair.start()
    keep(pair_rows, pair.at[:, half_rows], 3).start()
    lax.fori_loop(1, 2 * CHUNKS, unit, 0)
    finish(jnp.int32(last))
    turn(1)
    by_pair.wait_recv()
    copies.append(by_pair)
    for n in range(2 * CHUNKS):
        copies += [*to_other(n), to_across(n), to_side(n)]
        to_side(n).wait_recv()
    for n in range(CHUNKS):
        copies.append(to_back(n))
        to_back(n).wait_recv()
    keep(diag_rows, diagonal, 0).wait()
    for s in range(2):
        keep(local_turned.at[s], local.at[s], 1 + s).wait()
    keep(pair_rows, pair.at[:, half_rows], 3).wait()
    for copy in copies:
        copy.wait_send()


def assemble(results, diagonal, pair, local, side, back, out):
    frames = diagonal.shape[1]
    at_tm = lax.axis_index("tm")
    z, y = at_tm // 2, at_tm % 2

    def turn(value):
        return jnp.transpose(value, (1, 0))

    for r in range(diagonal.shape[0]):

        def put(dz, dy, value):
            block = (z + dz + 4) % 4 * 2 + (y + dy) % 2
            out[r, :, pl.ds(pl.multiple_of(block * frames, frames), frames)] = value

        put(0, 0, diagonal[r])
        value = results.decode(pair[r])
        put(0, 1, jnp.where(y == 0, value, turn(value)))
        for s in range(2):
            put(-1 - s, 0, local[s, r])
            put(-1 - s, 1, turn(results.decode(side[r, pl.ds(s * frames, frames), :])))
        value = results.decode(back[r])
        put(1, 0, value[:, :frames])
        put(1, 1, value[:, frames:])


def per_device_kernel(counts, dead_time, flat_field, cycle_map):
    frames, pixels = counts.shape
    tm, pix = lax.axis_size("tm"), lax.axis_size("pix")
    owned = CYCLES // pix
    partials = LogCode(0.0218, 6800.0 * pixels * 2, True)
    results = LogCode(1 / 140.0, 140.0, False)
    f32, bf16, i16 = jnp.float32, jnp.bfloat16, jnp.int16
    vmem, dma = pltpu.VMEM, pltpu.SemaphoreType.DMA
    both, half, step, units = 2 * frames, frames // 2, frames // CHUNKS, 2 * CHUNKS
    small = (owned, both)
    scratch = [
        vmem((owned, frames, frames), f32),
        vmem((owned, half, frames), i16),
        vmem((owned, both, frames), f32),
        vmem((2, owned, frames, frames), f32),
        vmem((CYCLES, TILE, pixels), bf16),
        vmem((both, pixels), bf16),
        vmem((both, pixels), bf16),
        vmem((units, 4, owned, step, both), f32),
        vmem((units, 2, owned, step, both), f32),
        *[vmem((units, owned, step, both), i16)] * 2,
        vmem((units, owned, step, both), f32),
        vmem((units, owned, step, frames), i16),
        vmem((units, owned, step, both), i16),
        vmem((2, 4, owned, half, frames), f32),
        vmem((2, 2, owned, half, frames), f32),
        *[vmem((2, owned, half, frames), i16)] * 2,
        vmem((2, owned, half, frames), f32),
        vmem((4, owned, half, frames), f32),
        vmem((2, owned, half, frames), f32),
        *[vmem((owned, half, frames), i16)] * 2,
        vmem((owned, half, frames), f32),
        *[vmem((CYCLES, both), f32)] * 4,
        *[vmem(small, f32)] * 4,
        vmem((both, owned), f32),
        vmem((frames, owned), f32),
        vmem(small, f32),
        dma((units, 2)), dma((units, 2)), dma((units,)), dma((units,)),
        dma((units,)), dma((units,)), dma((CHUNKS,)), dma((CHUNKS,)),
        dma((units,)), dma((units,)), dma((2,)), dma((2,)), dma((2,)), dma((2,)),
        dma((5,)), dma((5,)), dma((4,)), dma((2,)), dma((2,)), dma((2, 2)), dma((2, 2)), dma((2,)), dma((2,)),
    ]
    shapes = [
        ((owned, frames, frames), f32), ((owned, frames, frames), i16),
        ((2, owned, frames, frames), f32), ((owned, both, frames), i16), ((owned, frames, both), i16),
    ]
    pieces = pl.pallas_call(
        functools.partial(exchange, owned, partials, results),
        out_shape=[jax.ShapeDtypeStruct(*shape) for shape in shapes],
        in_specs=[pl.BlockSpec(memory_space=pltpu.VMEM)] * 4,
        out_specs=[pl.BlockSpec(memory_space=pl.ANY)] * 5,
        scratch_shapes=scratch,
        compiler_params=pltpu.CompilerParams(
            collective_id=0, has_side_effects=True, vmem_limit_bytes=60 << 20
        ),
    )(counts, dead_time[None, :], flat_field[None, :], cycle_map[None, :])
    group = owned // 2
    return pl.pallas_call(
        functools.partial(assemble, results),
        grid=(owned // group,),
        out_shape=jax.ShapeDtypeStruct((owned, frames, tm * frames), f32),
        in_specs=[
            pl.BlockSpec((group, *shape[1:]), lambda r: (r, 0, 0))
            if len(shape) == 3
            else pl.BlockSpec((shape[0], group, *shape[2:]), lambda r: (0, r, 0, 0))
            for shape, _ in shapes
        ],
        out_specs=pl.BlockSpec((group, frames, tm * frames), lambda r: (r, 0, 0)),
    )(*pieces)


def solution(mesh):
    kernel_path = fits_kernel(mesh.shape)
    device_program = per_device_kernel if kernel_path else per_device
    placed = (P("tm", "pix"), P("pix"), P("pix"), P("pix"))

    return jax.shard_map(
        device_program, mesh=mesh, in_specs=placed, out_specs=P("pix", "tm", None), check_vma=False
    )
```

```python
import functools
import math

import jax
import jax.numpy as jnp
from jax import lax
from jax.experimental import pallas as pl
from jax.experimental.pallas import tpu as pltpu
from jax.sharding import PartitionSpec as P

CYCLES = 32


def inner_extent(count):
    return max(d for d in range(1, count + 1) if count % d == 0 and d * d <= count)


class LogCode:
    def __init__(self, low, high, zero):
        self.low, self.zero = low, zero
        low, high = math.log2(low), math.log2(high)
        self.centre, self.steps = (high + low) / 2, 65400 / (high - low)

    def encode(self, value):
        level = (jnp.log2(jnp.maximum(value, self.low)) - self.centre) * self.steps
        return jnp.round(level).astype(jnp.int16)

    def decode(self, code):
        level = code.astype(jnp.float32)
        value = jnp.exp2(level * (1.0 / self.steps) + self.centre)
        return jnp.where(level > -32700 + 32, value, 0.0) if self.zero else value


def per_device(counts, dead_time, flat_field, cycle_map):
    intensity = (counts / (1.0 - dead_time[None, :] * counts) * flat_field[None, :]).astype(
        jnp.bfloat16
    )
    frames, pixels = intensity.shape
    tm, pix = lax.axis_size("tm"), lax.axis_size("pix")
    inner = inner_extent(tm)
    outer = tm // inner
    cores = 2 if pix % 2 == 0 else 1
    across = pix // cores
    owned = CYCLES // pix
    at_tm, at_pix = lax.axis_index("tm"), lax.axis_index("pix")
    z, y = at_tm // inner, at_tm % inner
    x, core = at_pix // cores, at_pix % cores

    def shift_z(value, k=1):
        return lax.ppermute(
            value, "tm", [(i, (i // inner + k) % outer * inner + i % inner) for i in range(tm)]
        )

    def shift_y(value, k):
        return lax.ppermute(
            value, "tm", [(i, i // inner * inner + (i % inner + k) % inner) for i in range(tm)]
        )

    def shift_x(value, k):
        return lax.ppermute(
            value, "pix", [(i, (i // cores + k) % across * cores + i % cores) for i in range(pix)]
        )

    def swap_core(value):
        return lax.ppermute(
            value, "pix", [(i, i // cores * cores + (i % cores + 1) % cores) for i in range(pix)]
        )

    half = outer // 2
    remote = {0: intensity}
    for s in range(1, half + 1):
        remote[s] = shift_z(remote[s - 1])
    beside = [intensity]
    for k in range(1, inner):
        beside.append(shift_y(intensity, k))

    def onehot_of(owner_core, ks):
        ids = jnp.concatenate(
            [
                ((x + k) % across * cores + owner_core) * owned
                + jnp.arange(owned, dtype=jnp.int32)
                for k in ks
            ]
        )
        return (cycle_map[None, :] == ids[:, None]).astype(jnp.bfloat16)

    other = (core + 1) % cores
    away_ks, own_ks = range(1, across), range(1)
    rows = frames + 8

    def gram(onehot, left, right, sums):
        masked = (onehot[:, None, :] * left[None, :, :]).reshape(-1, pixels)
        value = lax.dot_general(
            masked, right, (((1,), (1,)), ((), ())), preferred_element_type=jnp.float32
        ).reshape(onehot.shape[0], rows, right.shape[0])
        if sums is not None:
            own = lax.dot_general(
                onehot, sums, (((1,), (1,)), ((), ())), preferred_element_type=jnp.float32
            )
            value = value + jnp.pad(
                own[:, None, :], ((0, 0), (frames, 7), (0, right.shape[0] - frames))
            )
        return value

    partials = LogCode(0.0218, 6800.0 * pixels * cores, True)
    results = LogCode(1 / 140.0, 140.0, False)

    def reduce_owned(left, right, sums=None, exact=False):
        def part(owner_core, ks):
            return gram(onehot_of(owner_core, ks), left, right, sums)

        theirs = {}
        for name, ks in (("o", away_ks), ("x", own_ks)):
            if cores > 1 and len(ks):
                theirs[name] = swap_core(part(other, ks))
        total = None
        if across > 1:
            sent = part(core, away_ks)
            if cores > 1:
                sent = sent + theirs["o"]
            got = []
            for k in range(1, across):
                value = sent[(k - 1) * owned : k * owned]
                if not exact:
                    value = partials.encode(value)
                value = shift_x(value, k)
                got.append(value if exact else partials.decode(value))
            total = sum(got[1:], got[0])
        here = part(core, own_ks)
        if cores > 1:
            here = here + theirs["x"]
        here = lax.optimization_barrier(here)
        return here if total is None else here + total

    out = jnp.zeros((owned, frames, tm * frames), jnp.float32)

    def place(out, value, zs, ys):
        at = (zs % outer * inner + ys % inner) * frames
        return lax.dynamic_update_slice_in_dim(out, value, at, 2)

    ones = jnp.ones((8, pixels), jnp.bfloat16)
    extended = jnp.concatenate([intensity, ones], axis=0)
    total = reduce_owned(extended, extended, exact=True)
    row_sums = total[:, :frames, frames]
    scale = total[:, frames, frames][:, None, None] / row_sums[:, :, None]
    column_sums = [total[:, frames : frames + 1, :frames]]
    size = total[:, frames : frames + 1, frames : frames + 1]
    out = place(out, total[:, :frames, :frames] * scale / column_sums[0], z, y)
    group = jnp.concatenate(beside, axis=0)

    def beside_group(out):
        if inner == 1:
            return out
        total = reduce_owned(extended, group[frames:])
        for k in range(1, inner):
            part = total[:, :, (k - 1) * frames : k * frames]
            column_sums.append(part[:, frames : frames + 1])
            out = place(out, part[:, :frames] * scale / column_sums[k], z, y - k)
        return out

    def remote_group(s, out):
        left = jnp.concatenate([remote[s], jnp.zeros((8, pixels), jnp.bfloat16)], axis=0)
        total = reduce_owned(left, group, sums=remote[s])
        left_sums = jnp.transpose(total[:, frames : frames + 1, :frames], (0, 2, 1))
        value = total[:, :frames] * (size / left_sums) / jnp.concatenate(column_sums, axis=2)
        if 2 * s != outer:
            back = shift_z(results.encode(value), -s)
            back = results.decode(back)
            for k in range(inner):
                out = place(out, back[:, :, k * frames : (k + 1) * frames], z + s, y - k)
        for k in range(inner):
            block = jnp.transpose(value[:, :, k * frames : (k + 1) * frames], (0, 2, 1))
            if k > 0:
                block = results.decode(shift_y(results.encode(block), -k))
            out = place(out, block, z - s, y + k)
        return out

    out = beside_group(out)
    for s in range(1, half + 1):
        out = remote_group(s, out)
    return out


MESH = pl.DeviceIdType.MESH
TILE = 16
CHUNKS = 2
PIECES = 4


def fits_kernel(shape):
    inner = inner_extent(shape["tm"])
    return shape["tm"] // inner == 4 and inner == 2 and shape["pix"] == 4


def exchange(owned, partials, results, *refs):
    (counts, dead_time, flat_field, cycle_map,
     diagonal, pair, local, side_in, back_in, diag_rows, pair_rows, local_rows, local_turned,
     wide, right, ring, swap_out, swap_in, x_out, x_in, here, side_out, back_out,
     diag_out, diag_in, diag_x_out, diag_x_in, diag_here,
     pair_out, pair_in, pair_x_out, pair_x_in, pair_here,
     sums_out, sums_core, sums_chip, sums_x, scale_own, scale_side, scale_first, scale_second,
     columns, pair_columns, lanes,
     core_send, core_recv, x_send, x_recv, up_send, up_recv, back_send, back_recv,
     side_send, side_recv, diag_send, diag_recv, pair_send, pair_recv, sum_send, sum_recv, keep_sem,
     y_send, y_recv, diag_core_send, diag_core_recv, pair_core_send, pair_core_recv,
     fine_swap_out, fine_swap_in, fine_x_out, fine_x_in, fine_here, fine_side_out,
     fine_core_send, fine_core_recv, fine_x_send, fine_x_recv, fine_side_send, fine_side_recv,
     raw_counts, load_sem) = refs
    frames, pixels = counts.shape
    step, fine = frames // CHUNKS, frames // PIECES
    at_tm, at_pix = lax.axis_index("tm"), lax.axis_index("pix")
    z, y = at_tm // 2, at_tm % 2
    x, core = at_pix // 2, at_pix % 2
    to_y = {"tm": z * 2 + 1 - y}
    to_up = {"tm": (z + 1) % 4 * 2 + y}
    to_down = {"tm": (z + 3) % 4 * 2 + y}
    to_core = {"pix": x * 2 + 1 - core}
    to_x = {"pix": (1 - x) * 2 + core}
    own, beside, every = pl.ds(0, frames), pl.ds(frames, frames), pl.ds(0, 2 * frames)

    barrier = pltpu.get_barrier_semaphore()
    for target in (to_y, to_up, to_down, to_core, to_x):
        pl.semaphore_signal(barrier, inc=1, device_id=target, device_id_type=MESH)

    loads = [
        pltpu.make_async_copy(counts.at[rows], raw_counts.at[rows], load_sem.at[q])
        for q, rows in enumerate(pl.ds(q * fine, fine) for q in range(PIECES))
    ]
    for load in loads:
        load.start()

    def correct(i, carry):
        rows = pl.ds(pl.multiple_of(i * TILE, TILE), TILE)
        raw = raw_counts[rows, :]
        value = raw / (1.0 - dead_time[...] * raw) * flat_field[...]
        right[rows, :] = value.astype(jnp.bfloat16)
        return carry

    def correct_piece(q):
        loads[q].wait()
        lax.fori_loop(q * fine // TILE, (q + 1) * fine // TILE, correct, 0)

    def remote(source, target, send, recv, device):
        return pltpu.make_async_remote_copy(
            src_ref=source, dst_ref=target, send_sem=send, recv_sem=recv,
            device_id=device, device_id_type=MESH,
        )

    copies = []

    def start(*args):
        copy = remote(*args)
        copy.start()
        copies.append(copy)
        return copy

    def chunk(n):
        return pl.ds(pl.multiple_of(n * step, step), step)

    for q in range(PIECES // CHUNKS):
        correct_piece(q)
    pl.semaphore_wait(barrier, 5)

    def to_ring(n):
        return remote(right.at[chunk(n)], ring.at[chunk(n)], up_send.at[n], up_recv.at[n], to_up)

    to_rings = [to_ring(n) for n in range(CHUNKS)]
    to_rings[0].start()
    for q in range(PIECES // CHUNKS, PIECES):
        correct_piece(q)
    deep = pixels // 2

    def depth(h):
        return pl.ds(h * deep, deep)

    by_side = [
        start(right.at[own, depth(h)], right.at[beside, depth(h)], y_send.at[h], y_recv.at[h], to_y)
        for h in range(2)
    ]

    def piece(m, offset=0):
        return pl.ds(pl.multiple_of(offset + m * fine, fine), fine)

    def forward(m):
        return remote(ring.at[piece(m)], ring.at[piece(m, frames)],
                      up_send.at[m + CHUNKS], up_recv.at[m + CHUNKS], to_up)

    landed = [forward(m) for m in range(PIECES)]
    copies += to_rings + landed

    ids = lax.broadcasted_iota(jnp.int32, (CYCLES, pixels), 0)
    onehot = jnp.where(jnp.broadcast_to(cycle_map[...], (CYCLES, pixels)) == ids, 1.0, 0.0)
    counted = lax.dot_general(
        onehot.astype(jnp.bfloat16), right[own, :], (((1,), (1,)), ((), ())),
        preferred_element_type=jnp.float32,
    )
    size = jnp.sum(onehot, axis=1, keepdims=True)
    sums_out[:, own] = counted
    sums_out[:, beside] = jnp.broadcast_to(size, counted.shape)
    by_core = start(sums_out, sums_core, sum_send.at[0], sum_recv.at[0], to_core)

    def fill(r, carry):
        hit = jnp.broadcast_to(cycle_map[...], (TILE, pixels)) == r
        wide[r] = jnp.where(hit, 1.0, 0.0).astype(jnp.bfloat16)
        return carry

    lax.fori_loop(0, CYCLES // 2, fill, 0)
    by_core.wait_recv()
    sums_chip[...] = sums_out[...] + sums_core[...]
    by_x = start(sums_chip, sums_x, sum_send.at[1], sum_recv.at[1], to_x)
    lax.fori_loop(CYCLES // 2, CYCLES, fill, 0)
    by_x.wait_recv()
    mine = pl.ds(pl.multiple_of(at_pix * owned, owned), owned)
    scale_own[...] = sums_chip[mine, :] + sums_x[mine, :]
    by_y = start(scale_own, scale_side, sum_send.at[2], sum_recv.at[2], to_y)
    by_up = start(scale_own, scale_first, sum_send.at[3], sum_recv.at[3], to_up)
    for n in range(1, CHUNKS):
        to_rings[n].start()

    def product(left, rows, count, cols, made, j, ks, add):
        base = (lax.rem(x + 1 + j, 2) * 2 + lax.rem(core + 1 + j // 2, 2)) * owned
        block = left[rows, ks].reshape(count // TILE, TILE, ks.size)
        masked = jnp.concatenate(
            [(block * wide[base + i, :, ks][None]).reshape(count, ks.size) for i in range(owned)],
            axis=0,
        )
        value = lax.dot_general(
            masked, right[cols, ks], (((1,), (1,)), ((), ())), preferred_element_type=jnp.float32
        ).reshape(owned, count, cols.size)
        made[j] = made[j] + value if add else value

    def early(left, rows, count, cols, made):
        def body(j, carry):
            product(left, rows, count, cols, made, j, depth(0), False)
            return carry

        lax.fori_loop(0, 4, body, 0)

    def send_across(unit):
        unit["others"][0].wait_recv()
        unit["code_out"][...] = partials.encode(unit["block"][4][2] + unit["inn"][0])
        unit["across"].start()

    def settle(unit):
        unit["others"][1].wait_recv()
        unit["here"][...] = unit["block"][4][3] + unit["inn"][1]

    def reduce_unit(unit, before=None, late=False):
        ks = depth(1) if late else pl.ds(0, pixels)

        def body(j, carry):
            product(*unit["block"], j, ks, late)

            @pl.when(j == 0)
            def _():
                unit["others"][0].start()
                if before is not None:
                    send_across(before)

            @pl.when(j == 1)
            def _():
                unit["others"][1].start()
                if before is not None:
                    settle(before)

            return carry

        lax.fori_loop(0, 4, body, 0)

    half = frames // 2

    def keep(source, target, n):
        return pltpu.make_async_copy(source, target, keep_sem.at[n])

    def diag_core(n):
        return [
            remote(diag_out.at[n, g], diag_in.at[n, g],
                   diag_core_send.at[n, g], diag_core_recv.at[n, g], to_core)
            for g in range(2)
        ]

    def diag_across(n):
        return remote(diag_x_out.at[n], diag_x_in.at[n],
                      diag_send.at[n], diag_recv.at[n], to_x)

    def diag_unit(n):
        return dict(
            block=(right, pl.ds(n * half, half), half, own, diag_out.at[n]), inn=diag_in.at[n],
            others=diag_core(n), code_out=diag_x_out.at[n], across=diag_across(n), here=diag_here.at[n],
        )

    diags = [diag_unit(0), diag_unit(1)]
    reduce_unit(diags[0])
    reduce_unit(diags[1], diags[0])
    for unit in diags:
        copies += [*unit["others"], unit["across"]]

    def pass_on(n):
        remote(ring.at[chunk(n)], ring.at[chunk(n)], up_send.at[n], up_recv.at[n], to_up).wait_recv()
        for m in range(n * PIECES // CHUNKS, (n + 1) * PIECES // CHUNKS):
            landed[m].start()

    by_up.wait_recv()
    by_up2 = start(scale_first, scale_second, sum_send.at[4], sum_recv.at[4], to_up)
    for n in range(CHUNKS - 1):
        pass_on(n)
    half_rows = pl.ds(pl.multiple_of(y * half, half), half)
    pair_block = (right, pl.ds(pl.multiple_of(y * (frames + half), half), half), half,
                  pl.ds(pl.multiple_of((1 - y) * frames, frames), frames), pair_out)

    by_side[0].wait_recv()
    early(*pair_block)
    send_across(diags[1])
    settle(diags[1])
    early(ring, chunk(0), step, every, swap_out.at[0])
    size = scale_own[:, beside]
    own_sums = scale_own[:, own]
    own_columns = jnp.transpose(size / own_sums, (1, 0))
    columns[own, :] = jnp.transpose(size / scale_first[:, own], (1, 0))
    for n in range(2):
        rows = pl.ds(n * half, half)
        diags[n]["across"].wait_recv()
        for r in range(owned):
            value = diag_here[n, r] + partials.decode(diag_x_in[n, r])
            value = value * own_columns[n * half : (n + 1) * half, r : r + 1]
            diag_rows[r, rows, :] = value * (1.0 / own_sums[r : r + 1])
    keep(diag_rows, diagonal, 0).start()

    pair_across = remote(pair_x_out, pair_x_in, pair_send.at[1], pair_recv.at[1], to_x)
    pair_core = [
        remote(pair_out.at[g], pair_in.at[g], pair_core_send.at[g], pair_core_recv.at[g], to_core)
        for g in range(2)
    ]
    by_side[1].wait_recv()
    pass_on(CHUNKS - 1)
    pair_unit = dict(block=pair_block, others=pair_core, inn=pair_in, code_out=pair_x_out,
                     across=pair_across, here=pair_here)
    reduce_unit(pair_unit, late=True)
    copies += [*pair_core, pair_across]

    by_y.wait_recv()
    side_sums = scale_side[:, own]
    lower = y == 0
    pair_columns[...] = jnp.transpose(size / jnp.where(lower, own_sums, side_sums), (1, 0))
    pair_lanes = 1.0 / jnp.where(lower, side_sums, own_sums)
    lanes[...] = 1.0 / jnp.concatenate([own_sums, side_sums], axis=1)

    def coarse(n):
        rows = chunk(n)
        return dict(
            block=(ring, rows, step, every, swap_out.at[n]), rows=rows, inn=swap_in.at[n],
            others=[remote(swap_out.at[n, g], swap_in.at[n, g],
                           core_send.at[n, g], core_recv.at[n, g], to_core) for g in range(2)],
            code_out=x_out.at[n], code_in=x_in.at[n],
            across=remote(x_out.at[n], x_in.at[n], x_send.at[n], x_recv.at[n], to_x),
            here=here.at[n], side=side_out.at[n], back=back_out.at[n],
            to_side=remote(side_out.at[n], side_in.at[:, rows], side_send.at[n], side_recv.at[n], to_y),
            to_back=remote(back_out.at[n], back_in.at[:, rows], back_send.at[n], back_recv.at[n], to_down),
        )

    def fine_unit(m):
        rows = piece(m, frames)
        return dict(
            block=(ring, rows, fine, every, fine_swap_out.at[m]), rows=rows, inn=fine_swap_in.at[m],
            others=[remote(fine_swap_out.at[m, g], fine_swap_in.at[m, g],
                           fine_core_send.at[m, g], fine_core_recv.at[m, g], to_core)
                    for g in range(2)],
            code_out=fine_x_out.at[m], code_in=fine_x_in.at[m],
            across=remote(fine_x_out.at[m], fine_x_in.at[m], fine_x_send.at[m], fine_x_recv.at[m], to_x),
            here=fine_here.at[m], side=fine_side_out.at[m], back=None,
            to_side=remote(fine_side_out.at[m], side_in.at[:, rows],
                           fine_side_send.at[m], fine_side_recv.at[m], to_y),
        )

    by_pair = remote(pair_rows, pair.at[:, half_rows], pair_send.at[0], pair_recv.at[0], to_y)

    def finish(unit):
        unit["across"].wait_recv()
        rows, back = unit["rows"], unit["back"]
        for r in range(owned):
            value = unit["here"][r] + partials.decode(unit["code_in"][r])
            value = value * columns[rows, r : r + 1] * lanes[r : r + 1, :]
            if back is not None:
                back[r] = results.encode(value)
            unit["side"][r] = results.encode(value[:, frames:])
            local_rows[r, rows, :] = value[:, :frames]
        if back is not None:
            unit["to_back"].start()
        unit["to_side"].start()

    def turn(s):
        for r in range(owned):
            local_turned[s, r] = jnp.transpose(local_rows[r, pl.ds(s * frames, frames), :], (1, 0))
        keep(local_turned.at[s], local.at[s], 1 + s).start()

    chain = [*map(coarse, range(CHUNKS)), *map(fine_unit, range(PIECES))]
    for k, unit in enumerate(chain):
        if k >= CHUNKS:
            landed[k - CHUNKS].wait_recv()
        reduce_unit(unit, chain[k - 1] if k else pair_unit, late=k == 0)
        if k == len(chain) - 1:
            send_across(unit)
        if k == 1:
            pair_across.wait_recv()
            for r in range(owned):
                value = pair_here[r] + partials.decode(pair_x_in[r])
                value = value * pair_columns[half_rows, r : r + 1] * pair_lanes[r : r + 1]
                pair_rows[r] = results.encode(value)
            by_pair.start()
            keep(pair_rows, pair.at[:, half_rows], 3).start()
        if k >= 2:
            finish(chain[k - 2])
        if k == CHUNKS:
            by_up2.wait_recv()
            columns[beside, :] = jnp.transpose(size / scale_second[:, own], (1, 0))
        if k == CHUNKS + 1:
            turn(0)
    settle(chain[-1])
    finish(chain[-2])
    finish(chain[-1])
    turn(1)
    by_pair.wait_recv()
    copies.append(by_pair)
    for unit in chain:
        landing = [unit["to_side"]] + ([] if unit["back"] is None else [unit["to_back"]])
        for copy in landing:
            copy.wait_recv()
        copies += [*unit["others"], unit["across"], *landing]
    keep(diag_rows, diagonal, 0).wait()
    for s in range(2):
        keep(local_turned.at[s], local.at[s], 1 + s).wait()
    keep(pair_rows, pair.at[:, half_rows], 3).wait()
    for copy in copies:
        copy.wait_send()


def assemble(results, diagonal, pair, local, side, back, out):
    frames = diagonal.shape[1]
    at_tm = lax.axis_index("tm")
    z, y = at_tm // 2, at_tm % 2

    def turn(value):
        return jnp.transpose(value, (1, 0))

    for r in range(diagonal.shape[0]):

        def put(dz, dy, value):
            block = (z + dz + 4) % 4 * 2 + (y + dy) % 2
            out[r, :, pl.ds(pl.multiple_of(block * frames, frames), frames)] = value

        put(0, 0, diagonal[r])
        value = results.decode(pair[r])
        put(0, 1, jnp.where(y == 0, value, turn(value)))
        for s in range(2):
            put(-1 - s, 0, local[s, r])
            put(-1 - s, 1, turn(results.decode(side[r, pl.ds(s * frames, frames), :])))
        value = results.decode(back[r])
        put(1, 0, value[:, :frames])
        put(1, 1, value[:, frames:])


def per_device_kernel(counts, dead_time, flat_field, cycle_map):
    frames, pixels = counts.shape
    if frames % (PIECES * TILE):
        return per_device(counts, dead_time, flat_field, cycle_map)
    tm, pix = lax.axis_size("tm"), lax.axis_size("pix")
    owned = CYCLES // pix
    partials = LogCode(0.0218, 6800.0 * pixels * 2, True)
    results = LogCode(1 / 140.0, 140.0, False)
    f32, bf16, i16 = jnp.float32, jnp.bfloat16, jnp.int16
    vmem, dma = pltpu.VMEM, pltpu.SemaphoreType.DMA
    both, half, step, fine = 2 * frames, frames // 2, frames // CHUNKS, frames // PIECES
    units, pieces, rings = CHUNKS, PIECES, CHUNKS + PIECES
    small = (owned, both)
    scratch = [
        vmem((owned, frames, frames), f32),
        vmem((owned, half, frames), i16),
        vmem((owned, both, frames), f32),
        vmem((2, owned, frames, frames), f32),
        vmem((CYCLES, TILE, pixels), bf16),
        vmem((both, pixels), bf16),
        vmem((both, pixels), bf16),
        vmem((units, 4, owned, step, both), f32),
        vmem((units, 2, owned, step, both), f32),
        *[vmem((units, owned, step, both), i16)] * 2,
        vmem((units, owned, step, both), f32),
        vmem((units, owned, step, frames), i16),
        vmem((units, owned, step, both), i16),
        vmem((2, 4, owned, half, frames), f32),
        vmem((2, 2, owned, half, frames), f32),
        *[vmem((2, owned, half, frames), i16)] * 2,
        vmem((2, owned, half, frames), f32),
        vmem((4, owned, half, frames), f32),
        vmem((2, owned, half, frames), f32),
        *[vmem((owned, half, frames), i16)] * 2,
        vmem((owned, half, frames), f32),
        *[vmem((CYCLES, both), f32)] * 4,
        *[vmem(small, f32)] * 4,
        vmem((both, owned), f32),
        vmem((frames, owned), f32),
        vmem(small, f32),
        dma((units, 2)), dma((units, 2)), dma((units,)), dma((units,)),
        dma((rings,)), dma((rings,)), dma((CHUNKS,)), dma((CHUNKS,)),
        dma((units,)), dma((units,)), dma((2,)), dma((2,)), dma((2,)), dma((2,)),
        dma((5,)), dma((5,)), dma((4,)), dma((2,)), dma((2,)), dma((2, 2)), dma((2, 2)), dma((2,)), dma((2,)),
        vmem((pieces, 4, owned, fine, both), f32),
        vmem((pieces, 2, owned, fine, both), f32),
        *[vmem((pieces, owned, fine, both), i16)] * 2,
        vmem((pieces, owned, fine, both), f32),
        vmem((pieces, owned, fine, frames), i16),
        dma((pieces, 2)), dma((pieces, 2)), dma((pieces,)), dma((pieces,)), dma((pieces,)), dma((pieces,)),
        vmem((frames, pixels), f32), dma((pieces,)),
    ]
    shapes = [
        ((owned, frames, frames), f32), ((owned, frames, frames), i16),
        ((2, owned, frames, frames), f32), ((owned, both, frames), i16), ((owned, frames, both), i16),
    ]
    made = pl.pallas_call(
        functools.partial(exchange, owned, partials, results),
        out_shape=[jax.ShapeDtypeStruct(*shape) for shape in shapes],
        in_specs=[pl.BlockSpec(memory_space=pl.ANY)] + [pl.BlockSpec(memory_space=pltpu.VMEM)] * 3,
        out_specs=[pl.BlockSpec(memory_space=pl.ANY)] * 5,
        scratch_shapes=scratch,
        compiler_params=pltpu.CompilerParams(
            collective_id=0, has_side_effects=True, vmem_limit_bytes=60 << 20
        ),
    )(counts, dead_time[None, :], flat_field[None, :], cycle_map[None, :])
    group = owned // 2
    return pl.pallas_call(
        functools.partial(assemble, results),
        grid=(owned // group,),
        out_shape=jax.ShapeDtypeStruct((owned, frames, tm * frames), f32),
        in_specs=[
            pl.BlockSpec((group, *shape[1:]), lambda r: (r, 0, 0))
            if len(shape) == 3
            else pl.BlockSpec((shape[0], group, *shape[2:]), lambda r: (0, r, 0, 0))
            for shape, _ in shapes
        ],
        out_specs=pl.BlockSpec((group, frames, tm * frames), lambda r: (r, 0, 0)),
    )(*made)


def solution(mesh):
    kernel_path = fits_kernel(mesh.shape)
    device_program = per_device_kernel if kernel_path else per_device
    placed = (P("tm", "pix"), P("pix"), P("pix"), P("pix"))

    return jax.shard_map(
        device_program, mesh=mesh, in_specs=placed, out_specs=P("pix", "tm", None), check_vma=False
    )
```

```python
import functools
import math

import jax
import jax.numpy as jnp
from jax import lax
from jax.experimental import pallas as pl
from jax.experimental.pallas import tpu as pltpu
from jax.sharding import PartitionSpec as P

CYCLES = 32


def inner_extent(count):
    return max(d for d in range(1, count + 1) if count % d == 0 and d * d <= count)


class LogCode:
    def __init__(self, low, high, zero):
        self.low, self.zero = low, zero
        low, high = math.log2(low), math.log2(high)
        self.centre, self.steps = (high + low) / 2, 65400 / (high - low)

    def encode(self, value):
        level = (jnp.log2(jnp.maximum(value, self.low)) - self.centre) * self.steps
        return jnp.round(level).astype(jnp.int16)

    def decode(self, code):
        level = code.astype(jnp.float32)
        value = jnp.exp2(level * (1.0 / self.steps) + self.centre)
        return jnp.where(level > -32700 + 32, value, 0.0) if self.zero else value


def per_device(counts, dead_time, flat_field, cycle_map):
    intensity = (counts / (1.0 - dead_time[None, :] * counts) * flat_field[None, :]).astype(
        jnp.bfloat16
    )
    frames, pixels = intensity.shape
    tm, pix = lax.axis_size("tm"), lax.axis_size("pix")
    inner = inner_extent(tm)
    outer = tm // inner
    cores = 2 if pix % 2 == 0 else 1
    across = pix // cores
    owned = CYCLES // pix
    at_tm, at_pix = lax.axis_index("tm"), lax.axis_index("pix")
    z, y = at_tm // inner, at_tm % inner
    x, core = at_pix // cores, at_pix % cores

    def shift_z(value, k=1):
        return lax.ppermute(
            value, "tm", [(i, (i // inner + k) % outer * inner + i % inner) for i in range(tm)]
        )

    def shift_y(value, k):
        return lax.ppermute(
            value, "tm", [(i, i // inner * inner + (i % inner + k) % inner) for i in range(tm)]
        )

    def shift_x(value, k):
        return lax.ppermute(
            value, "pix", [(i, (i // cores + k) % across * cores + i % cores) for i in range(pix)]
        )

    def swap_core(value):
        return lax.ppermute(
            value, "pix", [(i, i // cores * cores + (i % cores + 1) % cores) for i in range(pix)]
        )

    half = outer // 2
    remote = {0: intensity}
    for s in range(1, half + 1):
        remote[s] = shift_z(remote[s - 1])
    beside = [intensity]
    for k in range(1, inner):
        beside.append(shift_y(intensity, k))

    def onehot_of(owner_core, ks):
        ids = jnp.concatenate(
            [
                ((x + k) % across * cores + owner_core) * owned
                + jnp.arange(owned, dtype=jnp.int32)
                for k in ks
            ]
        )
        return (cycle_map[None, :] == ids[:, None]).astype(jnp.bfloat16)

    other = (core + 1) % cores
    away_ks, own_ks = range(1, across), range(1)
    rows = frames + 8

    def gram(onehot, left, right, sums):
        masked = (onehot[:, None, :] * left[None, :, :]).reshape(-1, pixels)
        value = lax.dot_general(
            masked, right, (((1,), (1,)), ((), ())), preferred_element_type=jnp.float32
        ).reshape(onehot.shape[0], rows, right.shape[0])
        if sums is not None:
            own = lax.dot_general(
                onehot, sums, (((1,), (1,)), ((), ())), preferred_element_type=jnp.float32
            )
            value = value + jnp.pad(
                own[:, None, :], ((0, 0), (frames, 7), (0, right.shape[0] - frames))
            )
        return value

    partials = LogCode(0.0218, 6800.0 * pixels * cores, True)
    results = LogCode(1 / 140.0, 140.0, False)

    def reduce_owned(left, right, sums=None, exact=False):
        def part(owner_core, ks):
            return gram(onehot_of(owner_core, ks), left, right, sums)

        theirs = {}
        for name, ks in (("o", away_ks), ("x", own_ks)):
            if cores > 1 and len(ks):
                theirs[name] = swap_core(part(other, ks))
        total = None
        if across > 1:
            sent = part(core, away_ks)
            if cores > 1:
                sent = sent + theirs["o"]
            got = []
            for k in range(1, across):
                value = sent[(k - 1) * owned : k * owned]
                if not exact:
                    value = partials.encode(value)
                value = shift_x(value, k)
                got.append(value if exact else partials.decode(value))
            total = sum(got[1:], got[0])
        here = part(core, own_ks)
        if cores > 1:
            here = here + theirs["x"]
        here = lax.optimization_barrier(here)
        return here if total is None else here + total

    out = jnp.zeros((owned, frames, tm * frames), jnp.float32)

    def place(out, value, zs, ys):
        at = (zs % outer * inner + ys % inner) * frames
        return lax.dynamic_update_slice_in_dim(out, value, at, 2)

    ones = jnp.ones((8, pixels), jnp.bfloat16)
    extended = jnp.concatenate([intensity, ones], axis=0)
    total = reduce_owned(extended, extended, exact=True)
    row_sums = total[:, :frames, frames]
    scale = total[:, frames, frames][:, None, None] / row_sums[:, :, None]
    column_sums = [total[:, frames : frames + 1, :frames]]
    size = total[:, frames : frames + 1, frames : frames + 1]
    out = place(out, total[:, :frames, :frames] * scale / column_sums[0], z, y)
    group = jnp.concatenate(beside, axis=0)

    def beside_group(out):
        if inner == 1:
            return out
        total = reduce_owned(extended, group[frames:])
        for k in range(1, inner):
            part = total[:, :, (k - 1) * frames : k * frames]
            column_sums.append(part[:, frames : frames + 1])
            out = place(out, part[:, :frames] * scale / column_sums[k], z, y - k)
        return out

    def remote_group(s, out):
        left = jnp.concatenate([remote[s], jnp.zeros((8, pixels), jnp.bfloat16)], axis=0)
        total = reduce_owned(left, group, sums=remote[s])
        left_sums = jnp.transpose(total[:, frames : frames + 1, :frames], (0, 2, 1))
        value = total[:, :frames] * (size / left_sums) / jnp.concatenate(column_sums, axis=2)
        if 2 * s != outer:
            back = shift_z(results.encode(value), -s)
            back = results.decode(back)
            for k in range(inner):
                out = place(out, back[:, :, k * frames : (k + 1) * frames], z + s, y - k)
        for k in range(inner):
            block = jnp.transpose(value[:, :, k * frames : (k + 1) * frames], (0, 2, 1))
            if k > 0:
                block = results.decode(shift_y(results.encode(block), -k))
            out = place(out, block, z - s, y + k)
        return out

    out = beside_group(out)
    for s in range(1, half + 1):
        out = remote_group(s, out)
    return out


MESH = pl.DeviceIdType.MESH
TILE = 16
CHUNKS = 2
PIECES = 4
LAG = 3
GROUP = 2


def fits_kernel(shape):
    inner = inner_extent(shape["tm"])
    return shape["tm"] // inner == 4 and inner == 2 and shape["pix"] == 4


def exchange(owned, partials, results, *refs):
    (counts, dead_source, flat_source, cycle_source,
     diagonal, pair, local, side_in, back_in, diag_rows, pair_rows, local_rows, local_turned,
     wide, right, ring, swap_out, swap_in, x_out, x_in, here, side_out, back_out,
     diag_out, diag_in, diag_x_out, diag_x_in, diag_here,
     pair_out, pair_in, pair_x_out, pair_x_in, pair_here,
     sums_out, sums_core, sums_chip, sums_x, scale_own, scale_side, scale_first, scale_second,
     columns, pair_columns, lanes,
     core_send, core_recv, x_send, x_recv, up_send, up_recv, back_send, back_recv,
     side_send, side_recv, diag_send, diag_recv, pair_send, pair_recv, sum_send, sum_recv, keep_sem,
     y_send, y_recv, diag_core_send, diag_core_recv, pair_core_send, pair_core_recv,
     fine_swap_out, fine_swap_in, fine_x_out, fine_x_in, fine_here, fine_side_out,
     fine_core_send, fine_core_recv, fine_x_send, fine_x_recv, fine_side_send, fine_side_recv,
     raw_counts, load_sem, dead_time, flat_field, cycle_map) = refs
    frames, pixels = counts.shape
    step, fine = frames // CHUNKS, frames // PIECES
    at_tm, at_pix = lax.axis_index("tm"), lax.axis_index("pix")
    z, y = at_tm // 2, at_tm % 2
    x, core = at_pix // 2, at_pix % 2
    to_y = {"tm": z * 2 + 1 - y}
    to_up = {"tm": (z + 1) % 4 * 2 + y}
    to_down = {"tm": (z + 3) % 4 * 2 + y}
    to_core = {"pix": x * 2 + 1 - core}
    to_x = {"pix": (1 - x) * 2 + core}
    own, beside, every = pl.ds(0, frames), pl.ds(frames, frames), pl.ds(0, 2 * frames)

    barrier = pltpu.get_barrier_semaphore()
    for target in (to_y, to_up, to_down, to_core, to_x):
        pl.semaphore_signal(barrier, inc=1, device_id=target, device_id_type=MESH)

    loads = [
        pltpu.make_async_copy(counts.at[rows], raw_counts.at[rows], load_sem.at[q])
        for q, rows in enumerate(pl.ds(q * fine, fine) for q in range(PIECES))
    ]
    per_pixel = [
        pltpu.make_async_copy(source, target, load_sem.at[PIECES + k])
        for k, (source, target) in enumerate(
            ((dead_source, dead_time), (flat_source, flat_field), (cycle_source, cycle_map))
        )
    ]
    for load in [*per_pixel[:2], *loads, per_pixel[2]]:
        load.start()
    for load in per_pixel[:2]:
        load.wait()

    def correct(i, carry):
        rows = pl.ds(pl.multiple_of(i * TILE, TILE), TILE)
        raw = raw_counts[rows, :]
        value = raw / (1.0 - dead_time[...] * raw) * flat_field[...]
        right[rows, :] = value.astype(jnp.bfloat16)
        return carry

    def correct_piece(q):
        loads[q].wait()
        lax.fori_loop(q * fine // TILE, (q + 1) * fine // TILE, correct, 0)

    def remote(source, target, send, recv, device):
        return pltpu.make_async_remote_copy(
            src_ref=source, dst_ref=target, send_sem=send, recv_sem=recv,
            device_id=device, device_id_type=MESH,
        )

    copies = []

    def start(*args):
        copy = remote(*args)
        copy.start()
        copies.append(copy)
        return copy

    def chunk(n):
        return pl.ds(pl.multiple_of(n * step, step), step)

    for q in range(PIECES // CHUNKS):
        correct_piece(q)
    pl.semaphore_wait(barrier, 5)

    def to_ring(n):
        return remote(right.at[chunk(n)], ring.at[chunk(n)], up_send.at[n], up_recv.at[n], to_up)

    to_rings = [to_ring(n) for n in range(CHUNKS)]
    to_rings[0].start()
    for q in range(PIECES // CHUNKS, PIECES):
        correct_piece(q)
    deep = pixels // 2

    def depth(h):
        return pl.ds(0, deep) if h == 0 else pl.ds(deep, pixels - deep)

    by_side = [
        start(right.at[own, depth(h)], right.at[beside, depth(h)], y_send.at[h], y_recv.at[h], to_y)
        for h in range(2)
    ]

    def piece(m, offset=0):
        return pl.ds(pl.multiple_of(offset + m * fine, fine), fine)

    def forward(m):
        return remote(ring.at[piece(m)], ring.at[piece(m, frames)],
                      up_send.at[m + CHUNKS], up_recv.at[m + CHUNKS], to_up)

    landed = [forward(m) for m in range(PIECES)]
    copies += to_rings + landed

    per_pixel[2].wait()
    ids = lax.broadcasted_iota(jnp.int32, (CYCLES, pixels), 0)
    onehot = jnp.where(jnp.broadcast_to(cycle_map[...], (CYCLES, pixels)) == ids, 1.0, 0.0)
    counted = lax.dot_general(
        onehot.astype(jnp.bfloat16), right[own, :], (((1,), (1,)), ((), ())),
        preferred_element_type=jnp.float32,
    )
    size = jnp.sum(onehot, axis=1, keepdims=True)
    sums_out[:, own] = counted
    sums_out[:, beside] = jnp.broadcast_to(size, counted.shape)
    by_core = start(sums_out, sums_core, sum_send.at[0], sum_recv.at[0], to_core)

    def fill(r, carry):
        hit = jnp.broadcast_to(cycle_map[...], (TILE, pixels)) == r
        wide[r] = jnp.where(hit, 1.0, 0.0).astype(jnp.bfloat16)
        return carry

    lax.fori_loop(0, CYCLES // 2, fill, 0)
    by_core.wait_recv()
    sums_chip[...] = sums_out[...] + sums_core[...]
    by_x = start(sums_chip, sums_x, sum_send.at[1], sum_recv.at[1], to_x)
    lax.fori_loop(CYCLES // 2, CYCLES, fill, 0)
    by_x.wait_recv()
    mine = pl.ds(pl.multiple_of(at_pix * owned, owned), owned)
    scale_own[...] = sums_chip[mine, :] + sums_x[mine, :]
    by_y = start(scale_own, scale_side, sum_send.at[2], sum_recv.at[2], to_y)
    by_up = start(scale_own, scale_first, sum_send.at[3], sum_recv.at[3], to_up)
    for n in range(1, CHUNKS):
        to_rings[n].start()

    def product(left, rows, count, cols, made, j, ks, add):
        base = (lax.rem(x + 1 + j, 2) * 2 + lax.rem(core + 1 + j // 2, 2)) * owned
        block = left[rows, ks].reshape(count // TILE, TILE, ks.size)
        masked = jnp.concatenate(
            [(block * wide[base + i, :, ks][None]).reshape(count, ks.size) for i in range(owned)],
            axis=0,
        )
        value = lax.dot_general(
            masked, right[cols, ks], (((1,), (1,)), ((), ())), preferred_element_type=jnp.float32
        ).reshape(owned, count, cols.size)
        made[j] = made[j] + value if add else value

    def early(left, rows, count, cols, made):
        def body(j, carry):
            product(left, rows, count, cols, made, j, depth(0), False)
            return carry

        lax.fori_loop(0, 4, body, 0)

    def send_across(unit):
        unit["others"][0].wait_recv()
        unit["code_out"][...] = partials.encode(unit["block"][4][2] + unit["inn"][0])
        unit["across"].start()

    def settle(unit):
        unit["others"][1].wait_recv()
        unit["here"][...] = unit["block"][4][3] + unit["inn"][1]

    def reduce_unit(unit, before=None, late=False, final=False):
        ks = depth(1) if late else pl.ds(0, pixels)

        def body(j, carry):
            product(*unit["block"], j, ks, late)

            @pl.when(j == 0)
            def _():
                unit["others"][0].start()
                if before is not None:
                    send_across(before)

            @pl.when(j == 1)
            def _():
                unit["others"][1].start()
                if before is not None:
                    settle(before)

            if final:

                @pl.when(j == 2)
                def _():
                    send_across(unit)

            return carry

        lax.fori_loop(0, 4, body, 0)

    half = frames // 2

    def keep(source, target, n):
        return pltpu.make_async_copy(source, target, keep_sem.at[n])

    def diag_core(n):
        return [
            remote(diag_out.at[n, g], diag_in.at[n, g],
                   diag_core_send.at[n, g], diag_core_recv.at[n, g], to_core)
            for g in range(2)
        ]

    def diag_across(n):
        return remote(diag_x_out.at[n], diag_x_in.at[n],
                      diag_send.at[n], diag_recv.at[n], to_x)

    def diag_unit(n):
        return dict(
            block=(right, pl.ds(n * half, half), half, own, diag_out.at[n]), inn=diag_in.at[n],
            others=diag_core(n), code_out=diag_x_out.at[n], across=diag_across(n), here=diag_here.at[n],
        )

    diags = [diag_unit(0), diag_unit(1)]
    reduce_unit(diags[0])
    reduce_unit(diags[1], diags[0])
    for unit in diags:
        copies += [*unit["others"], unit["across"]]

    def pass_on(n):
        remote(ring.at[chunk(n)], ring.at[chunk(n)], up_send.at[n], up_recv.at[n], to_up).wait_recv()
        for m in range(n * PIECES // CHUNKS, (n + 1) * PIECES // CHUNKS):
            landed[m].start()

    by_up.wait_recv()
    by_up2 = start(scale_first, scale_second, sum_send.at[4], sum_recv.at[4], to_up)
    for n in range(CHUNKS - 1):
        pass_on(n)
    half_rows = pl.ds(pl.multiple_of(y * half, half), half)
    pair_block = (right, pl.ds(pl.multiple_of(y * (frames + half), half), half), half,
                  pl.ds(pl.multiple_of((1 - y) * frames, frames), frames), pair_out)

    by_side[0].wait_recv()
    early(*pair_block)
    send_across(diags[1])
    settle(diags[1])
    early(ring, chunk(0), step, every, swap_out.at[0])
    size = scale_own[:, beside]
    own_sums = scale_own[:, own]
    own_columns = jnp.transpose(size / own_sums, (1, 0))
    columns[own, :] = jnp.transpose(size / scale_first[:, own], (1, 0))
    for n in range(2):
        rows = pl.ds(n * half, half)
        diags[n]["across"].wait_recv()
        for r in range(owned):
            value = diag_here[n, r] + partials.decode(diag_x_in[n, r])
            value = value * own_columns[n * half : (n + 1) * half, r : r + 1]
            diag_rows[r, rows, :] = value * (1.0 / own_sums[r : r + 1])
    keep(diag_rows, diagonal, 0).start()

    pair_across = remote(pair_x_out, pair_x_in, pair_send.at[1], pair_recv.at[1], to_x)
    pair_core = [
        remote(pair_out.at[g], pair_in.at[g], pair_core_send.at[g], pair_core_recv.at[g], to_core)
        for g in range(2)
    ]
    by_side[1].wait_recv()
    pass_on(CHUNKS - 1)
    pair_unit = dict(block=pair_block, others=pair_core, inn=pair_in, code_out=pair_x_out,
                     across=pair_across, here=pair_here)
    reduce_unit(pair_unit, late=True)
    copies += [*pair_core, pair_across]

    by_y.wait_recv()
    side_sums = scale_side[:, own]
    lower = y == 0
    pair_columns[...] = jnp.transpose(size / jnp.where(lower, own_sums, side_sums), (1, 0))
    pair_lanes = 1.0 / jnp.where(lower, side_sums, own_sums)
    lanes[...] = 1.0 / jnp.concatenate([own_sums, side_sums], axis=1)

    def coarse(n):
        rows = chunk(n)
        return dict(
            block=(ring, rows, step, every, swap_out.at[n]), rows=rows, inn=swap_in.at[n],
            others=[remote(swap_out.at[n, g], swap_in.at[n, g],
                           core_send.at[n, g], core_recv.at[n, g], to_core) for g in range(2)],
            code_out=x_out.at[n], code_in=x_in.at[n],
            across=remote(x_out.at[n], x_in.at[n], x_send.at[n], x_recv.at[n], to_x),
            here=here.at[n], side=side_out.at[n], back=back_out.at[n],
            to_side=remote(side_out.at[n], side_in.at[:, rows], side_send.at[n], side_recv.at[n], to_y),
            to_back=remote(back_out.at[n], back_in.at[:, rows], back_send.at[n], back_recv.at[n], to_down),
        )

    def fine_unit(m):
        rows = piece(m, frames)
        return dict(
            block=(ring, rows, fine, every, fine_swap_out.at[m]), rows=rows, inn=fine_swap_in.at[m],
            others=[remote(fine_swap_out.at[m, g], fine_swap_in.at[m, g],
                           fine_core_send.at[m, g], fine_core_recv.at[m, g], to_core)
                    for g in range(2)],
            code_out=fine_x_out.at[m], code_in=fine_x_in.at[m],
            across=remote(fine_x_out.at[m], fine_x_in.at[m], fine_x_send.at[m], fine_x_recv.at[m], to_x),
            here=fine_here.at[m], side=fine_side_out.at[m], back=None,
            to_side=remote(fine_side_out.at[m], side_in.at[:, rows],
                           fine_side_send.at[m], fine_side_recv.at[m], to_y),
        )

    by_pair = remote(pair_rows, pair.at[:, half_rows], pair_send.at[0], pair_recv.at[0], to_y)

    def finish(unit):
        unit["across"].wait_recv()
        rows, back = unit["rows"], unit["back"]
        for r in range(owned):
            value = unit["here"][r] + partials.decode(unit["code_in"][r])
            value = value * columns[rows, r : r + 1] * lanes[r : r + 1, :]
            if back is not None:
                back[r] = results.encode(value)
            unit["side"][r] = results.encode(value[:, frames:])
            local_rows[r, rows, :] = value[:, :frames]
        if back is not None:
            unit["to_back"].start()
        unit["to_side"].start()

    def turn(s):
        for r in range(owned):
            local_turned[s, r] = jnp.transpose(local_rows[r, pl.ds(s * frames, frames), :], (1, 0))
        keep(local_turned.at[s], local.at[s], 1 + s).start()

    chain = [*map(coarse, range(CHUNKS)), *map(fine_unit, range(PIECES))]
    for k, unit in enumerate(chain):
        if k >= CHUNKS:
            landed[k - CHUNKS].wait_recv()
        reduce_unit(unit, chain[k - 1] if k else pair_unit, k == 0, k == len(chain) - 1)
        if k == 1:
            pair_across.wait_recv()
            for r in range(owned):
                value = pair_here[r] + partials.decode(pair_x_in[r])
                value = value * pair_columns[half_rows, r : r + 1] * pair_lanes[r : r + 1]
                pair_rows[r] = results.encode(value)
            by_pair.start()
            keep(pair_rows, pair.at[:, half_rows], 3).start()
        if k >= LAG:
            finish(chain[k - LAG])
        if k == CHUNKS:
            by_up2.wait_recv()
            columns[beside, :] = jnp.transpose(size / scale_second[:, own], (1, 0))
        if k == CHUNKS - 1 + LAG:
            turn(0)
    settle(chain[-1])
    for unit in chain[-LAG:-1]:
        finish(unit)
    finish(chain[-1])
    turn(1)
    by_pair.wait_recv()
    copies.append(by_pair)
    for unit in chain:
        landing = [unit["to_side"]] + ([] if unit["back"] is None else [unit["to_back"]])
        for copy in landing:
            copy.wait_recv()
        copies += [*unit["others"], unit["across"], *landing]
    keep(diag_rows, diagonal, 0).wait()
    for s in range(2):
        keep(local_turned.at[s], local.at[s], 1 + s).wait()
    keep(pair_rows, pair.at[:, half_rows], 3).wait()
    for copy in copies:
        copy.wait_send()


def assemble(results, *refs):
    inputs, out, held, rows, in_sem, out_sem = refs[:5], refs[5], refs[6:11], refs[11], refs[12], refs[13]
    diagonal, pair, local, side, back = held
    owned = diagonal.shape[0]

    def cut(ref, r):
        span = pl.ds(r, GROUP)
        return ref.at[:, span] if len(ref.shape) == 4 else ref.at[span]

    loads = [
        [
            pltpu.make_async_copy(cut(source, r), cut(target, r), in_sem.at[r // GROUP, k])
            for k, (source, target) in enumerate(zip(inputs, held))
        ]
        for r in range(0, owned, GROUP)
    ]
    for group in loads:
        for load in group:
            load.start()
    frames = diagonal.shape[1]
    at_tm = lax.axis_index("tm")
    z, y = at_tm // 2, at_tm % 2

    def turn(value):
        return jnp.transpose(value, (1, 0))

    stores = []
    for r in range(owned):
        if r % GROUP == 0:
            for load in loads[r // GROUP]:
                load.wait()

        def put(dz, dy, value):
            block = (z + dz + 4) % 4 * 2 + (y + dy) % 2
            rows[r, :, pl.ds(pl.multiple_of(block * frames, frames), frames)] = value

        put(0, 0, diagonal[r])
        value = results.decode(pair[r])
        put(0, 1, jnp.where(y == 0, value, turn(value)))
        for s in range(2):
            put(-1 - s, 0, local[s, r])
            put(-1 - s, 1, turn(results.decode(side[r, pl.ds(s * frames, frames), :])))
        value = results.decode(back[r])
        put(1, 0, value[:, :frames])
        put(1, 1, value[:, frames:])
        if r % GROUP == GROUP - 1:
            span = pl.ds(r - GROUP + 1, GROUP)
            stores.append(pltpu.make_async_copy(rows.at[span], out.at[span], out_sem.at[r // GROUP]))
            stores[-1].start()
    for store in stores:
        store.wait()


def per_device_kernel(counts, dead_time, flat_field, cycle_map):
    frames, pixels = counts.shape
    if frames % (PIECES * TILE):
        return per_device(counts, dead_time, flat_field, cycle_map)
    tm, pix = lax.axis_size("tm"), lax.axis_size("pix")
    owned = CYCLES // pix
    partials = LogCode(0.0218, 6800.0 * pixels * 2, True)
    results = LogCode(1 / 140.0, 140.0, False)
    f32, bf16, i16 = jnp.float32, jnp.bfloat16, jnp.int16
    vmem, dma = pltpu.VMEM, pltpu.SemaphoreType.DMA
    both, half, step, fine = 2 * frames, frames // 2, frames // CHUNKS, frames // PIECES
    units, pieces, rings = CHUNKS, PIECES, CHUNKS + PIECES
    small = (owned, both)
    scratch = [
        vmem((owned, frames, frames), f32),
        vmem((owned, half, frames), i16),
        vmem((owned, both, frames), f32),
        vmem((2, owned, frames, frames), f32),
        vmem((CYCLES, TILE, pixels), bf16),
        vmem((both, pixels), bf16),
        vmem((both, pixels), bf16),
        vmem((units, 4, owned, step, both), f32),
        vmem((units, 2, owned, step, both), f32),
        *[vmem((units, owned, step, both), i16)] * 2,
        vmem((units, owned, step, both), f32),
        vmem((units, owned, step, frames), i16),
        vmem((units, owned, step, both), i16),
        vmem((2, 4, owned, half, frames), f32),
        vmem((2, 2, owned, half, frames), f32),
        *[vmem((2, owned, half, frames), i16)] * 2,
        vmem((2, owned, half, frames), f32),
        vmem((4, owned, half, frames), f32),
        vmem((2, owned, half, frames), f32),
        *[vmem((owned, half, frames), i16)] * 2,
        vmem((owned, half, frames), f32),
        *[vmem((CYCLES, both), f32)] * 4,
        *[vmem(small, f32)] * 4,
        vmem((both, owned), f32),
        vmem((frames, owned), f32),
        vmem(small, f32),
        dma((units, 2)), dma((units, 2)), dma((units,)), dma((units,)),
        dma((rings,)), dma((rings,)), dma((CHUNKS,)), dma((CHUNKS,)),
        dma((units,)), dma((units,)), dma((2,)), dma((2,)), dma((2,)), dma((2,)),
        dma((5,)), dma((5,)), dma((4,)), dma((2,)), dma((2,)), dma((2, 2)), dma((2, 2)), dma((2,)), dma((2,)),
        vmem((pieces, 4, owned, fine, both), f32),
        vmem((pieces, 2, owned, fine, both), f32),
        *[vmem((pieces, owned, fine, both), i16)] * 2,
        vmem((pieces, owned, fine, both), f32),
        vmem((pieces, owned, fine, frames), i16),
        dma((pieces, 2)), dma((pieces, 2)), dma((pieces,)), dma((pieces,)), dma((pieces,)), dma((pieces,)),
        vmem((frames, pixels), f32), dma((pieces + 3,)),
        *[vmem((1, pixels), f32)] * 2, vmem((1, pixels), jnp.int32),
    ]
    shapes = [
        ((owned, frames, frames), f32), ((owned, frames, frames), i16),
        ((2, owned, frames, frames), f32), ((owned, both, frames), i16), ((owned, frames, both), i16),
    ]
    made = pl.pallas_call(
        functools.partial(exchange, owned, partials, results),
        out_shape=[jax.ShapeDtypeStruct(*shape) for shape in shapes],
        in_specs=[pl.BlockSpec(memory_space=pl.ANY)] * 4,
        out_specs=[pl.BlockSpec(memory_space=pl.ANY)] * 5,
        scratch_shapes=scratch,
        compiler_params=pltpu.CompilerParams(
            collective_id=0, has_side_effects=True, vmem_limit_bytes=60 << 20
        ),
    )(counts, dead_time[None, :], flat_field[None, :], cycle_map[None, :])
    return pl.pallas_call(
        functools.partial(assemble, results),
        out_shape=jax.ShapeDtypeStruct((owned, frames, tm * frames), f32),
        in_specs=[pl.BlockSpec(memory_space=pl.ANY)] * len(shapes),
        out_specs=pl.BlockSpec(memory_space=pl.ANY),
        scratch_shapes=[
            *[vmem(*shape) for shape in shapes],
            vmem((owned, frames, tm * frames), f32),
            dma((owned // GROUP, len(shapes))), dma((owned // GROUP,)),
        ],
        compiler_params=pltpu.CompilerParams(vmem_limit_bytes=60 << 20),
    )(*made)


def solution(mesh):
    kernel_path = fits_kernel(mesh.shape)
    device_program = per_device_kernel if kernel_path else per_device
    placed = (P("tm", "pix"), P("pix"), P("pix"), P("pix"))

    return jax.shard_map(
        device_program, mesh=mesh, in_specs=placed, out_specs=P("pix", "tm", None), check_vma=False
    )
```

```python
import functools
import math

import jax
import jax.numpy as jnp
from jax import lax
from jax.experimental import pallas as pl
from jax.experimental.pallas import tpu as pltpu
from jax.sharding import PartitionSpec as P

CYCLES = 32


def inner_extent(count):
    return max(d for d in range(1, count + 1) if count % d == 0 and d * d <= count)


class LogCode:
    def __init__(self, low, high, zero):
        self.low, self.zero = low, zero
        low, high = math.log2(low), math.log2(high)
        self.centre, self.steps = (high + low) / 2, 65400 / (high - low)

    def encode(self, value):
        level = (jnp.log2(jnp.maximum(value, self.low)) - self.centre) * self.steps
        return jnp.round(level).astype(jnp.int16)

    def decode(self, code):
        level = code.astype(jnp.float32)
        value = jnp.exp2(level * (1.0 / self.steps) + self.centre)
        return jnp.where(level > -32700 + 32, value, 0.0) if self.zero else value


def per_device(counts, dead_time, flat_field, cycle_map):
    intensity = (counts / (1.0 - dead_time[None, :] * counts) * flat_field[None, :]).astype(
        jnp.bfloat16
    )
    frames, pixels = intensity.shape
    tm, pix = lax.axis_size("tm"), lax.axis_size("pix")
    inner = inner_extent(tm)
    outer = tm // inner
    cores = 2 if pix % 2 == 0 else 1
    across = pix // cores
    owned = CYCLES // pix
    at_tm, at_pix = lax.axis_index("tm"), lax.axis_index("pix")
    z, y = at_tm // inner, at_tm % inner
    x, core = at_pix // cores, at_pix % cores

    def shift_z(value, k=1):
        return lax.ppermute(
            value, "tm", [(i, (i // inner + k) % outer * inner + i % inner) for i in range(tm)]
        )

    def shift_y(value, k):
        return lax.ppermute(
            value, "tm", [(i, i // inner * inner + (i % inner + k) % inner) for i in range(tm)]
        )

    def shift_x(value, k):
        return lax.ppermute(
            value, "pix", [(i, (i // cores + k) % across * cores + i % cores) for i in range(pix)]
        )

    def swap_core(value):
        return lax.ppermute(
            value, "pix", [(i, i // cores * cores + (i % cores + 1) % cores) for i in range(pix)]
        )

    half = outer // 2
    remote = {0: intensity}
    for s in range(1, half + 1):
        remote[s] = shift_z(remote[s - 1])
    beside = [intensity]
    for k in range(1, inner):
        beside.append(shift_y(intensity, k))

    def onehot_of(owner_core, ks):
        ids = jnp.concatenate(
            [
                ((x + k) % across * cores + owner_core) * owned
                + jnp.arange(owned, dtype=jnp.int32)
                for k in ks
            ]
        )
        return (cycle_map[None, :] == ids[:, None]).astype(jnp.bfloat16)

    other = (core + 1) % cores
    away_ks, own_ks = range(1, across), range(1)
    rows = frames + 8

    def gram(onehot, left, right, sums):
        masked = (onehot[:, None, :] * left[None, :, :]).reshape(-1, pixels)
        value = lax.dot_general(
            masked, right, (((1,), (1,)), ((), ())), preferred_element_type=jnp.float32
        ).reshape(onehot.shape[0], rows, right.shape[0])
        if sums is not None:
            own = lax.dot_general(
                onehot, sums, (((1,), (1,)), ((), ())), preferred_element_type=jnp.float32
            )
            value = value + jnp.pad(
                own[:, None, :], ((0, 0), (frames, 7), (0, right.shape[0] - frames))
            )
        return value

    partials = LogCode(0.0218, 6800.0 * pixels * cores, True)
    results = LogCode(1 / 140.0, 140.0, False)

    def reduce_owned(left, right, sums=None, exact=False):
        def part(owner_core, ks):
            return gram(onehot_of(owner_core, ks), left, right, sums)

        theirs = {}
        for name, ks in (("o", away_ks), ("x", own_ks)):
            if cores > 1 and len(ks):
                theirs[name] = swap_core(part(other, ks))
        total = None
        if across > 1:
            sent = part(core, away_ks)
            if cores > 1:
                sent = sent + theirs["o"]
            got = []
            for k in range(1, across):
                value = sent[(k - 1) * owned : k * owned]
                if not exact:
                    value = partials.encode(value)
                value = shift_x(value, k)
                got.append(value if exact else partials.decode(value))
            total = sum(got[1:], got[0])
        here = part(core, own_ks)
        if cores > 1:
            here = here + theirs["x"]
        here = lax.optimization_barrier(here)
        return here if total is None else here + total

    out = jnp.zeros((owned, frames, tm * frames), jnp.float32)

    def place(out, value, zs, ys):
        at = (zs % outer * inner + ys % inner) * frames
        return lax.dynamic_update_slice_in_dim(out, value, at, 2)

    ones = jnp.ones((8, pixels), jnp.bfloat16)
    extended = jnp.concatenate([intensity, ones], axis=0)
    total = reduce_owned(extended, extended, exact=True)
    row_sums = total[:, :frames, frames]
    scale = total[:, frames, frames][:, None, None] / row_sums[:, :, None]
    column_sums = [total[:, frames : frames + 1, :frames]]
    size = total[:, frames : frames + 1, frames : frames + 1]
    out = place(out, total[:, :frames, :frames] * scale / column_sums[0], z, y)
    group = jnp.concatenate(beside, axis=0)

    def beside_group(out):
        if inner == 1:
            return out
        total = reduce_owned(extended, group[frames:])
        for k in range(1, inner):
            part = total[:, :, (k - 1) * frames : k * frames]
            column_sums.append(part[:, frames : frames + 1])
            out = place(out, part[:, :frames] * scale / column_sums[k], z, y - k)
        return out

    def remote_group(s, out):
        left = jnp.concatenate([remote[s], jnp.zeros((8, pixels), jnp.bfloat16)], axis=0)
        total = reduce_owned(left, group, sums=remote[s])
        left_sums = jnp.transpose(total[:, frames : frames + 1, :frames], (0, 2, 1))
        value = total[:, :frames] * (size / left_sums) / jnp.concatenate(column_sums, axis=2)
        if 2 * s != outer:
            back = shift_z(results.encode(value), -s)
            back = results.decode(back)
            for k in range(inner):
                out = place(out, back[:, :, k * frames : (k + 1) * frames], z + s, y - k)
        for k in range(inner):
            block = jnp.transpose(value[:, :, k * frames : (k + 1) * frames], (0, 2, 1))
            if k > 0:
                block = results.decode(shift_y(results.encode(block), -k))
            out = place(out, block, z - s, y + k)
        return out

    out = beside_group(out)
    for s in range(1, half + 1):
        out = remote_group(s, out)
    return out


MESH = pl.DeviceIdType.MESH
TILE = 16
CHUNKS = 2
PIECES = 4
LAG = 3
GROUP = 1


def fits_kernel(shape):
    inner = inner_extent(shape["tm"])
    return shape["tm"] // inner == 4 and inner == 2 and shape["pix"] == 4


def exchange(owned, partials, results, *refs):
    (counts, dead_source, flat_source, cycle_source,
     diagonal, pair, local, side_in, back_in, diag_rows, pair_rows, local_rows, local_turned,
     wide, right, ring, swap_out, swap_in, x_out, x_in, here, side_out, back_out,
     diag_out, diag_in, diag_x_out, diag_x_in, diag_here,
     pair_out, pair_in, pair_x_out, pair_x_in, pair_here,
     sums_out, sums_core, sums_chip, sums_x, scale_own, scale_side, scale_first, scale_second,
     columns, pair_columns, lanes,
     core_send, core_recv, x_send, x_recv, up_send, up_recv, back_send, back_recv,
     side_send, side_recv, diag_send, diag_recv, pair_send, pair_recv, sum_send, sum_recv, keep_sem,
     y_send, y_recv, diag_core_send, diag_core_recv, pair_core_send, pair_core_recv,
     fine_swap_out, fine_swap_in, fine_x_out, fine_x_in, fine_here, fine_side_out,
     fine_core_send, fine_core_recv, fine_x_send, fine_x_recv, fine_side_send, fine_side_recv,
     raw_counts, load_sem, dead_time, flat_field, cycle_map) = refs
    frames, pixels = counts.shape
    step, fine = frames // CHUNKS, frames // PIECES
    at_tm, at_pix = lax.axis_index("tm"), lax.axis_index("pix")
    z, y = at_tm // 2, at_tm % 2
    x, core = at_pix // 2, at_pix % 2
    to_y = {"tm": z * 2 + 1 - y}
    to_up = {"tm": (z + 3) % 4 * 2 + y}
    to_down = {"tm": (z + 1) % 4 * 2 + y}
    to_core = {"pix": x * 2 + 1 - core}
    to_x = {"pix": (1 - x) * 2 + core}
    own, beside, every = pl.ds(0, frames), pl.ds(frames, frames), pl.ds(0, 2 * frames)

    barrier = pltpu.get_barrier_semaphore()
    for target in (to_y, to_up, to_down, to_core, to_x):
        pl.semaphore_signal(barrier, inc=1, device_id=target, device_id_type=MESH)

    loads = [
        pltpu.make_async_copy(counts.at[rows], raw_counts.at[rows], load_sem.at[q])
        for q, rows in enumerate(pl.ds(q * fine, fine) for q in range(PIECES))
    ]
    per_pixel = [
        pltpu.make_async_copy(source, target, load_sem.at[PIECES + k])
        for k, (source, target) in enumerate(
            ((dead_source, dead_time), (flat_source, flat_field), (cycle_source, cycle_map))
        )
    ]
    for load in [*per_pixel[:2], *loads, per_pixel[2]]:
        load.start()
    for load in per_pixel[:2]:
        load.wait()

    def correct(i, carry):
        rows = pl.ds(pl.multiple_of(i * TILE, TILE), TILE)
        raw = raw_counts[rows, :]
        value = raw / (1.0 - dead_time[...] * raw) * flat_field[...]
        right[rows, :] = value.astype(jnp.bfloat16)
        return carry

    def correct_piece(q):
        loads[q].wait()
        lax.fori_loop(q * fine // TILE, (q + 1) * fine // TILE, correct, 0)

    def remote(source, target, send, recv, device):
        return pltpu.make_async_remote_copy(
            src_ref=source, dst_ref=target, send_sem=send, recv_sem=recv,
            device_id=device, device_id_type=MESH,
        )

    copies = []

    def start(*args):
        copy = remote(*args)
        copy.start()
        copies.append(copy)
        return copy

    def chunk(n):
        return pl.ds(pl.multiple_of(n * step, step), step)

    for q in range(PIECES // CHUNKS):
        correct_piece(q)
    pl.semaphore_wait(barrier, 5)

    def to_ring(n):
        return remote(right.at[chunk(n)], ring.at[chunk(n)], up_send.at[n], up_recv.at[n], to_up)

    to_rings = [to_ring(n) for n in range(CHUNKS)]
    to_rings[0].start()
    for q in range(PIECES // CHUNKS, PIECES):
        correct_piece(q)
    deep = pixels // 2

    def depth(h):
        return pl.ds(0, deep) if h == 0 else pl.ds(deep, pixels - deep)

    by_side = [
        start(right.at[own, depth(h)], right.at[beside, depth(h)], y_send.at[h], y_recv.at[h], to_y)
        for h in range(2)
    ]

    def piece(m, offset=0):
        return pl.ds(pl.multiple_of(offset + m * fine, fine), fine)

    def forward(m):
        return remote(ring.at[piece(m)], ring.at[piece(m, frames)],
                      up_send.at[m + CHUNKS], up_recv.at[m + CHUNKS], to_up)

    landed = [forward(m) for m in range(PIECES)]
    copies += to_rings + landed

    per_pixel[2].wait()
    ids = lax.broadcasted_iota(jnp.int32, (CYCLES, pixels), 0)
    onehot = jnp.where(jnp.broadcast_to(cycle_map[...], (CYCLES, pixels)) == ids, 1.0, 0.0)
    counted = lax.dot_general(
        onehot.astype(jnp.bfloat16), right[own, :], (((1,), (1,)), ((), ())),
        preferred_element_type=jnp.float32,
    )
    size = jnp.sum(onehot, axis=1, keepdims=True)
    sums_out[:, own] = counted
    sums_out[:, beside] = jnp.broadcast_to(size, counted.shape)
    by_core = start(sums_out, sums_core, sum_send.at[0], sum_recv.at[0], to_core)

    def fill(r, carry):
        hit = jnp.broadcast_to(cycle_map[...], (TILE, pixels)) == r
        wide[r] = jnp.where(hit, 1.0, 0.0).astype(jnp.bfloat16)
        return carry

    lax.fori_loop(0, CYCLES // 2, fill, 0)
    by_core.wait_recv()
    sums_chip[...] = sums_out[...] + sums_core[...]
    by_x = start(sums_chip, sums_x, sum_send.at[1], sum_recv.at[1], to_x)
    lax.fori_loop(CYCLES // 2, CYCLES, fill, 0)
    by_x.wait_recv()
    mine = pl.ds(pl.multiple_of(at_pix * owned, owned), owned)
    scale_own[...] = sums_chip[mine, :] + sums_x[mine, :]
    by_y = start(scale_own, scale_side, sum_send.at[2], sum_recv.at[2], to_y)
    by_up = start(scale_own, scale_first, sum_send.at[3], sum_recv.at[3], to_up)
    for n in range(1, CHUNKS):
        to_rings[n].start()

    def product(left, rows, count, cols, made, j, ks, add):
        base = (lax.rem(x + 1 + j, 2) * 2 + lax.rem(core + 1 + j // 2, 2)) * owned
        block = left[rows, ks].reshape(count // TILE, TILE, ks.size)
        masked = jnp.concatenate(
            [(block * wide[base + i, :, ks][None]).reshape(count, ks.size) for i in range(owned)],
            axis=0,
        )
        value = lax.dot_general(
            masked, right[cols, ks], (((1,), (1,)), ((), ())), preferred_element_type=jnp.float32
        ).reshape(owned, count, cols.size)
        made[j] = made[j] + value if add else value

    def early(left, rows, count, cols, made):
        def body(j, carry):
            product(left, rows, count, cols, made, j, depth(0), False)
            return carry

        lax.fori_loop(0, 4, body, 0)

    def send_across(unit):
        unit["others"][0].wait_recv()
        unit["code_out"][...] = partials.encode(unit["block"][4][2] + unit["inn"][0])
        unit["across"].start()

    def settle(unit):
        unit["others"][1].wait_recv()
        unit["here"][...] = unit["block"][4][3] + unit["inn"][1]

    def reduce_unit(unit, before=None, late=False, final=False):
        ks = depth(1) if late else pl.ds(0, pixels)

        def body(j, carry):
            product(*unit["block"], j, ks, late)

            @pl.when(j == 0)
            def _():
                unit["others"][0].start()
                if before is not None:
                    send_across(before)

            @pl.when(j == 1)
            def _():
                unit["others"][1].start()
                if before is not None:
                    settle(before)

            if final:

                @pl.when(j == 2)
                def _():
                    send_across(unit)

            return carry

        lax.fori_loop(0, 4, body, 0)

    half = frames // 2

    def keep(source, target, n):
        return pltpu.make_async_copy(source, target, keep_sem.at[n])

    def diag_core(n):
        return [
            remote(diag_out.at[n, g], diag_in.at[n, g],
                   diag_core_send.at[n, g], diag_core_recv.at[n, g], to_core)
            for g in range(2)
        ]

    def diag_across(n):
        return remote(diag_x_out.at[n], diag_x_in.at[n],
                      diag_send.at[n], diag_recv.at[n], to_x)

    def diag_unit(n):
        return dict(
            block=(right, pl.ds(n * half, half), half, own, diag_out.at[n]), inn=diag_in.at[n],
            others=diag_core(n), code_out=diag_x_out.at[n], across=diag_across(n), here=diag_here.at[n],
        )

    diags = [diag_unit(0), diag_unit(1)]
    reduce_unit(diags[0])
    reduce_unit(diags[1], diags[0])
    for unit in diags:
        copies += [*unit["others"], unit["across"]]

    def pass_on(n):
        remote(ring.at[chunk(n)], ring.at[chunk(n)], up_send.at[n], up_recv.at[n], to_up).wait_recv()
        for m in range(n * PIECES // CHUNKS, (n + 1) * PIECES // CHUNKS):
            landed[m].start()

    by_up.wait_recv()
    by_up2 = start(scale_first, scale_second, sum_send.at[4], sum_recv.at[4], to_up)
    for n in range(CHUNKS - 1):
        pass_on(n)
    half_rows = pl.ds(pl.multiple_of(y * half, half), half)
    pair_block = (right, pl.ds(pl.multiple_of(y * (frames + half), half), half), half,
                  pl.ds(pl.multiple_of((1 - y) * frames, frames), frames), pair_out)

    by_side[0].wait_recv()
    early(*pair_block)
    send_across(diags[1])
    settle(diags[1])
    early(ring, chunk(0), step, every, swap_out.at[0])
    size = scale_own[:, beside]
    own_sums = scale_own[:, own]
    own_columns = jnp.transpose(size / own_sums, (1, 0))
    columns[own, :] = jnp.transpose(size / scale_first[:, own], (1, 0))
    for n in range(2):
        rows = pl.ds(n * half, half)
        diags[n]["across"].wait_recv()
        for r in range(owned):
            value = diag_here[n, r] + partials.decode(diag_x_in[n, r])
            value = value * own_columns[n * half : (n + 1) * half, r : r + 1]
            diag_rows[r, rows, :] = value * (1.0 / own_sums[r : r + 1])
    keep(diag_rows, diagonal, 0).start()

    pair_across = remote(pair_x_out, pair_x_in, pair_send.at[1], pair_recv.at[1], to_x)
    pair_core = [
        remote(pair_out.at[g], pair_in.at[g], pair_core_send.at[g], pair_core_recv.at[g], to_core)
        for g in range(2)
    ]
    by_side[1].wait_recv()
    pass_on(CHUNKS - 1)
    pair_unit = dict(block=pair_block, others=pair_core, inn=pair_in, code_out=pair_x_out,
                     across=pair_across, here=pair_here)
    reduce_unit(pair_unit, late=True)
    copies += [*pair_core, pair_across]

    by_y.wait_recv()
    side_sums = scale_side[:, own]
    lower = y == 0
    pair_columns[...] = jnp.transpose(size / jnp.where(lower, own_sums, side_sums), (1, 0))
    pair_lanes = 1.0 / jnp.where(lower, side_sums, own_sums)
    lanes[...] = 1.0 / jnp.concatenate([own_sums, side_sums], axis=1)

    def coarse(n):
        rows = chunk(n)
        return dict(
            block=(ring, rows, step, every, swap_out.at[n]), rows=rows, inn=swap_in.at[n],
            others=[remote(swap_out.at[n, g], swap_in.at[n, g],
                           core_send.at[n, g], core_recv.at[n, g], to_core) for g in range(2)],
            code_out=x_out.at[n], code_in=x_in.at[n],
            across=remote(x_out.at[n], x_in.at[n], x_send.at[n], x_recv.at[n], to_x),
            here=here.at[n], side=side_out.at[n], back=back_out.at[n],
            to_side=remote(side_out.at[n], side_in.at[:, rows], side_send.at[n], side_recv.at[n], to_y),
            to_back=remote(back_out.at[n], back_in.at[:, rows], back_send.at[n], back_recv.at[n], to_down),
        )

    def fine_unit(m):
        rows = piece(m, frames)
        return dict(
            block=(ring, rows, fine, every, fine_swap_out.at[m]), rows=rows, inn=fine_swap_in.at[m],
            others=[remote(fine_swap_out.at[m, g], fine_swap_in.at[m, g],
                           fine_core_send.at[m, g], fine_core_recv.at[m, g], to_core)
                    for g in range(2)],
            code_out=fine_x_out.at[m], code_in=fine_x_in.at[m],
            across=remote(fine_x_out.at[m], fine_x_in.at[m], fine_x_send.at[m], fine_x_recv.at[m], to_x),
            here=fine_here.at[m], side=fine_side_out.at[m], back=None,
            to_side=remote(fine_side_out.at[m], side_in.at[:, rows],
                           fine_side_send.at[m], fine_side_recv.at[m], to_y),
        )

    by_pair = remote(pair_rows, pair.at[:, half_rows], pair_send.at[0], pair_recv.at[0], to_y)

    def finish(unit):
        unit["across"].wait_recv()
        rows, back = unit["rows"], unit["back"]
        for r in range(owned):
            value = unit["here"][r] + partials.decode(unit["code_in"][r])
            value = value * columns[rows, r : r + 1] * lanes[r : r + 1, :]
            if back is not None:
                back[r] = results.encode(value)
            unit["side"][r] = results.encode(value[:, frames:])
            local_rows[r, rows, :] = value[:, :frames]
        if back is not None:
            unit["to_back"].start()
        unit["to_side"].start()

    def turn(s):
        for r in range(owned):
            local_turned[s, r] = jnp.transpose(local_rows[r, pl.ds(s * frames, frames), :], (1, 0))
        keep(local_turned.at[s], local.at[s], 1 + s).start()

    chain = [*map(coarse, range(CHUNKS)), *map(fine_unit, range(PIECES))]
    for k, unit in enumerate(chain):
        if k >= CHUNKS:
            landed[k - CHUNKS].wait_recv()
        reduce_unit(unit, chain[k - 1] if k else pair_unit, k == 0, k == len(chain) - 1)
        if k == 1:
            pair_across.wait_recv()
            for r in range(owned):
                value = pair_here[r] + partials.decode(pair_x_in[r])
                value = value * pair_columns[half_rows, r : r + 1] * pair_lanes[r : r + 1]
                pair_rows[r] = results.encode(value)
            by_pair.start()
            keep(pair_rows, pair.at[:, half_rows], 3).start()
        if k >= LAG:
            finish(chain[k - LAG])
        if k == CHUNKS:
            by_up2.wait_recv()
            columns[beside, :] = jnp.transpose(size / scale_second[:, own], (1, 0))
        if k == CHUNKS - 1 + LAG:
            turn(0)
    settle(chain[-1])
    for unit in chain[-LAG:-1]:
        finish(unit)
    finish(chain[-1])
    turn(1)
    by_pair.wait_recv()
    copies.append(by_pair)
    for unit in chain:
        landing = [unit["to_side"]] + ([] if unit["back"] is None else [unit["to_back"]])
        for copy in landing:
            copy.wait_recv()
        copies += [*unit["others"], unit["across"], *landing]
    keep(diag_rows, diagonal, 0).wait()
    for s in range(2):
        keep(local_turned.at[s], local.at[s], 1 + s).wait()
    keep(pair_rows, pair.at[:, half_rows], 3).wait()
    for copy in copies:
        copy.wait_send()


def assemble(results, *refs):
    inputs, out, held, rows, in_sem, out_sem = refs[:5], refs[5], refs[6:11], refs[11], refs[12], refs[13]
    diagonal, pair, local, side, back = held
    owned = diagonal.shape[0]

    def cut(ref, r):
        span = pl.ds(r, GROUP)
        return ref.at[:, span] if len(ref.shape) == 4 else ref.at[span]

    loads = [
        [
            pltpu.make_async_copy(cut(source, r), cut(target, r), in_sem.at[r // GROUP, k])
            for k, (source, target) in enumerate(zip(inputs, held))
        ]
        for r in range(0, owned, GROUP)
    ]
    for group in loads:
        for load in group:
            load.start()
    frames = diagonal.shape[1]
    at_tm = lax.axis_index("tm")
    z, y = at_tm // 2, at_tm % 2

    def turn(value):
        return jnp.transpose(value, (1, 0))

    stores = []
    for r in range(owned):
        if r % GROUP == 0:
            for load in loads[r // GROUP]:
                load.wait()

        def put(dz, dy, value):
            block = (z + dz + 4) % 4 * 2 + (y + dy) % 2
            rows[r, :, pl.ds(pl.multiple_of(block * frames, frames), frames)] = value

        put(0, 0, diagonal[r])
        value = results.decode(pair[r])
        put(0, 1, jnp.where(y == 0, value, turn(value)))
        for s in range(2):
            put(1 + s, 0, local[s, r])
            put(1 + s, 1, turn(results.decode(side[r, pl.ds(s * frames, frames), :])))
        value = results.decode(back[r])
        put(-1, 0, value[:, :frames])
        put(-1, 1, value[:, frames:])
        if r % GROUP == GROUP - 1:
            span = pl.ds(r - GROUP + 1, GROUP)
            stores.append(pltpu.make_async_copy(rows.at[span], out.at[span], out_sem.at[r // GROUP]))
            stores[-1].start()
    for store in stores:
        store.wait()


def per_device_kernel(counts, dead_time, flat_field, cycle_map):
    frames, pixels = counts.shape
    if frames % (PIECES * TILE):
        return per_device(counts, dead_time, flat_field, cycle_map)
    tm, pix = lax.axis_size("tm"), lax.axis_size("pix")
    owned = CYCLES // pix
    partials = LogCode(0.0218, 6800.0 * pixels * 2, True)
    results = LogCode(1 / 140.0, 140.0, False)
    f32, bf16, i16 = jnp.float32, jnp.bfloat16, jnp.int16
    vmem, dma = pltpu.VMEM, pltpu.SemaphoreType.DMA
    both, half, step, fine = 2 * frames, frames // 2, frames // CHUNKS, frames // PIECES
    units, pieces, rings = CHUNKS, PIECES, CHUNKS + PIECES
    small = (owned, both)
    scratch = [
        vmem((owned, frames, frames), f32),
        vmem((owned, half, frames), i16),
        vmem((owned, both, frames), f32),
        vmem((2, owned, frames, frames), f32),
        vmem((CYCLES, TILE, pixels), bf16),
        vmem((both, pixels), bf16),
        vmem((both, pixels), bf16),
        vmem((units, 4, owned, step, both), f32),
        vmem((units, 2, owned, step, both), f32),
        *[vmem((units, owned, step, both), i16)] * 2,
        vmem((units, owned, step, both), f32),
        vmem((units, owned, step, frames), i16),
        vmem((units, owned, step, both), i16),
        vmem((2, 4, owned, half, frames), f32),
        vmem((2, 2, owned, half, frames), f32),
        *[vmem((2, owned, half, frames), i16)] * 2,
        vmem((2, owned, half, frames), f32),
        vmem((4, owned, half, frames), f32),
        vmem((2, owned, half, frames), f32),
        *[vmem((owned, half, frames), i16)] * 2,
        vmem((owned, half, frames), f32),
        *[vmem((CYCLES, both), f32)] * 4,
        *[vmem(small, f32)] * 4,
        vmem((both, owned), f32),
        vmem((frames, owned), f32),
        vmem(small, f32),
        dma((units, 2)), dma((units, 2)), dma((units,)), dma((units,)),
        dma((rings,)), dma((rings,)), dma((CHUNKS,)), dma((CHUNKS,)),
        dma((units,)), dma((units,)), dma((2,)), dma((2,)), dma((2,)), dma((2,)),
        dma((5,)), dma((5,)), dma((4,)), dma((2,)), dma((2,)), dma((2, 2)), dma((2, 2)), dma((2,)), dma((2,)),
        vmem((pieces, 4, owned, fine, both), f32),
        vmem((pieces, 2, owned, fine, both), f32),
        *[vmem((pieces, owned, fine, both), i16)] * 2,
        vmem((pieces, owned, fine, both), f32),
        vmem((pieces, owned, fine, frames), i16),
        dma((pieces, 2)), dma((pieces, 2)), dma((pieces,)), dma((pieces,)), dma((pieces,)), dma((pieces,)),
        vmem((frames, pixels), f32), dma((pieces + 3,)),
        *[vmem((1, pixels), f32)] * 2, vmem((1, pixels), jnp.int32),
    ]
    shapes = [
        ((owned, frames, frames), f32), ((owned, frames, frames), i16),
        ((2, owned, frames, frames), f32), ((owned, both, frames), i16), ((owned, frames, both), i16),
    ]
    made = pl.pallas_call(
        functools.partial(exchange, owned, partials, results),
        out_shape=[jax.ShapeDtypeStruct(*shape) for shape in shapes],
        in_specs=[pl.BlockSpec(memory_space=pl.ANY)] * 4,
        out_specs=[pl.BlockSpec(memory_space=pl.ANY)] * 5,
        scratch_shapes=scratch,
        compiler_params=pltpu.CompilerParams(
            collective_id=0, has_side_effects=True, vmem_limit_bytes=60 << 20
        ),
    )(counts, dead_time[None, :], flat_field[None, :], cycle_map[None, :])
    return pl.pallas_call(
        functools.partial(assemble, results),
        out_shape=jax.ShapeDtypeStruct((owned, frames, tm * frames), f32),
        in_specs=[pl.BlockSpec(memory_space=pl.ANY)] * len(shapes),
        out_specs=pl.BlockSpec(memory_space=pl.ANY),
        scratch_shapes=[
            *[vmem(*shape) for shape in shapes],
            vmem((owned, frames, tm * frames), f32),
            dma((owned // GROUP, len(shapes))), dma((owned // GROUP,)),
        ],
        compiler_params=pltpu.CompilerParams(vmem_limit_bytes=60 << 20),
    )(*made)


def solution(mesh):
    kernel_path = fits_kernel(mesh.shape)
    device_program = per_device_kernel if kernel_path else per_device
    placed = (P("tm", "pix"), P("pix"), P("pix"), P("pix"))

    return jax.shard_map(
        device_program, mesh=mesh, in_specs=placed, out_specs=P("pix", "tm", None), check_vma=False
    )
```
